32 devices in a mesh: chan: 8 (over z, y), tm: 4 (over x, core).
Axes of the slice: x: 2, y: 2, z: 4, core: 2. Of those that a mesh axis runs over, the one named last changes fastest.
Arguments:
- samples: float32 [256, 4096], P('chan', 'tm'), may hold values from -6 to 6
- thresholds: int32 [3, 6], replicated, may hold values from 8 to 48
- sources: int32 [64], replicated, may hold values from 0 to 255
Outputs:
- correlations: float32 [64, 256, 512], P(None, ('chan', 'tm'))
The draws below stay inside these ranges and needn't reach their ends.
Inputs may be any that keep to these rules, and one draw needn't show every extreme that they name: Channel numbers of the virtual sources; two may be equal.
All inputs are finite; a program needn't handle non-finite values.
Results may differ from the reference program's by a relative error of at most 0.0074.
Values may be sent and summed in bfloat16 or wider, within the bound.
A program may use at most 64 MiB of HBM per device.

```python
import math
import jax
import jax.numpy as jnp
from jax import lax

N = 1024
LEVELS = 3
SOURCES = 64
BINS = 512
LAGS = 512
CHANNELS = 256
WINDOWS = 4
TIME = 4096


def touch_ends(entries, key, low, largest):
    spot = [jax.random.randint(jax.random.fold_in(key, axis), (), 0, length) for axis, length in enumerate(entries.shape)]
    longest = entries.shape.index(max(entries.shape))
    beside = spot[:longest] + [(spot[longest] + 1) % entries.shape[longest]] + spot[longest + 1:]
    return entries.at[tuple(spot)].set(low).at[tuple(beside)].set(largest)


def level_of(own_key, shape, shards, smallest, high):
    loudness = 1.0
    for dim, parts in shards:
        heights = jax.random.uniform(jax.random.fold_in(jax.random.fold_in(own_key, 6), dim), (parts,), jnp.float32, smallest / len(shards), high / len(shards))
        loudness = loudness * jnp.repeat(jnp.exp(heights), shape[dim] // parts).reshape((-1,) + (1,) * (len(shape) - 1 - dim))
    return loudness


def noise(key, shape, spread, most, cuts=(), held_as=jnp.bfloat16):
    entries = spread * jax.random.normal(key, shape, jnp.float32)
    if cuts:
        entries = entries * level_of(key, shape, cuts, -0.22, 0.18)
    return jnp.clip(entries, -most, most).astype(held_as)


def setup_inputs(seed: int = 0) -> dict:
    key_list = jax.random.split(jax.random.key(seed), 4)
    samples = noise(key_list[0], (CHANNELS, TIME), 1.0, 6.0, ((0, 8), (1, 4)), jnp.float32)
    thresholds = touch_ends(jax.random.randint(key_list[1], (LEVELS, 6), 8, 49), jax.random.fold_in(key_list[1], 1), 8, 48).astype(jnp.int32)
    sources = touch_ends(jax.random.randint(key_list[2], (SOURCES,), 0, CHANNELS), jax.random.fold_in(key_list[2], 1), 0, CHANNELS - 1).astype(jnp.int32)
    return dict(samples=samples, thresholds=thresholds, sources=sources)


daubechies = [0.2303778133088964, 0.7148465705529155, 0.6308807679298587, -0.0279837694168599, -0.1870348117190931, 0.0308413818355607, 0.0328830116668852, -0.010597401785069]

def filter_bank():
    lowpass = list(daubechies)
    highpass = [(1.0 if tap_index % 2 == 0 else -1.0) * daubechies[7 - tap_index] for tap_index in range(8)]
    return [(lowpass, highpass), (lowpass[::-1], highpass[::-1])]

def analyse(extended, filter_taps, dimension, length):
    summed = filter_taps[0] * lax.slice_in_dim(extended, 0, length - 1, 2, dimension)
    for tap_index in range(1, 8):
        summed = summed + filter_taps[tap_index] * lax.slice_in_dim(extended, tap_index, tap_index + length - 1, 2, dimension)
    return summed

def synthesise(low_ext, high_ext, low_taps, high_taps, dimension, length):
    even_part = None
    odd_part = None
    for step_index in range(4):
        even_term = low_taps[2 * step_index + 1] * lax.slice_in_dim(low_ext, 3 - step_index, 3 - step_index + length, 1, dimension) + high_taps[2 * step_index + 1] * lax.slice_in_dim(high_ext, 3 - step_index, 3 - step_index + length, 1, dimension)
        odd_term = low_taps[2 * step_index] * lax.slice_in_dim(low_ext, 4 - step_index, 4 - step_index + length, 1, dimension) + high_taps[2 * step_index] * lax.slice_in_dim(high_ext, 4 - step_index, 4 - step_index + length, 1, dimension)
        even_part = even_term if even_part is None else even_part + even_term
        odd_part = odd_term if odd_part is None else odd_part + odd_term
    woven = jnp.stack([even_part, odd_part], dimension + 1)
    new_shape = list(even_part.shape)
    new_shape[dimension] = 2 * new_shape[dimension]
    return woven.reshape(new_shape)

def shrink_band(band_aa, band_ab, band_ba, band_bb, cutoff_one, cutoff_two):
    root_half = 1.0 / math.sqrt(2.0)
    real_one = (band_aa - band_bb) * root_half
    imaginary_one = (band_ab + band_ba) * root_half
    real_two = (band_aa + band_bb) * root_half
    imaginary_two = (band_ab - band_ba) * root_half
    magnitude_one = jnp.sqrt(real_one * real_one + imaginary_one * imaginary_one)
    magnitude_two = jnp.sqrt(real_two * real_two + imaginary_two * imaginary_two)
    factor_one = jnp.maximum(magnitude_one - cutoff_one, 0.0) / jnp.maximum(magnitude_one, cutoff_one)
    factor_two = jnp.maximum(magnitude_two - cutoff_two, 0.0) / jnp.maximum(magnitude_two, cutoff_two)
    real_one = real_one * factor_one
    imaginary_one = imaginary_one * factor_one
    real_two = real_two * factor_two
    imaginary_two = imaginary_two * factor_two
    return ((real_one + real_two) * root_half, (imaginary_one + imaginary_two) * root_half, (imaginary_one - imaginary_two) * root_half, (real_two - real_one) * root_half)

def shrink_level(bands, thresholds, level_index):
    cutoffs = thresholds[level_index].astype(jnp.float32) / 32.0
    result = [[None, None, None] for tree_index in range(4)]
    for orient in range(3):
        shrunk = shrink_band(bands[0][orient + 1], bands[1][orient + 1], bands[2][orient + 1], bands[3][orient + 1], cutoffs[2 * orient], cutoffs[2 * orient + 1])
        for tree_index in range(4):
            result[tree_index][orient] = shrunk[tree_index]
    return result

def wrap_extend(values, width, dimension):
    size_along = values.shape[dimension]
    head_part = lax.slice_in_dim(values, size_along - width, size_along, 1, dimension)
    tail_part = lax.slice_in_dim(values, 0, width, 1, dimension)
    return jnp.concatenate([head_part, values, tail_part], dimension)

def denoise(samples, thresholds):
    bank = filter_bank()
    tree_list = [(0, 0), (0, 1), (1, 0), (1, 1)]
    current = [samples, samples, samples, samples]
    saved = []
    for level_index in range(LEVELS):
        bands = []
        for tree_index in range(4):
            chan_tree, time_tree = tree_list[tree_index]
            source_band = current[tree_index]
            extended = wrap_extend(source_band, 3, 1)
            time_low = analyse(extended, bank[time_tree][0], 1, source_band.shape[1])
            time_high = analyse(extended, bank[time_tree][1], 1, source_band.shape[1])
            low_ext = wrap_extend(time_low, 3, 0)
            high_ext = wrap_extend(time_high, 3, 0)
            row_count = source_band.shape[0]
            bands.append([analyse(low_ext, bank[chan_tree][0], 0, row_count), analyse(high_ext, bank[chan_tree][0], 0, row_count), analyse(low_ext, bank[chan_tree][1], 0, row_count), analyse(high_ext, bank[chan_tree][1], 0, row_count)])
        current = [band_set[0] for band_set in bands]
        saved.append(shrink_level(bands, thresholds, level_index))
    for level_index in reversed(range(LEVELS)):
        details = saved[level_index]
        rebuilt = []
        for tree_index in range(4):
            chan_tree, time_tree = tree_list[tree_index]
            lowband = current[tree_index]
            band_lh, band_hl, band_hh = details[tree_index]
            time_low = synthesise(wrap_extend(lowband, 2, 0), wrap_extend(band_hl, 2, 0), bank[chan_tree][0], bank[chan_tree][1], 0, lowband.shape[0])
            time_high = synthesise(wrap_extend(band_lh, 2, 0), wrap_extend(band_hh, 2, 0), bank[chan_tree][0], bank[chan_tree][1], 0, lowband.shape[0])
            rebuilt.append(synthesise(wrap_extend(time_low, 2, 1), wrap_extend(time_high, 2, 1), bank[time_tree][0], bank[time_tree][1], 1, time_low.shape[1]))
        current = rebuilt
    return (0.25 * (current[0] + current[1] + current[2] + current[3])).astype(jnp.bfloat16)

def dft_table():
    sample_index = jnp.arange(N, dtype=jnp.int32)
    frequency = jnp.arange(BINS, dtype=jnp.int32)
    phases = (sample_index[:, None] * frequency[None, :] % N).astype(jnp.float32) * (2.0 * math.pi / N)
    return jnp.concatenate([jnp.cos(phases), -jnp.sin(phases)], 1).astype(jnp.bfloat16)

def lag_table(window_count):
    frequency = jnp.arange(BINS, dtype=jnp.int32)
    shifts = jnp.arange(LAGS, dtype=jnp.int32) - LAGS // 2
    phases = jnp.mod(frequency[:, None] * shifts[None, :], N).astype(jnp.float32) * (2.0 * math.pi / N)
    weights = jnp.where(frequency == 0, 1.0, 2.0).astype(jnp.float32)[:, None] / math.sqrt(window_count * N)
    return jnp.concatenate([weights * jnp.cos(phases), -weights * jnp.sin(phases)], 0).astype(jnp.bfloat16)

def correlate(source_block, first_recv, second_recv, table):
    half_width = source_block.shape[-1] // 2
    stacked = jnp.concatenate([source_block[:, :, :half_width], source_block[:, :, half_width:]], 1).astype(jnp.float32)
    cross_real = jnp.einsum('skf,rkf->srf', stacked, first_recv)
    cross_imag = jnp.einsum('skf,rkf->srf', stacked, second_recv)
    cross_spec = lax.optimization_barrier(jnp.concatenate([cross_real, cross_imag], -1).astype(jnp.bfloat16)).astype(jnp.float32)
    flat = cross_spec.reshape(-1, cross_spec.shape[-1])
    result = jnp.dot(flat, table.astype(jnp.float32), preferred_element_type=jnp.float32)
    return result.reshape(source_block.shape[0], first_recv.shape[0], table.shape[1])

def reference(samples, thresholds, sources):
    denoised = lax.optimization_barrier(denoise(samples, thresholds)).astype(jnp.float32)
    spectra = jnp.dot(denoised.reshape(-1, N), dft_table().astype(jnp.float32), preferred_element_type=jnp.float32)
    whitened = spectra * lax.rsqrt(lax.optimization_barrier(jnp.mean(spectra * spectra, axis=1, keepdims=True)) + 1e-05)
    whitened = lax.optimization_barrier(whitened.astype(jnp.bfloat16)).astype(jnp.float32)
    whitened = whitened.reshape(CHANNELS, WINDOWS, N)
    picked = whitened[sources.astype(jnp.int32)]
    recv_real = whitened[:, :, :BINS]
    recv_imag = whitened[:, :, BINS:]
    first_recv = jnp.concatenate([recv_real, recv_imag], 1)
    second_recv = jnp.concatenate([-recv_imag, recv_real], 1)
    table = lag_table(WINDOWS)
    blocks = picked.reshape(SOURCES // 8, 8, WINDOWS, N)
    result = lax.map(lambda block_item: correlate(block_item, first_recv, second_recv, table), blocks)
    return result.reshape(SOURCES, CHANNELS, LAGS)
```

```python
import functools
import math

import jax
import jax.numpy as jnp
import numpy as np
from jax import lax
from jax.experimental import pallas as pl
from jax.experimental.pallas import tpu as pltpu
from jax.sharding import PartitionSpec as P

N = 1024
LEVELS = 3
BINS = 512
LAGS = 512
BLOCK = 128
HALF = 64
MESH = pl.DeviceIdType.MESH

daubechies = [
    0.2303778133088964,
    0.7148465705529155,
    0.6308807679298587,
    -0.0279837694168599,
    -0.1870348117190931,
    0.0308413818355607,
    0.0328830116668852,
    -0.010597401785069,
]


def filter_bank():
    lowpass = list(daubechies)
    highpass = [(1.0 if k % 2 == 0 else -1.0) * daubechies[7 - k] for k in range(8)]
    return [(lowpass, highpass), (lowpass[::-1], highpass[::-1])]


def bank_matrix(length):
    half = length // 2
    out = np.zeros((2, 2, half, length))
    rows = np.arange(half)
    for tree, pair in enumerate(filter_bank()):
        for band, taps in enumerate(pair):
            for k in range(8):
                np.add.at(out[tree, band], (rows, (2 * rows + k - 3) % length), taps[k])
    return out.reshape(2, length, length)


def halves(matrix):
    m32 = np.asarray(matrix, np.float32)
    hi = m32.astype(jnp.bfloat16)
    lo = (m32 - hi.astype(np.float32)).astype(jnp.bfloat16)
    return np.stack([hi, lo])


def dft_table():
    t = np.arange(N)
    f = np.arange(BINS)
    phases = ((t[:, None] * f[None, :]) % N).astype(np.float64) * (2.0 * math.pi / N)
    table = np.concatenate([np.cos(phases), -np.sin(phases)], 1)
    return table.astype(np.float32).astype(jnp.bfloat16)


def split(x):
    hi = x.astype(jnp.bfloat16)
    lo = (x - hi.astype(jnp.float32)).astype(jnp.bfloat16)
    return hi, lo


def dot(a, b, trans_b):
    dims = (((1,), (1 if trans_b else 0,)), ((), ()))
    return lax.dot_general(a, b, dims, preferred_element_type=jnp.float32)


def dot3(a, b, trans_b=False):
    return dot(a[0], b[0], trans_b) + (dot(a[1], b[0], trans_b) + dot(a[0], b[1], trans_b))


def greet_all():
    n_tm = lax.axis_size("tm")
    n = lax.axis_size("chan") * n_tm
    me = lax.axis_index("chan") * n_tm + lax.axis_index("tm")
    barrier = pltpu.get_barrier_semaphore()

    def greet(k, carry):
        d = lax.rem(me + k, n)
        pl.semaphore_signal(
            barrier, inc=1, device_id=(d // n_tm, lax.rem(d, n_tm)), device_id_type=MESH
        )
        return carry

    lax.fori_loop(1, n, greet, 0)


def gather(
    samples, slab, rim_slab, blocks, rims, edge, send, recv, edge_send, edge_recv
):
    n_chan, n_tm = lax.axis_size("chan"), lax.axis_size("tm")
    c, t = lax.axis_index("chan"), lax.axis_index("tm")
    rows, width = samples.shape
    count = width // BLOCK
    rep = n_chan // count
    values = samples[...]
    for j in range(count):
        right, left = (BLOCK * (j + 1)) % width, (BLOCK * j - HALF) % width
        blocks[j] = values[:, BLOCK * j : BLOCK * (j + 1)]
        rims[j] = jnp.concatenate(
            [values[:, right : right + HALF], values[:, left : left + HALF]], 1
        ).astype(jnp.bfloat16)
    rims[count] = jnp.concatenate([values[:, :HALF], values[:, width - HALF :]], 1).astype(
        jnp.bfloat16
    )
    pl.semaphore_wait(pltpu.get_barrier_semaphore(), n_chan * n_tm - 1)
    mine = pl.ds(pl.multiple_of(c * rows, rows), rows)
    place = c // rep

    def pair(to, rows_at, landing):
        return (
            pltpu.make_async_remote_copy(
                src_ref=blocks.at[to // rep],
                dst_ref=slab.at[rows_at, :],
                send_sem=send.at[to],
                recv_sem=recv.at[landing],
                device_id=(to, t),
                device_id_type=MESH,
            ),
            pltpu.make_async_remote_copy(
                src_ref=rims.at[to // rep],
                dst_ref=rim_slab.at[rows_at, :],
                send_sem=send.at[n_chan + to],
                recv_sem=recv.at[n_chan + landing],
                device_id=(to, t),
                device_id_type=MESH,
            ),
        )

    def remote(to):
        return pair(to, mine, c)

    def incoming(source):
        return pair(source, pl.ds(pl.multiple_of(source * rows, rows), rows), source)

    def rim(to, shift, r):
        return pltpu.make_async_remote_copy(
            src_ref=rims.at[count],
            dst_ref=edge.at[mine, :],
            send_sem=edge_send.at[r],
            recv_sem=edge_recv.at[c],
            device_id=(to, lax.rem(t + shift, n_tm)),
            device_id_type=MESH,
        )

    for r in range(rep):
        rim(r, 1, r).start()
        rim((count - 1) * rep + r, n_tm - 1, rep + r).start()
    slab[mine, :] = blocks[place]
    rim_slab[mine, :] = rims[place]

    def start(k, carry):
        for copy in remote(lax.rem(c + k, n_chan)):
            copy.start()
        return carry

    lax.fori_loop(1, n_chan, start, 0)

    def finish(k, carry):
        for copy in incoming(lax.rem(c + n_chan - k, n_chan)):
            copy.wait_recv()
        return carry

    lax.fori_loop(1, n_chan, finish, 0)
    at_edge = jnp.logical_or(place == 0, place == count - 1)

    @pl.when(at_edge)
    def _():
        def take(source, carry):
            pltpu.make_async_remote_copy(
                src_ref=rims.at[count],
                dst_ref=edge.at[pl.ds(pl.multiple_of(source * rows, rows), rows), :],
                send_sem=edge_send.at[0],
                recv_sem=edge_recv.at[source],
                device_id=(source, lax.rem(t + 1, n_tm)),
                device_id_type=MESH,
            ).wait_recv()
            return carry

        lax.fori_loop(0, n_chan, take, 0)

    left = lax.broadcasted_iota(jnp.int32, edge.shape, 1) < HALF

    @pl.when(place == 0)
    def _():
        rim_slab[...] = jnp.where(left, rim_slab[...], edge[...])

    @pl.when(place == count - 1)
    def _():
        rim_slab[...] = jnp.where(left, edge[...], rim_slab[...])

    def sent(k, carry):
        for copy in remote(lax.rem(c + k, n_chan)):
            copy.wait_send()
        return carry

    lax.fori_loop(1, n_chan, sent, 0)
    for r in range(rep):
        rim(r, 1, r).wait_send()
        rim((count - 1) * rep + r, n_tm - 1, rep + r).wait_send()


def shrink(aa, ab, ba, bb, cut_one, cut_two):
    root_half = 1.0 / math.sqrt(2.0)
    re1 = (aa - bb) * root_half
    im1 = (ab + ba) * root_half
    re2 = (aa + bb) * root_half
    im2 = (ab - ba) * root_half
    f1 = jnp.maximum(1.0 - cut_one * lax.rsqrt(re1 * re1 + im1 * im1), 0.0) * root_half
    f2 = jnp.maximum(1.0 - cut_two * lax.rsqrt(re2 * re2 + im2 * im2), 0.0) * root_half
    re1, im1, re2, im2 = re1 * f1, im1 * f1, re2 * f2, im2 * f2
    return re1 + re2, im1 + im2, im1 - im2, re2 - re1


def cut_maps(cuts, level, shape, low_rows, low_cols):
    row_low = lax.broadcasted_iota(jnp.int32, shape, 0) < low_rows
    col_low = lax.broadcasted_iota(jnp.int32, shape, 1) < low_cols
    pick = []
    for k in range(2):
        lh, hl, hh = (cuts[level, 2 * o + k].astype(jnp.float32) / 32.0 for o in range(3))
        pick.append(jnp.where(row_low, lh, jnp.where(col_low, hl, hh)))
    return pick[0], pick[1], jnp.logical_and(row_low, col_low)


def packed(matrix):
    hi, lo = halves(matrix)
    return np.concatenate(
        [np.concatenate([hi, hi], -1), np.concatenate([lo, np.zeros_like(lo)], -1)], -2
    )


def by_rows(x, weight):
    y = dot(jnp.concatenate(split(x), 1), weight, True)
    half = weight.shape[0] // 2
    return y[:, :half] + y[:, half:]


def by_cols(weight, x):
    y = dot(weight, jnp.concatenate(split(x), 0), False)
    half = weight.shape[0] // 2
    return y[:half] + y[half:]


def both_ways(bands, chan_weight, time_weight):
    rows, cols = bands[0].shape
    timed = []
    for q in range(2):
        timed.append(by_rows(jnp.concatenate([bands[q], bands[2 + q]], 0), time_weight[q]))
    out = []
    for p in range(2):
        part = slice(p * rows, (p + 1) * rows)
        y = by_cols(chan_weight[p], jnp.concatenate([timed[0][part], timed[1][part]], 1))
        out += [y[:, :cols], y[:, cols:]]
    return out


def denoise(cuts, slab, rim_slab, sources, tables, picked, cleaned, coefs):
    c1, c1t, t1, c2, c2t, t2, t2t, c3, c3t, t3, t3t = tables
    trees = [(0, 0), (0, 1), (1, 0), (1, 1)]
    rows = slab.shape[0]
    cols = 2 * BLOCK
    hi, lo = split(slab[...])
    rim = rim_slab[...]
    x = jnp.concatenate([hi, rim], 1), jnp.concatenate([lo, jnp.zeros_like(rim)], 1)
    first = split(dot3(x, (t1[0], t1[1]), True))
    coefs[...] = dot3((c1[0], c1[1]), first)
    hr, hc = rows // 2, cols // 2
    corners = [
        (slice(p * rows, p * rows + hr), slice(q * cols, q * cols + hc)) for p, q in trees
    ]
    lows = both_ways([coefs[a, b] for a, b in corners], c2, t2)
    deep = both_ways(lows, c3, t3)
    live = hr // 2
    deep = [band[:live] for band in deep]
    one, two, kept = cut_maps(cuts, 2, deep[0].shape, hr // 4, hc // 4)
    shrunk = shrink(*deep, one, two)
    deep = [jnp.where(kept, a, b) for a, b in zip(deep, shrunk)]
    rest = jnp.zeros((hr - live, hc), jnp.float32)
    inner = both_ways([jnp.concatenate([band, rest], 0) for band in deep], c3t, t3t)
    one, two, kept = cut_maps(cuts, 1, lows[0].shape, hr // 2, hc // 2)
    shrunk = shrink(*lows, one, two)
    outer = both_ways([jnp.where(kept, a, b) for a, b in zip(inner, shrunk)], c2t, t2t)
    for orient, (row_high, col_high) in enumerate([(0, 1), (1, 0), (1, 1)]):
        spots = [
            (
                slice(p * rows + row_high * hr, p * rows + row_high * hr + hr),
                slice(q * cols + col_high * hc, q * cols + col_high * hc + hc),
            )
            for p, q in trees
        ]
        top = [
            cuts[0, 2 * orient + k].astype(jnp.float32) / 32.0 for k in range(2)
        ]
        done = shrink(*[coefs[a, b] for a, b in spots], top[0], top[1])
        for (a, b), cell in zip(spots, done):
            coefs[a, b] = cell
    for (a, b), band in zip(corners, outer):
        coefs[a, b] = band
    hi, lo = split(coefs[...])
    t_hi, t_lo = t1[0, :, :BLOCK], t1[1, :, :BLOCK]
    y = dot(hi, jnp.concatenate([t_hi, t_lo], 1), False)
    timed = jnp.concatenate(split(y[:, :BLOCK] + y[:, BLOCK:] + dot(lo, t_hi, False)), 1)
    y = dot(c1t[0], timed, False)
    whole = y[:, :BLOCK] + y[:, BLOCK:] + dot(c1t[1], timed[:, :BLOCK], False)
    result = (0.25 * whole).astype(jnp.bfloat16)
    cleaned[...] = result.astype(jnp.float32).reshape(rows // 8, 8, BLOCK).astype(jnp.bfloat16)
    one_hot = jnp.where(
        lax.broadcasted_iota(jnp.int32, (rows, sources.shape[1]), 0) == sources[...], 1.0, 0.0
    )
    chosen = jnp.transpose(one_hot).astype(jnp.bfloat16)
    picked[...] = dot(chosen, result, False).astype(jnp.bfloat16)


def spread(picks, cleaned, receivers, near, far, across, recv, send, land, own):
    n_chan, n_tm = lax.axis_size("chan"), lax.axis_size("tm")
    c, t = lax.axis_index("chan"), lax.axis_index("tm")
    blocks = picks.shape[0]
    count = blocks // n_tm
    rep = n_chan // count
    pairs = n_tm // 2
    share = cleaned.shape[0] * 8 // (n_chan * n_tm)
    place, copy_index, core = c // rep, lax.rem(c, rep), lax.rem(t, 2)
    mine = t * count + place

    def move(block, sem, chan, tm):
        return pltpu.make_async_remote_copy(
            src_ref=picks.at[block],
            dst_ref=picks.at[block],
            send_sem=sem,
            recv_sem=recv.at[block],
            device_id=(chan, tm),
            device_id_type=MESH,
        )

    def group(k):
        return move(mine, near.at[k], lax.rem(place + k, count) * rep + copy_index, t)

    def along(u, k):
        to = lax.rem(t // 2 + u, pairs) * 2 + core
        chan = lax.rem(place + k, count) * rep + copy_index
        return move(mine, far.at[u * count + k], chan, to)

    def beside(u, k):
        other = lax.rem(t // 2 + pairs - u, pairs) * 2 + core
        block = other * count + lax.rem(place + count - k, count)
        return move(block, across.at[u * count + k], c, t + 1 - 2 * core)

    def rows_of(dc, dt):
        return (dc * n_tm + dt) * share // 8

    def personal(k):
        dc = lax.rem(place + k // n_tm, count) * rep + copy_index
        dt = lax.rem(t + lax.rem(k, n_tm), n_tm)
        return pltpu.make_async_remote_copy(
            src_ref=cleaned.at[rows_of(dc, dt)],
            dst_ref=receivers.at[mine],
            send_sem=send.at[k],
            recv_sem=land.at[mine],
            device_id=(dc, dt),
            device_id_type=MESH,
        )

    def each(low, high, act):
        def body(k, carry):
            act(k)
            return carry

        lax.fori_loop(low, high, body, 0)

    def await_block(block):
        move(block, near.at[0], c, t + 1 - 2 * core).wait_recv()

    def relay(k):
        @pl.when(k > 0)
        def _():
            await_block(t * count + lax.rem(place + count - k, count))

        beside(0, k).start()

    each(1, count, lambda k: group(k).start())
    for u in range(1, pairs):
        each(0, count, lambda k, u=u: along(u, k).start())
    local = pltpu.make_async_copy(cleaned.at[rows_of(c, t)], receivers.at[mine], own)
    local.start()
    relay(0)
    each(1, blocks, lambda k: personal(k).start())
    each(1, count, relay)
    for u in range(1, pairs):

        def cross_over(k, u=u):
            other = lax.rem(t // 2 + pairs - u, pairs) * 2 + core
            await_block(other * count + lax.rem(place + count - k, count))
            beside(u, k).start()

        each(0, count, cross_over)
    for u in range(pairs):

        def last(k, u=u):
            other = lax.rem(t // 2 + pairs - u, pairs) * 2 + 1 - core
            await_block(other * count + lax.rem(place + count - k, count))

        each(0, count, last)

    def landed(k):
        block = lax.rem(mine + k, blocks)
        pltpu.make_async_remote_copy(
            src_ref=cleaned.at[0],
            dst_ref=receivers.at[block],
            send_sem=send.at[0],
            recv_sem=land.at[block],
            device_id=(c, t + 1 - 2 * core),
            device_id_type=MESH,
        ).wait_recv()

    local.wait()
    each(1, blocks, landed)
    each(1, count, lambda k: group(k).wait_send())
    each(1, blocks, lambda k: personal(k).wait_send())
    for u in range(pairs):
        each(0, count, lambda k, u=u: beside(u, k).wait_send())
        if u:
            each(0, count, lambda k, u=u: along(u, k).wait_send())


def whole_kernel(n_tables, same, cuts, samples, sources, *refs):
    stored, refs = refs[:n_tables], refs[n_tables:]
    cross, picks, receivers, white, heard = refs[:5]
    held, refs = refs[5 : 5 + n_tables], refs[5 + n_tables :]
    here, refs = refs[:4], refs[4:]
    slab, rim_slab, blocks, rims, edge, coefs, cleaned, loads = refs[:8]
    gather_sems, spread_sems = refs[8:12], refs[12:]
    inputs = [
        pltpu.make_async_copy(a, b, here[3].at[i])
        for i, (a, b) in enumerate(zip((cuts, samples, sources), here))
    ]
    inputs[1].start()
    greet_all()
    inputs[0].start()
    inputs[2].start()
    copies = [pltpu.make_async_copy(a, b, loads.at[i]) for i, (a, b) in enumerate(zip(stored, held))]
    for copy in copies:
        copy.start()
    inputs[1].wait()
    cuts, samples, sources = here[:3]
    gather(samples, slab, rim_slab, blocks, rims, edge, *gather_sems)
    inputs[0].wait()
    inputs[2].wait()
    for copy in copies[:-1]:
        copy.wait()
    c1t, t1, c2, c2t, c3, c3t = held[:6]
    extra = [t1, c2, c2t, c3, c3t] if same else held[6:-1]
    tables = [extra[0], c1t, t1, extra[1], extra[2], c2, c2t, extra[3], extra[4], c3, c3t]
    n_tm = lax.axis_size("tm")
    count = picks.shape[0] // n_tm
    rep = lax.axis_size("chan") // count
    mine = lax.axis_index("tm") * count + lax.axis_index("chan") // rep
    denoise(cuts, slab, rim_slab, sources, tables, picks.at[mine], cleaned, coefs)
    spread(picks, cleaned, receivers, *spread_sems)
    copies[-1].wait()
    correlate(picks, receivers, held[-1], white, heard, cross)


def correlate(picks, receivers, table, white, heard, cross):
    per_window = N // BLOCK
    windows, sources = picks.shape[0] // per_window, picks.shape[1]

    def window(ref, w):
        return jnp.concatenate([ref[w * per_window + j] for j in range(per_window)], 1)

    def whiten(block):
        spectra = dot(block, table[...], False)
        scale = lax.rsqrt(jnp.mean(spectra * spectra, axis=1, keepdims=True) + 1e-05)
        return (spectra * scale).astype(jnp.bfloat16).astype(jnp.float32)

    heard_rows = [window(receivers, w).astype(jnp.float32) for w in range(windows)]
    joined = jnp.concatenate(
        [window(picks, w) for w in range(windows)]
        + [jnp.concatenate(heard_rows, 0).astype(jnp.bfloat16)],
        0,
    )
    spectra = whiten(joined)
    base = windows * sources
    for part in range(N // BLOCK):
        white[part] = spectra[:base, BLOCK * part : BLOCK * (part + 1)]
    for w in range(windows):
        heard[w] = spectra[base + 8 * w : base + 8 * w + 8]
    weight = jnp.where(lax.broadcasted_iota(jnp.int32, (1, BLOCK), 1) == 0, 1.0, 2.0)

    def body(g, carry):
        for chunk in range(BINS // BLOCK):
            lo = chunk * BLOCK
            hi = BINS + lo
            real = [None, None]
            imag = [None, None]
            for w in range(windows):
                rr = heard[w, :, lo : lo + BLOCK]
                ri = heard[w, :, hi : hi + BLOCK]
                for j in range(2):
                    spread = pl.ds(w * sources + 2 * g + j, 8, stride=0)
                    pr = white.at[chunk][spread, :]
                    pi = white.at[chunk + BINS // BLOCK][spread, :]
                    a = pr * rr + pi * ri
                    b = pi * rr - pr * ri
                    real[j] = a if real[j] is None else real[j] + a
                    imag[j] = b if imag[j] is None else imag[j] + b
            factor = weight if chunk == 0 else 2.0
            spot = pl.ds(pl.multiple_of(16 * g, 16), 16)
            cross[spot, lo : lo + BLOCK] = (jnp.concatenate(real, 0) * factor).astype(jnp.bfloat16)
            cross[spot, hi : hi + BLOCK] = (jnp.concatenate(imag, 0) * factor).astype(jnp.bfloat16)
        return carry

    lax.fori_loop(0, sources // 2, body, 0)


def lag_kernel(scale, cross, lags, out):
    out[...] = dot(cross[...], lags[...], False) * scale


def local(samples, thresholds, sources):
    n_chan, n_tm = lax.axis_size("chan"), lax.axis_size("tm")
    rows, width = samples.shape
    channels = rows * n_chan
    count = width // BLOCK
    rep = n_chan // count
    blocks = count * n_tm
    windows = n_tm * width // N
    picked_count = sources.shape[0]
    vmem = pl.BlockSpec(memory_space=pltpu.VMEM)
    hbm = pl.BlockSpec(memory_space=pltpu.HBM)
    dma = pltpu.SemaphoreType.DMA
    f32, bf16 = jnp.float32, jnp.bfloat16
    big = (40 if channels == 2 * BLOCK else 55) * 1024 * 1024

    def wide(matrix):
        return halves(matrix.reshape(-1, matrix.shape[-1]))

    def flipped(matrix):
        return np.swapaxes(matrix, -1, -2)

    def cornered(matrix):
        size = matrix.shape[-1]
        return np.pad(matrix, ((0, 0), (0, size), (0, size)))

    def pack_pair(length):
        second, third = bank_matrix(length // 2), cornered(bank_matrix(length // 4))
        return [packed(m) for m in (second, flipped(second), third, flipped(third))]

    same = channels == 2 * BLOCK
    c1, t1 = wide(bank_matrix(channels)), wide(bank_matrix(2 * BLOCK))
    chan, time = pack_pair(channels), pack_pair(2 * BLOCK)
    tables = [np.ascontiguousarray(flipped(c1)), t1, *time]
    if not same:
        tables += [c1, *chan]
    tables.append(dft_table())

    far_count = blocks // 2
    cross = pl.pallas_call(
        functools.partial(whole_kernel, len(tables), same),
        out_shape=pltpu.VMEM((picked_count * 8, N), bf16),
        in_specs=[hbm] * (3 + len(tables)),
        out_specs=vmem,
        scratch_shapes=[
            pltpu.VMEM((blocks, picked_count, BLOCK), bf16),
            pltpu.VMEM((blocks, 8, BLOCK), bf16),
            pltpu.VMEM((N // BLOCK, windows * picked_count, BLOCK), f32),
            pltpu.VMEM((windows, 8, N), f32),
        ]
        + [pltpu.VMEM(a.shape, bf16) for a in tables]
        + [
            pltpu.SMEM(thresholds.shape, jnp.int32),
            pltpu.VMEM(samples.shape, f32),
            pltpu.VMEM((1, picked_count), jnp.int32),
            dma((3,)),
        ]
        + [
            pltpu.VMEM((channels, BLOCK), f32),
            pltpu.VMEM((channels, BLOCK), bf16),
            pltpu.VMEM((count, rows, BLOCK), f32),
            pltpu.VMEM((count + 1, rows, BLOCK), bf16),
            pltpu.VMEM((channels, BLOCK), bf16),
            pltpu.VMEM((2 * channels, 4 * BLOCK), f32),
            pltpu.VMEM((channels // 8, 8, BLOCK), bf16),
            dma((len(tables),)),
            dma((2 * n_chan,)),
            dma((2 * n_chan,)),
            dma((2 * rep,)),
            dma((n_chan,)),
            dma((count,)),
            dma((far_count,)),
            dma((far_count,)),
            dma((blocks,)),
            dma((blocks,)),
            dma((blocks,)),
            dma,
        ],
        compiler_params=pltpu.CompilerParams(
            collective_id=0, has_side_effects=True, vmem_limit_bytes=big
        ),
        name="whole",
    )(*[
        pltpu.with_memory_space_constraint(a, pltpu.HBM)
        for a in (thresholds, samples, sources[None, :], *[jnp.asarray(a) for a in tables])
    ])

    half = LAGS // 2
    dft = tables[-1]
    lags = np.ascontiguousarray(np.concatenate([dft[N - half :], dft[:half]], 0).T)
    out = pl.pallas_call(
        functools.partial(lag_kernel, 1.0 / math.sqrt(windows * N)),
        out_shape=jax.ShapeDtypeStruct((picked_count * 8, LAGS), f32),
        in_specs=[vmem, vmem],
        out_specs=vmem,
        compiler_params=pltpu.CompilerParams(vmem_limit_bytes=16 * 1024 * 1024),
        name="lags",
    )(cross, jnp.asarray(lags))

    out = out.reshape(picked_count, 8, LAGS)
    share = channels // (n_chan * n_tm)
    if share < 8:
        place = lax.axis_index("chan") * n_tm + lax.axis_index("tm")
        out = lax.dynamic_slice_in_dim(out, lax.rem(place * share, 8), share, 1)
    return out


def solution(mesh):
    return jax.shard_map(
        local,
        mesh=mesh,
        in_specs=(P("chan", "tm"), P(), P()),
        out_specs=P(None, ("chan", "tm"), None),
        check_vma=False,
    )
```

```python
import functools
import math

import jax
import jax.numpy as jnp
import numpy as np
from jax import lax
from jax.experimental import pallas as pl
from jax.experimental.pallas import tpu as pltpu
from jax.sharding import PartitionSpec as P

N = 1024
LEVELS = 3
BINS = 512
LAGS = 512
BLOCK = 128
HALF = 64
MESH = pl.DeviceIdType.MESH

daubechies = [
    0.2303778133088964,
    0.7148465705529155,
    0.6308807679298587,
    -0.0279837694168599,
    -0.1870348117190931,
    0.0308413818355607,
    0.0328830116668852,
    -0.010597401785069,
]


def filter_bank():
    lowpass = list(daubechies)
    highpass = [(1.0 if k % 2 == 0 else -1.0) * daubechies[7 - k] for k in range(8)]
    return [(lowpass, highpass), (lowpass[::-1], highpass[::-1])]


def bank_matrix(length):
    half = length // 2
    out = np.zeros((2, 2, half, length))
    rows = np.arange(half)
    for tree, pair in enumerate(filter_bank()):
        for band, taps in enumerate(pair):
            for k in range(8):
                np.add.at(out[tree, band], (rows, (2 * rows + k - 3) % length), taps[k])
    return out


def levels_of(length):
    first, second, third = (bank_matrix(length >> level) for level in range(3))
    parts = [first[0, 0], first[1, 0], first[0, 1], first[1, 1]]
    for tree in range(2):
        parts += [second[tree, band] @ first[tree, 0] for band in range(2)]
    for tree in range(2):
        low = second[tree, 0] @ first[tree, 0]
        parts += [third[tree, band] @ low for band in range(2)]
    return np.concatenate(parts, 0)


def halves(matrix):
    m32 = np.asarray(matrix, np.float32)
    hi = m32.astype(jnp.bfloat16)
    lo = (m32 - hi.astype(np.float32)).astype(jnp.bfloat16)
    return np.stack([hi, lo])


def two_halves(matrix):
    return np.concatenate(list(halves(matrix)), 0)


def stacked(matrix):
    hi, lo = halves(matrix)
    n = matrix.shape[1]
    parts = [hi[: 2 * n], lo[n : 2 * n], lo[:n]]
    parts += [x[at] for at in (slice(2 * n, 3 * n), slice(3 * n, None)) for x in (hi, lo)]
    return np.concatenate(parts, 0)


def dft_table():
    t = np.arange(N)
    f = np.arange(BINS)
    phases = ((t[:, None] * f[None, :]) % N).astype(np.float64) * (2.0 * math.pi / N)
    table = np.concatenate([np.cos(phases), -np.sin(phases)], 1)
    return table.astype(np.float32).astype(jnp.bfloat16)


def split(x):
    hi = x.astype(jnp.bfloat16)
    lo = (x - hi.astype(jnp.float32)).astype(jnp.bfloat16)
    return hi, lo


def dot(a, b, trans_b):
    dims = (((1,), (1 if trans_b else 0,)), ((), ()))
    return lax.dot_general(a, b, dims, preferred_element_type=jnp.float32)


def greet_all():
    n_tm = lax.axis_size("tm")
    n = lax.axis_size("chan") * n_tm
    me = lax.axis_index("chan") * n_tm + lax.axis_index("tm")
    barrier = pltpu.get_barrier_semaphore()

    def greet(k, carry):
        d = lax.rem(me + k, n)
        pl.semaphore_signal(
            barrier, inc=1, device_id=(d // n_tm, lax.rem(d, n_tm)), device_id_type=MESH
        )
        return carry

    lax.fori_loop(1, n, greet, 0)


def gather(samples, slab, window, edge, send, recv, edge_send, edge_recv):
    n_chan, n_tm = lax.axis_size("chan"), lax.axis_size("tm")
    c, t = lax.axis_index("chan"), lax.axis_index("tm")
    rows, width = samples.shape
    count = width // BLOCK
    rep = n_chan // count
    values = samples[...]
    turned = jnp.concatenate([values[:, width - HALF :], values, values[:, :HALF]], 1)
    for j in range(count + 1):
        window[j] = turned[:, BLOCK * j : BLOCK * (j + 1)].astype(jnp.bfloat16)
    pl.semaphore_wait(pltpu.get_barrier_semaphore(), n_chan * n_tm - 1)
    mine = pl.ds(pl.multiple_of(c * rows, rows), rows)
    place = c // rep

    def remote(to, rows_at, landing):
        return pltpu.make_async_remote_copy(
            src_ref=window.at[pl.ds(to // rep, 2)],
            dst_ref=slab.at[:, rows_at, :],
            send_sem=send.at[to],
            recv_sem=recv.at[landing],
            device_id=(to, t),
            device_id_type=MESH,
        )

    def rim(to, shift, r, rows_at, landing):
        return pltpu.make_async_remote_copy(
            src_ref=window.at[0],
            dst_ref=edge.at[rows_at, :],
            send_sem=edge_send.at[r],
            recv_sem=edge_recv.at[landing],
            device_id=(to, lax.rem(t + shift, n_tm)),
            device_id_type=MESH,
        )

    def each(low, high, act):
        def body(k, carry):
            act(k)
            return carry

        lax.fori_loop(low, high, body, 0)

    def from_source(source):
        return pl.ds(pl.multiple_of(source * rows, rows), rows), source

    rim_sends = []
    for r in range(rep):
        rim_sends.append(rim(r, 1, r, mine, c))
        rim_sends.append(rim((count - 1) * rep + r, n_tm - 1, rep + r, mine, c))
    each(1, n_chan, lambda k: remote(lax.rem(c + k, n_chan), mine, c).start())
    for copy in rim_sends:
        copy.start()
    for j in range(2):
        slab[j, mine, :] = window[place + j]

    def arrived(k):
        source = lax.rem(c + n_chan - k, n_chan)
        remote(source, *from_source(source)).wait_recv()

    each(1, n_chan, arrived)

    @pl.when(jnp.logical_or(place == 0, place == count - 1))
    def _():
        each(0, n_chan, lambda source: rim(source, 1, 0, *from_source(source)).wait_recv())

    left = lax.broadcasted_iota(jnp.int32, edge.shape, 1) < HALF

    @pl.when(place == 0)
    def _():
        slab[0] = jnp.where(left, edge[...], slab[0])

    @pl.when(place == count - 1)
    def _():
        slab[1] = jnp.where(left, slab[1], edge[...])

    each(1, n_chan, lambda k: remote(lax.rem(c + k, n_chan), mine, c).wait_send())
    for copy in rim_sends:
        copy.wait_send()


def shrink(aa, ab, ba, bb, cut_one, cut_two):
    re1, im1, re2, im2 = aa - bb, ab + ba, aa + bb, ab - ba
    f1 = jnp.maximum(0.5 - cut_one * lax.rsqrt(re1 * re1 + im1 * im1), 0.0)
    f2 = jnp.maximum(0.5 - cut_two * lax.rsqrt(re2 * re2 + im2 * im2), 0.0)
    re1, im1, re2, im2 = re1 * f1, im1 * f1, re2 * f2, im2 * f2
    return re1 + re2, im1 + im2, im1 - im2, re2 - re1


def cut_of(cuts, level, orient):
    scale = math.sqrt(0.5) / 32.0
    return [cuts[level, 2 * orient + k].astype(jnp.float32) * scale for k in range(2)]


def cut_maps(cuts, level, shape):
    row_low = lax.broadcasted_iota(jnp.int32, shape, 0) < shape[0] // 2
    col_low = lax.broadcasted_iota(jnp.int32, shape, 1) < shape[1] // 2
    lh, hl, hh = (cut_of(cuts, level, o) for o in range(3))
    pick = [jnp.where(row_low, lh[k], jnp.where(col_low, hl[k], hh[k])) for k in range(2)]
    return pick[0], pick[1], jnp.logical_and(row_low, col_low)


def quarters(x):
    r, n = x.shape[0] // 2, x.shape[1] // 2
    return x[:r, :n], x[:r, n:], x[r:, :n], x[r:, n:]


def joined(parts):
    aa, ab, ba, bb = parts
    return jnp.concatenate(
        [jnp.concatenate([aa, ab], 1), jnp.concatenate([ba, bb], 1)], 0
    )


def synthesised(x, table):
    rows = x.shape[0]
    y = dot(jnp.concatenate(split(x), 0), table, False)
    return y[:rows, :BLOCK] + (y[:rows, BLOCK:] + y[rows:, :BLOCK])


def denoise(cuts, slab, chosen, tables, picked, cleaned):
    chan, chan_back, time, time_back = tables
    rows = slab.shape[1]
    length = time.shape[1]
    deep = time_back.shape[0]
    x = jnp.concatenate([slab[0], slab[1]], 1)
    y = dot(time[...], x, True)

    def timed(low, high):
        return y[low[0] : low[1]] + y[high[0] : high[1]]

    first_low = split(timed((0, length), (3 * length, 4 * length)))
    first_high = split(timed((length, 2 * length), (2 * length, 3 * length)))
    second = split(timed((4 * length, 5 * length), (5 * length, 6 * length)))
    third = split(timed((6 * length, 6 * length + length // 2), (6 * length + length // 2, 7 * length)))

    a = dot(chan[: 4 * rows, :], first_high[0], True)
    b = dot(chan[: 2 * rows, :], first_high[1], True)
    lh = joined(shrink(*quarters(a[:rows] + (a[3 * rows :] + b[:rows])), *cut_of(cuts, 0, 0)))
    hh = a[rows : 2 * rows] + (a[2 * rows : 3 * rows] + b[rows:])
    hh = joined(shrink(*quarters(hh), *cut_of(cuts, 0, 2)))
    a = dot(chan[rows : 3 * rows, :], first_low[0], True)
    b = dot(chan[rows : 2 * rows, :], first_low[1], True)
    hl = joined(shrink(*quarters(a[:rows] + (a[rows:] + b)), *cut_of(cuts, 0, 1)))

    a = dot(chan[4 * rows : 6 * rows, :], second[0], True)
    z = quarters(a[:rows] + (a[rows:] + dot(chan[4 * rows : 5 * rows, :], second[1], True)))
    one, two, kept = cut_maps(cuts, 1, z[0].shape)
    mid = joined([jnp.where(kept, 0.0, p) for p in shrink(*z, one, two)])

    a = dot(chan[6 * rows :, :], jnp.concatenate(third, 0), True)
    width = a.shape[1] // 2
    z = quarters(a[: rows // 2, :width] + (a[: rows // 2, width:] + a[rows // 2 :, :width]))
    one, two, kept = cut_maps(cuts, 2, z[0].shape)
    last = joined([jnp.where(kept, p, q) for p, q in zip(z, shrink(*z, one, two))])

    back = jnp.concatenate(
        [
            synthesised(lh, time_back[length : 2 * length, :]),
            synthesised(jnp.concatenate([hl, hh], 1), time_back[: 2 * length, :]),
            synthesised(mid, time_back[2 * length : 3 * length, :]),
            synthesised(last, time_back[3 * length : deep, :]),
        ],
        0,
    )
    y = dot(chan_back[...], jnp.concatenate(split(back), 1), False)
    whole = y[:rows, :BLOCK] + (y[:rows, BLOCK:] + y[rows:, :BLOCK])
    result = (0.25 * whole).astype(jnp.bfloat16)
    cleaned[...] = result.astype(jnp.float32).reshape(rows // 8, 8, BLOCK).astype(jnp.bfloat16)
    picked[...] = dot(chosen[...], result, False).astype(jnp.bfloat16)


def spread(picks, cleaned, receivers, near, far, across, recv, send, land, own):
    n_chan, n_tm = lax.axis_size("chan"), lax.axis_size("tm")
    c, t = lax.axis_index("chan"), lax.axis_index("tm")
    blocks = picks.shape[0]
    count = blocks // n_tm
    rep = n_chan // count
    pairs = n_tm // 2
    share = cleaned.shape[0] * 8 // (n_chan * n_tm)
    place, copy_index, core = c // rep, lax.rem(c, rep), lax.rem(t, 2)
    mine = t * count + place

    def move(block, sem, chan, tm):
        return pltpu.make_async_remote_copy(
            src_ref=picks.at[block],
            dst_ref=picks.at[block],
            send_sem=sem,
            recv_sem=recv.at[block],
            device_id=(chan, tm),
            device_id_type=MESH,
        )

    def group(k):
        return move(mine, near.at[k], lax.rem(place + k, count) * rep + copy_index, t)

    def along(u, k):
        to = lax.rem(t // 2 + u, pairs) * 2 + core
        chan = lax.rem(place + k, count) * rep + copy_index
        return move(mine, far.at[u * count + k], chan, to)

    def beside(u, k):
        other = lax.rem(t // 2 + pairs - u, pairs) * 2 + core
        block = other * count + lax.rem(place + count - k, count)
        return move(block, across.at[u * count + k], c, t + 1 - 2 * core)

    def rows_of(dc, dt):
        return (dc * n_tm + dt) * share // 8

    def personal(k):
        dc = lax.rem(place + k // n_tm, count) * rep + copy_index
        dt = lax.rem(t + lax.rem(k, n_tm), n_tm)
        return pltpu.make_async_remote_copy(
            src_ref=cleaned.at[rows_of(dc, dt)],
            dst_ref=receivers.at[mine],
            send_sem=send.at[k],
            recv_sem=land.at[mine],
            device_id=(dc, dt),
            device_id_type=MESH,
        )

    def each(low, high, act):
        def body(k, carry):
            act(k)
            return carry

        lax.fori_loop(low, high, body, 0)

    def await_block(block):
        move(block, near.at[0], c, t + 1 - 2 * core).wait_recv()

    def relay(k):
        @pl.when(k > 0)
        def _():
            await_block(t * count + lax.rem(place + count - k, count))

        beside(0, k).start()

    each(1, count, lambda k: group(k).start())
    for u in range(1, pairs):
        each(0, count, lambda k, u=u: along(u, k).start())
    local = pltpu.make_async_copy(cleaned.at[rows_of(c, t)], receivers.at[mine], own)
    local.start()
    relay(0)
    each(1, blocks, lambda k: personal(k).start())
    each(1, count, relay)
    for u in range(1, pairs):

        def cross_over(k, u=u):
            other = lax.rem(t // 2 + pairs - u, pairs) * 2 + core
            await_block(other * count + lax.rem(place + count - k, count))
            beside(u, k).start()

        each(0, count, cross_over)
    for u in range(pairs):

        def last(k, u=u):
            other = lax.rem(t // 2 + pairs - u, pairs) * 2 + 1 - core
            await_block(other * count + lax.rem(place + count - k, count))

        each(0, count, last)

    def landed(k):
        block = lax.rem(mine + k, blocks)
        pltpu.make_async_remote_copy(
            src_ref=cleaned.at[0],
            dst_ref=receivers.at[block],
            send_sem=send.at[0],
            recv_sem=land.at[block],
            device_id=(c, t + 1 - 2 * core),
            device_id_type=MESH,
        ).wait_recv()

    local.wait()
    each(1, blocks, landed)
    each(1, count, lambda k: group(k).wait_send())
    each(1, blocks, lambda k: personal(k).wait_send())
    for u in range(pairs):
        each(0, count, lambda k, u=u: beside(u, k).wait_send())
        if u:
            each(0, count, lambda k, u=u: along(u, k).wait_send())


def whole_kernel(n_tables, cuts, samples, sources, *refs):
    stored, refs = refs[:n_tables], refs[n_tables:]
    cross, picks, receivers, white, heard = refs[:5]
    held, refs = refs[5 : 5 + n_tables], refs[5 + n_tables :]
    here, refs = refs[:4], refs[4:]
    slab, window, edge, chosen, cleaned, loads = refs[:6]
    gather_sems, spread_sems = refs[6:10], refs[10:]
    inputs = [
        pltpu.make_async_copy(a, b, here[3].at[i])
        for i, (a, b) in enumerate(zip((cuts, samples, sources), here))
    ]
    inputs[1].start()
    greet_all()
    inputs[0].start()
    inputs[2].start()
    copies = [pltpu.make_async_copy(a, b, loads.at[i]) for i, (a, b) in enumerate(zip(stored, held))]
    for copy in copies:
        copy.start()
    inputs[2].wait()
    cuts, samples, sources = here[:3]
    one_hot = jnp.where(
        lax.broadcasted_iota(jnp.int32, chosen.shape[::-1], 0) == sources[...], 1.0, 0.0
    )
    chosen[...] = jnp.transpose(one_hot).astype(jnp.bfloat16)
    inputs[1].wait()
    gather(samples, slab, window, edge, *gather_sems)
    inputs[0].wait()
    for copy in copies[:-1]:
        copy.wait()
    time, time_back, chan_back = held[:3]
    chan = held[3] if n_tables == 5 else time
    n_tm = lax.axis_size("tm")
    count = picks.shape[0] // n_tm
    rep = lax.axis_size("chan") // count
    mine = lax.axis_index("tm") * count + lax.axis_index("chan") // rep
    denoise(cuts, slab, chosen, (chan, chan_back, time, time_back), picks.at[mine], cleaned)
    spread(picks, cleaned, receivers, *spread_sems)
    copies[-1].wait()
    correlate(picks, receivers, held[-1], white, heard, cross)


def correlate(picks, receivers, table, white, heard, cross):
    per_window = N // BLOCK
    windows, sources = picks.shape[0] // per_window, picks.shape[1]

    def window(ref, w):
        return jnp.concatenate([ref[w * per_window + j] for j in range(per_window)], 1)

    def whiten(block):
        spectra = dot(block, table[...], False)
        scale = lax.rsqrt(jnp.mean(spectra * spectra, axis=1, keepdims=True) + 1e-05)
        return (spectra * scale).astype(jnp.bfloat16).astype(jnp.float32)

    heard_rows = [window(receivers, w).astype(jnp.float32) for w in range(windows)]
    joined = jnp.concatenate(
        [window(picks, w) for w in range(windows)]
        + [jnp.concatenate(heard_rows, 0).astype(jnp.bfloat16)],
        0,
    )
    spectra = whiten(joined)
    base = windows * sources
    for part in range(N // BLOCK):
        white[part] = spectra[:base, BLOCK * part : BLOCK * (part + 1)]
    for w in range(windows):
        heard[w] = spectra[base + 8 * w : base + 8 * w + 8]
    weight = jnp.where(lax.broadcasted_iota(jnp.int32, (1, BLOCK), 1) == 0, 1.0, 2.0)

    def body(g, carry):
        for chunk in range(BINS // BLOCK):
            lo = chunk * BLOCK
            hi = BINS + lo
            real = [None, None]
            imag = [None, None]
            for w in range(windows):
                rr = heard[w, :, lo : lo + BLOCK]
                ri = heard[w, :, hi : hi + BLOCK]
                for j in range(2):
                    spread = pl.ds(w * sources + 2 * g + j, 8, stride=0)
                    pr = white.at[chunk][spread, :]
                    pi = white.at[chunk + BINS // BLOCK][spread, :]
                    a = pr * rr + pi * ri
                    b = pi * rr - pr * ri
                    real[j] = a if real[j] is None else real[j] + a
                    imag[j] = b if imag[j] is None else imag[j] + b
            factor = weight if chunk == 0 else 2.0
            spot = pl.ds(pl.multiple_of(16 * g, 16), 16)
            cross[spot, lo : lo + BLOCK] = (jnp.concatenate(real, 0) * factor).astype(jnp.bfloat16)
            cross[spot, hi : hi + BLOCK] = (jnp.concatenate(imag, 0) * factor).astype(jnp.bfloat16)
        return carry

    lax.fori_loop(0, sources // 2, body, 0)


def lag_kernel(scale, cross, lags, out):
    out[...] = dot(cross[...], lags[...], False) * scale


def local(samples, thresholds, sources):
    n_chan, n_tm = lax.axis_size("chan"), lax.axis_size("tm")
    rows, width = samples.shape
    channels = rows * n_chan
    count = width // BLOCK
    rep = n_chan // count
    blocks = count * n_tm
    windows = n_tm * width // N
    picked_count = sources.shape[0]
    vmem = pl.BlockSpec(memory_space=pltpu.VMEM)
    hbm = pl.BlockSpec(memory_space=pltpu.HBM)
    dma = pltpu.SemaphoreType.DMA
    f32, bf16 = jnp.float32, jnp.bfloat16
    big = (40 if channels == 2 * BLOCK else 55) * 1024 * 1024

    time = stacked(levels_of(2 * BLOCK))
    back = halves(levels_of(2 * BLOCK)[:, HALF : HALF + BLOCK])
    chan = levels_of(channels)
    chan_back = two_halves(np.ascontiguousarray(chan.T))
    tables = [time, np.concatenate([back[0], back[1]], 1), chan_back]
    if channels != 2 * BLOCK:
        tables.append(stacked(chan))
    tables.append(dft_table())

    far_count = blocks // 2
    cross = pl.pallas_call(
        functools.partial(whole_kernel, len(tables)),
        out_shape=pltpu.VMEM((picked_count * 8, N), bf16),
        in_specs=[hbm] * (3 + len(tables)),
        out_specs=vmem,
        scratch_shapes=[
            pltpu.VMEM((blocks, picked_count, BLOCK), bf16),
            pltpu.VMEM((blocks, 8, BLOCK), bf16),
            pltpu.VMEM((N // BLOCK, windows * picked_count, BLOCK), f32),
            pltpu.VMEM((windows, 8, N), f32),
        ]
        + [pltpu.VMEM(a.shape, bf16) for a in tables]
        + [
            pltpu.SMEM(thresholds.shape, jnp.int32),
            pltpu.VMEM(samples.shape, f32),
            pltpu.VMEM((1, picked_count), jnp.int32),
            dma((3,)),
        ]
        + [
            pltpu.VMEM((2, channels, BLOCK), bf16),
            pltpu.VMEM((count + 1, rows, BLOCK), bf16),
            pltpu.VMEM((channels, BLOCK), bf16),
            pltpu.VMEM((picked_count, channels), bf16),
            pltpu.VMEM((channels // 8, 8, BLOCK), bf16),
            dma((len(tables),)),
            dma((n_chan,)),
            dma((n_chan,)),
            dma((2 * rep,)),
            dma((n_chan,)),
            dma((count,)),
            dma((far_count,)),
            dma((far_count,)),
            dma((blocks,)),
            dma((blocks,)),
            dma((blocks,)),
            dma,
        ],
        compiler_params=pltpu.CompilerParams(
            collective_id=0, has_side_effects=True, vmem_limit_bytes=big
        ),
        name="whole",
    )(*[
        pltpu.with_memory_space_constraint(a, pltpu.HBM)
        for a in (thresholds, samples, sources[None, :], *[jnp.asarray(a) for a in tables])
    ])

    half = LAGS // 2
    dft = tables[-1]
    lags = np.ascontiguousarray(np.concatenate([dft[N - half :], dft[:half]], 0).T)
    out = pl.pallas_call(
        functools.partial(lag_kernel, 1.0 / math.sqrt(windows * N)),
        out_shape=jax.ShapeDtypeStruct((picked_count * 8, LAGS), f32),
        in_specs=[vmem, vmem],
        out_specs=vmem,
        compiler_params=pltpu.CompilerParams(vmem_limit_bytes=16 * 1024 * 1024),
        name="lags",
    )(cross, jnp.asarray(lags))

    out = out.reshape(picked_count, 8, LAGS)
    share = channels // (n_chan * n_tm)
    if share < 8:
        place = lax.axis_index("chan") * n_tm + lax.axis_index("tm")
        out = lax.dynamic_slice_in_dim(out, lax.rem(place * share, 8), share, 1)
    return out


def solution(mesh):
    return jax.shard_map(
        local,
        mesh=mesh,
        in_specs=(P("chan", "tm"), P(), P()),
        out_specs=P(None, ("chan", "tm"), None),
        check_vma=False,
    )
```

```python
import functools
import math

import jax
import jax.numpy as jnp
import numpy as np
from jax import lax
from jax.experimental import pallas as pl
from jax.experimental.pallas import tpu as pltpu
from jax.sharding import PartitionSpec as P

N = 1024
LEVELS = 3
BINS = 512
LAGS = 512
BLOCK = 128
HALF = 64
MESH = pl.DeviceIdType.MESH

daubechies = [
    0.2303778133088964,
    0.7148465705529155,
    0.6308807679298587,
    -0.0279837694168599,
    -0.1870348117190931,
    0.0308413818355607,
    0.0328830116668852,
    -0.010597401785069,
]


def filter_bank():
    lowpass = list(daubechies)
    highpass = [(1.0 if k % 2 == 0 else -1.0) * daubechies[7 - k] for k in range(8)]
    return [(lowpass, highpass), (lowpass[::-1], highpass[::-1])]


def bank_matrix(length):
    half = length // 2
    out = np.zeros((2, 2, half, length))
    rows = np.arange(half)
    for tree, pair in enumerate(filter_bank()):
        for band, taps in enumerate(pair):
            for k in range(8):
                np.add.at(out[tree, band], (rows, (2 * rows + k - 3) % length), taps[k])
    return out


def levels_of(length):
    first, second, third = (bank_matrix(length >> level) for level in range(3))
    parts = [first[0, 0], first[1, 0], first[0, 1], first[1, 1]]
    for tree in range(2):
        parts += [second[tree, band] @ first[tree, 0] for band in range(2)]
    for tree in range(2):
        low = second[tree, 0] @ first[tree, 0]
        parts += [third[tree, band] @ low for band in range(2)]
    return np.concatenate(parts, 0)


def halves(matrix):
    m32 = np.asarray(matrix, np.float32)
    hi = m32.astype(jnp.bfloat16)
    lo = (m32 - hi.astype(np.float32)).astype(jnp.bfloat16)
    return np.stack([hi, lo])


def two_halves(matrix):
    return np.concatenate(list(halves(matrix)), 0)


def stacked(matrix):
    hi, lo = halves(matrix)
    n = matrix.shape[1]
    parts = [hi[: 2 * n], lo[n : 2 * n], lo[:n]]
    parts += [x[at] for at in (slice(2 * n, 3 * n), slice(3 * n, None)) for x in (hi, lo)]
    return np.concatenate(parts, 0)


def dft_table():
    t = np.arange(N)
    f = np.arange(BINS)
    phases = ((t[:, None] * f[None, :]) % N).astype(np.float64) * (2.0 * math.pi / N)
    table = np.concatenate([np.cos(phases), -np.sin(phases)], 1)
    return table.astype(np.float32).astype(jnp.bfloat16)


def split(x):
    hi = x.astype(jnp.bfloat16)
    lo = (x - hi.astype(jnp.float32)).astype(jnp.bfloat16)
    return hi, lo


def dot(a, b, trans_b):
    dims = (((1,), (1 if trans_b else 0,)), ((), ()))
    return lax.dot_general(a, b, dims, preferred_element_type=jnp.float32)


def wrap(x, n):
    return jnp.where(x >= n, x - n, x)


def ratio(x, n):
    return x if n == 1 else x // n


def each(low, high, act):
    def body(k, carry):
        act(k)
        return carry

    if high - low <= 1:
        for k in range(low, high):
            act(k)
    else:
        lax.fori_loop(low, high, body, 0)


def greet_all():
    n_chan, n_tm = lax.axis_size("chan"), lax.axis_size("tm")
    c, t = lax.axis_index("chan"), lax.axis_index("tm")
    barrier = pltpu.get_barrier_semaphore()
    for j in range(n_tm):
        to = wrap(t + j, n_tm)

        def greet(k, to=to):
            pl.semaphore_signal(
                barrier, inc=1, device_id=(wrap(c + k, n_chan), to), device_id_type=MESH
            )

        each(0 if j else 1, n_chan, greet)


def gather(samples, slab, window, edge, sent, recv, edge_sent, edge_recv):
    n_chan, n_tm = lax.axis_size("chan"), lax.axis_size("tm")
    c, t = lax.axis_index("chan"), lax.axis_index("tm")
    rows, width = samples.shape
    channels = slab.shape[1]
    count = width // BLOCK
    rep = n_chan // count
    values = samples[...]
    turned = jnp.concatenate([values[:, width - HALF :], values, values[:, :HALF]], 1)
    for j in range(count + 1):
        window[j] = turned[:, BLOCK * j : BLOCK * (j + 1)].astype(jnp.bfloat16)
    pl.semaphore_wait(pltpu.get_barrier_semaphore(), n_chan * n_tm - 1)
    mine = pl.ds(pl.multiple_of(c * rows, rows), rows)
    place = ratio(c, rep)

    def remote(to):
        return pltpu.make_async_remote_copy(
            src_ref=window.at[pl.ds(ratio(to, rep), 2)],
            dst_ref=slab.at[:, mine, :],
            send_sem=sent,
            recv_sem=recv,
            device_id=(to, t),
            device_id_type=MESH,
        )

    def rim(to, shift):
        return pltpu.make_async_remote_copy(
            src_ref=window.at[0],
            dst_ref=edge.at[mine, :],
            send_sem=edge_sent,
            recv_sem=edge_recv,
            device_id=(to, wrap(t + shift, n_tm)),
            device_id_type=MESH,
        )

    each(1, n_chan, lambda k: remote(n_chan - k - jnp.where(c >= n_chan - k, 1, 0)).start())
    for r in range(rep):
        rim(r, 1).start()
        rim((count - 1) * rep + r, n_tm - 1).start()
    for j in range(2):
        slab[j, mine, :] = window[place + j]

    def bytes_of(ref, sem):
        return pltpu.make_async_copy(ref, ref, sem)

    others = channels - rows
    bytes_of(slab.at[:, pl.ds(0, others), :], recv).wait()

    @pl.when(jnp.logical_or(place == 0, place == count - 1))
    def _():
        bytes_of(edge, edge_recv).wait()

    left = lax.broadcasted_iota(jnp.int32, edge.shape, 1) < HALF

    @pl.when(place == 0)
    def _():
        slab[0] = jnp.where(left, edge[...], slab[0])

    @pl.when(place == count - 1)
    def _():
        slab[1] = jnp.where(left, slab[1], edge[...])

    def settle():
        bytes_of(slab.at[:, pl.ds(0, others), :], sent).wait()
        bytes_of(window.at[pl.ds(0, 2 * rep)], edge_sent).wait()

    return settle


def shrink(aa, ab, ba, bb, cut_one, cut_two):
    re1, im1, re2, im2 = aa - bb, ab + ba, aa + bb, ab - ba
    f1 = jnp.maximum(0.5 - cut_one * lax.rsqrt(re1 * re1 + im1 * im1), 0.0)
    f2 = jnp.maximum(0.5 - cut_two * lax.rsqrt(re2 * re2 + im2 * im2), 0.0)
    re1, im1, re2, im2 = re1 * f1, im1 * f1, re2 * f2, im2 * f2
    return re1 + re2, im1 + im2, im1 - im2, re2 - re1


def cut_of(cuts, level, orient):
    scale = math.sqrt(0.5) / 32.0
    return [cuts[level, 2 * orient + k].astype(jnp.float32) * scale for k in range(2)]


def cut_maps(cuts, level, shape):
    row_low = lax.broadcasted_iota(jnp.int32, shape, 0) < shape[0] // 2
    col_low = lax.broadcasted_iota(jnp.int32, shape, 1) < shape[1] // 2
    lh, hl, hh = (cut_of(cuts, level, o) for o in range(3))
    pick = [jnp.where(row_low, lh[k], jnp.where(col_low, hl[k], hh[k])) for k in range(2)]
    return pick[0], pick[1], jnp.logical_and(row_low, col_low)


def quarters(x):
    r, n = x.shape[0] // 2, x.shape[1] // 2
    return x[:r, :n], x[:r, n:], x[r:, :n], x[r:, n:]


def joined(parts):
    aa, ab, ba, bb = parts
    return jnp.concatenate(
        [jnp.concatenate([aa, ab], 1), jnp.concatenate([ba, bb], 1)], 0
    )


def synthesised(x, table):
    rows = x.shape[0]
    y = dot(jnp.concatenate(split(x), 0), table, False)
    return y[:rows, :BLOCK] + (y[:rows, BLOCK:] + y[rows:, :BLOCK])


def denoise(cuts, slab, chosen, tables, picked, cleaned):
    chan, chan_back, time, time_back = tables
    rows = slab.shape[1]
    length = time.shape[1]
    deep = time_back.shape[0]
    x = jnp.concatenate([slab[0], slab[1]], 1)
    y = dot(time[...], x, True)

    def timed(low, high):
        return y[low[0] : low[1]] + y[high[0] : high[1]]

    first_low = split(timed((0, length), (3 * length, 4 * length)))
    first_high = split(timed((length, 2 * length), (2 * length, 3 * length)))
    second = split(timed((4 * length, 5 * length), (5 * length, 6 * length)))
    third = split(timed((6 * length, 6 * length + length // 2), (6 * length + length // 2, 7 * length)))

    a = dot(chan[: 4 * rows, :], first_high[0], True)
    b = dot(chan[: 2 * rows, :], first_high[1], True)
    lh = joined(shrink(*quarters(a[:rows] + (a[3 * rows :] + b[:rows])), *cut_of(cuts, 0, 0)))
    hh = a[rows : 2 * rows] + (a[2 * rows : 3 * rows] + b[rows:])
    hh = joined(shrink(*quarters(hh), *cut_of(cuts, 0, 2)))
    a = dot(chan[rows : 3 * rows, :], first_low[0], True)
    b = dot(chan[rows : 2 * rows, :], first_low[1], True)
    hl = joined(shrink(*quarters(a[:rows] + (a[rows:] + b)), *cut_of(cuts, 0, 1)))

    a = dot(chan[4 * rows : 6 * rows, :], second[0], True)
    z = quarters(a[:rows] + (a[rows:] + dot(chan[4 * rows : 5 * rows, :], second[1], True)))
    one, two, kept = cut_maps(cuts, 1, z[0].shape)
    mid = joined([jnp.where(kept, 0.0, p) for p in shrink(*z, one, two)])

    a = dot(chan[6 * rows :, :], jnp.concatenate(third, 0), True)
    width = a.shape[1] // 2
    z = quarters(a[: rows // 2, :width] + (a[: rows // 2, width:] + a[rows // 2 :, :width]))
    one, two, kept = cut_maps(cuts, 2, z[0].shape)
    last = joined([jnp.where(kept, p, q) for p, q in zip(z, shrink(*z, one, two))])

    back = jnp.concatenate(
        [
            synthesised(lh, time_back[length : 2 * length, :]),
            synthesised(jnp.concatenate([hl, hh], 1), time_back[: 2 * length, :]),
            synthesised(mid, time_back[2 * length : 3 * length, :]),
            synthesised(last, time_back[3 * length : deep, :]),
        ],
        0,
    )
    y = dot(chan_back[...], jnp.concatenate(split(back), 1), False)
    whole = y[:rows, :BLOCK] + (y[:rows, BLOCK:] + y[rows:, :BLOCK])
    result = (0.25 * whole).astype(jnp.bfloat16)
    cleaned[...] = result.astype(jnp.float32).reshape(rows // 8, 8, BLOCK).astype(jnp.bfloat16)
    picked[...] = dot(chosen[...], result, False).astype(jnp.bfloat16)


def spread(picks, cleaned, receivers, sent, recv, crossed, sent_rows, landed):
    n_chan, n_tm = lax.axis_size("chan"), lax.axis_size("tm")
    c, t = lax.axis_index("chan"), lax.axis_index("tm")
    blocks = picks.shape[0]
    count = blocks // n_tm
    rep = n_chan // count
    pairs = n_tm // 2
    share = cleaned.shape[0] * 8 // (n_chan * n_tm)
    place = ratio(c, rep)
    copy_index = c - place * rep
    pair = t // 2
    core = t - 2 * pair
    other_core = t + 1 - 2 * core
    mine = t * count + place

    def move(block, sem, chan, tm):
        return pltpu.make_async_remote_copy(
            src_ref=picks.at[block],
            dst_ref=picks.at[block],
            send_sem=sent,
            recv_sem=sem,
            device_id=(chan, tm),
            device_id_type=MESH,
        )

    def chan_of(place):
        return place * rep + copy_index

    def block_at(k, u):
        tm = t if u == 0 else wrap(pair + pairs - u, pairs) * 2 + core
        return tm * count + (place if isinstance(k, int) and k == 0 else wrap(place + count - k, count))

    def rows_of(dc, dt):
        at = dc * n_tm + dt
        return at * (share // 8) if share % 8 == 0 else at * share // 8

    def personal(k):
        to = k + jnp.where(k >= place * n_tm + t, 1, 0)
        chan, to_tm = chan_of(to // n_tm), lax.rem(to, n_tm)
        return pltpu.make_async_remote_copy(
            src_ref=cleaned.at[rows_of(chan, to_tm)],
            dst_ref=receivers.at[mine],
            send_sem=sent_rows,
            recv_sem=landed,
            device_id=(chan, to_tm),
            device_id_type=MESH,
        )

    def relay(k, u):
        block = block_at(k, u)
        copy = move(block, crossed, c, other_core)
        if u or not isinstance(k, int) or k:
            move(block, recv.at[block], c, other_core).wait_recv()
        copy.start()

    def along_chan(k):
        to = k + jnp.where(k >= place, 1, 0)
        move(mine, recv.at[mine], chan_of(to), t).start()

    each(0, count - 1, along_chan)
    for u in range(1, pairs):
        to = wrap(pair + u, pairs) * 2 + core
        each(0, count, lambda k, to=to: move(mine, recv.at[mine], chan_of(k), to).start())
    local = pltpu.make_async_copy(cleaned.at[rows_of(c, t)], receivers.at[mine], landed)
    local.start()
    relay(0, 0)
    each(0, blocks - 1, lambda k: personal(k).start())
    for u in range(pairs):
        each(0 if u else 1, count, lambda k, u=u: relay(k, u))

    def bytes_of(ref, sem):
        return pltpu.make_async_copy(ref, ref, sem)

    bytes_of(picks.at[pl.ds(0, blocks // 2)], crossed).wait()
    bytes_of(receivers, landed).wait()

    def settle():
        bytes_of(picks.at[pl.ds(0, blocks - 1)], sent).wait()
        bytes_of(receivers.at[pl.ds(0, blocks - 1)], sent_rows).wait()

    return settle


def whole_kernel(n_tables, cuts, samples, sources, *refs):
    stored, refs = refs[:n_tables], refs[n_tables:]
    cross, picks, receivers, white, heard = refs[:5]
    held, refs = refs[5 : 5 + n_tables], refs[5 + n_tables :]
    here, refs = refs[:4], refs[4:]
    slab, window, edge, chosen, cleaned, loads = refs[:6]
    gather_sems, spread_sems = refs[6:10], refs[10:]
    inputs = [
        pltpu.make_async_copy(a, b, here[3].at[i])
        for i, (a, b) in enumerate(zip((cuts, samples, sources), here))
    ]
    inputs[1].start()
    greet_all()
    inputs[0].start()
    inputs[2].start()
    copies = [pltpu.make_async_copy(a, b, loads.at[i]) for i, (a, b) in enumerate(zip(stored, held))]
    for copy in copies:
        copy.start()
    inputs[2].wait()
    cuts, samples, sources = here[:3]
    one_hot = jnp.where(
        lax.broadcasted_iota(jnp.int32, chosen.shape[::-1], 0) == sources[...], 1.0, 0.0
    )
    chosen[...] = jnp.transpose(one_hot).astype(jnp.bfloat16)
    inputs[1].wait()
    gathered = gather(samples, slab, window, edge, *gather_sems)
    inputs[0].wait()
    for copy in copies[:-1]:
        copy.wait()
    time, time_back, chan_back = held[:3]
    chan = held[3] if n_tables == 5 else time
    n_tm = lax.axis_size("tm")
    count = picks.shape[0] // n_tm
    rep = lax.axis_size("chan") // count
    mine = lax.axis_index("tm") * count + ratio(lax.axis_index("chan"), rep)
    denoise(cuts, slab, chosen, (chan, chan_back, time, time_back), picks.at[mine], cleaned)
    spreading = spread(picks, cleaned, receivers, *spread_sems)
    copies[-1].wait()
    correlate(picks, receivers, held[-1], white, heard, cross)
    gathered()
    spreading()


def correlate(picks, receivers, table, white, heard, cross):
    per_window = N // BLOCK
    windows, sources = picks.shape[0] // per_window, picks.shape[1]

    def window(ref, w):
        return jnp.concatenate([ref[w * per_window + j] for j in range(per_window)], 1)

    def whiten(block):
        spectra = dot(block, table[...], False)
        scale = lax.rsqrt(jnp.mean(spectra * spectra, axis=1, keepdims=True) + 1e-05)
        return (spectra * scale).astype(jnp.bfloat16).astype(jnp.float32)

    heard_rows = [window(receivers, w).astype(jnp.float32) for w in range(windows)]
    joined = jnp.concatenate(
        [window(picks, w) for w in range(windows)]
        + [jnp.concatenate(heard_rows, 0).astype(jnp.bfloat16)],
        0,
    )
    spectra = whiten(joined)
    base = windows * sources
    chunks = BINS // BLOCK
    weight = jnp.where(lax.broadcasted_iota(jnp.int32, (1, BLOCK), 1) == 0, 1.0, 2.0)
    for part in range(chunks):
        real = spectra[:, BLOCK * part : BLOCK * (part + 1)]
        imag = spectra[:, BINS + BLOCK * part : BINS + BLOCK * (part + 1)]
        white[part] = real[:base]
        white[chunks + part] = imag[:base]
        white[2 * chunks + part] = real[:base] + imag[:base]
        real, imag = (x[base:] * (2.0 if part else weight) for x in (real, imag))
        heard[part] = real
        heard[chunks + part] = real + imag
        heard[2 * chunks + part] = real - imag

    for part in range(chunks):
        around = [
            [heard[kind * chunks + part, 8 * w : 8 * w + 8, :] for kind in range(3)]
            for w in range(windows)
        ]
        lo = part * BLOCK
        hi = BINS + lo

        def body(g, carry, part=part, around=around, lo=lo, hi=hi):
            real, imag = [], []
            for j in range(16):
                sums = [None] * 3
                for w in range(windows):
                    spot = pl.ds(w * sources + 16 * g + j, 8, stride=0)
                    for n, (kind, near) in enumerate(zip((2, 0, 1), around[w])):
                        term = white.at[kind * chunks + part][spot, :] * near
                        sums[n] = term if sums[n] is None else sums[n] + term
                real.append(sums[0] - sums[2])
                imag.append(sums[0] - sums[1])
            spot = pl.ds(pl.multiple_of(128 * g, 128), 128)
            cross[spot, lo : lo + BLOCK] = jnp.concatenate(real, 0).astype(jnp.bfloat16)
            cross[spot, hi : hi + BLOCK] = jnp.concatenate(imag, 0).astype(jnp.bfloat16)
            return carry

        lax.fori_loop(0, sources // 16, body, 0)


def lag_kernel(scale, cross, lags, out):
    out[...] = dot(cross[...], lags[...], False) * scale


def local(samples, thresholds, sources):
    n_chan, n_tm = lax.axis_size("chan"), lax.axis_size("tm")
    rows, width = samples.shape
    channels = rows * n_chan
    count = width // BLOCK
    rep = n_chan // count
    blocks = count * n_tm
    windows = n_tm * width // N
    picked_count = sources.shape[0]
    vmem = pl.BlockSpec(memory_space=pltpu.VMEM)
    hbm = pl.BlockSpec(memory_space=pltpu.HBM)
    dma = pltpu.SemaphoreType.DMA
    f32, bf16 = jnp.float32, jnp.bfloat16
    big = (40 if channels == 2 * BLOCK else 55) * 1024 * 1024

    time = stacked(levels_of(2 * BLOCK))
    back = halves(levels_of(2 * BLOCK)[:, HALF : HALF + BLOCK])
    chan = levels_of(channels)
    chan_back = two_halves(np.ascontiguousarray(chan.T))
    tables = [time, np.concatenate([back[0], back[1]], 1), chan_back]
    if channels != 2 * BLOCK:
        tables.append(stacked(chan))
    tables.append(dft_table())

    cross = pl.pallas_call(
        functools.partial(whole_kernel, len(tables)),
        out_shape=pltpu.VMEM((picked_count * 8, N), bf16),
        in_specs=[hbm] * (3 + len(tables)),
        out_specs=vmem,
        scratch_shapes=[
            pltpu.VMEM((blocks, picked_count, BLOCK), bf16),
            pltpu.VMEM((blocks, 8, BLOCK), bf16),
            pltpu.VMEM((3 * BINS // BLOCK, windows * picked_count, BLOCK), f32),
            pltpu.VMEM((3 * BINS // BLOCK, windows * 8, BLOCK), f32),
        ]
        + [pltpu.VMEM(a.shape, bf16) for a in tables]
        + [
            pltpu.SMEM(thresholds.shape, jnp.int32),
            pltpu.VMEM(samples.shape, f32),
            pltpu.VMEM((1, picked_count), jnp.int32),
            dma((3,)),
        ]
        + [
            pltpu.VMEM((2, channels, BLOCK), bf16),
            pltpu.VMEM((count + 1, rows, BLOCK), bf16),
            pltpu.VMEM((channels, BLOCK), bf16),
            pltpu.VMEM((picked_count, channels), bf16),
            pltpu.VMEM((channels // 8, 8, BLOCK), bf16),
            dma((len(tables),)),
            dma,
            dma,
            dma,
            dma,
            dma,
            dma((blocks,)),
            dma,
            dma,
            dma,
        ],
        compiler_params=pltpu.CompilerParams(
            collective_id=0, has_side_effects=True, vmem_limit_bytes=big
        ),
        name="whole",
    )(*[
        pltpu.with_memory_space_constraint(a, pltpu.HBM)
        for a in (thresholds, samples, sources[None, :], *[jnp.asarray(a) for a in tables])
    ])

    half = LAGS // 2
    dft = tables[-1]
    lags = np.ascontiguousarray(np.concatenate([dft[N - half :], dft[:half]], 0).T)
    out = pl.pallas_call(
        functools.partial(lag_kernel, 1.0 / math.sqrt(windows * N)),
        out_shape=jax.ShapeDtypeStruct((picked_count * 8, LAGS), f32),
        in_specs=[vmem, vmem],
        out_specs=vmem,
        compiler_params=pltpu.CompilerParams(vmem_limit_bytes=16 * 1024 * 1024),
        name="lags",
    )(cross, jnp.asarray(lags))

    out = out.reshape(picked_count, 8, LAGS)
    share = channels // (n_chan * n_tm)
    if share < 8:
        place = lax.axis_index("chan") * n_tm + lax.axis_index("tm")
        out = lax.dynamic_slice_in_dim(out, lax.rem(place * share, 8), share, 1)
    return out


def solution(mesh):
    return jax.shard_map(
        local,
        mesh=mesh,
        in_specs=(P("chan", "tm"), P(), P()),
        out_specs=P(None, ("chan", "tm"), None),
        check_vma=False,
    )
```

```python
import functools
import math

import jax
import jax.numpy as jnp
import numpy as np
from jax import lax
from jax.experimental import pallas as pl
from jax.experimental.pallas import tpu as pltpu
from jax.sharding import PartitionSpec as P

N = 1024
LEVELS = 3
BINS = 512
LAGS = 512
BLOCK = 128
HALF = 64
MESH = pl.DeviceIdType.MESH

daubechies = [
    0.2303778133088964,
    0.7148465705529155,
    0.6308807679298587,
    -0.0279837694168599,
    -0.1870348117190931,
    0.0308413818355607,
    0.0328830116668852,
    -0.010597401785069,
]


def filter_bank():
    lowpass = list(daubechies)
    highpass = [(1.0 if k % 2 == 0 else -1.0) * daubechies[7 - k] for k in range(8)]
    return [(lowpass, highpass), (lowpass[::-1], highpass[::-1])]


def bank_matrix(length):
    half = length // 2
    out = np.zeros((2, 2, half, length))
    rows = np.arange(half)
    for tree, pair in enumerate(filter_bank()):
        for band, taps in enumerate(pair):
            for k in range(8):
                np.add.at(out[tree, band], (rows, (2 * rows + k - 3) % length), taps[k])
    return out


def levels_of(length):
    first, second, third = (bank_matrix(length >> level) for level in range(3))
    parts = [first[0, 0], first[1, 0], first[0, 1], first[1, 1]]
    for tree in range(2):
        parts += [second[tree, band] @ first[tree, 0] for band in range(2)]
    for tree in range(2):
        low = second[tree, 0] @ first[tree, 0]
        parts += [third[tree, band] @ low for band in range(2)]
    return np.concatenate(parts, 0)


def halves(matrix):
    m32 = np.asarray(matrix, np.float32)
    hi = m32.astype(jnp.bfloat16)
    lo = (m32 - hi.astype(np.float32)).astype(jnp.bfloat16)
    return np.stack([hi, lo])


def two_halves(matrix):
    return np.concatenate(list(halves(matrix)), 0)


def stacked(matrix):
    hi, lo = halves(matrix)
    n = matrix.shape[1]
    parts = [hi[: 2 * n], lo[n : 2 * n], lo[:n]]
    parts += [x[at] for at in (slice(2 * n, 3 * n), slice(3 * n, None)) for x in (hi, lo)]
    return np.concatenate(parts, 0)


def dft_table():
    t = np.arange(N)
    f = np.arange(BINS)
    phases = ((t[:, None] * f[None, :]) % N).astype(np.float64) * (2.0 * math.pi / N)
    table = np.concatenate([np.cos(phases), -np.sin(phases)], 1)
    return table.astype(np.float32).astype(jnp.bfloat16)


def split(x):
    hi = x.astype(jnp.bfloat16)
    lo = (x - hi.astype(jnp.float32)).astype(jnp.bfloat16)
    return hi, lo


def dot(a, b, trans_b):
    dims = (((1,), (1 if trans_b else 0,)), ((), ()))
    return lax.dot_general(a, b, dims, preferred_element_type=jnp.float32)


def wrap(x, n):
    return jnp.where(x >= n, x - n, x)


def ratio(x, n):
    return x if n == 1 else x // n


def each(low, high, act):
    def body(k, carry):
        act(k)
        return carry

    if high - low <= 1:
        for k in range(low, high):
            act(k)
    else:
        lax.fori_loop(low, high, body, 0)


def greet_all():
    n_chan, n_tm = lax.axis_size("chan"), lax.axis_size("tm")
    c, t = lax.axis_index("chan"), lax.axis_index("tm")
    barrier = pltpu.get_barrier_semaphore()
    for j in range(n_tm):
        to = wrap(t + j, n_tm)

        def greet(k, to=to):
            pl.semaphore_signal(
                barrier, inc=1, device_id=(wrap(c + k, n_chan), to), device_id_type=MESH
            )

        each(0 if j else 1, n_chan, greet)


def gather(samples, slab, window, edge, sent, recv, edge_sent, edge_recv):
    n_chan, n_tm = lax.axis_size("chan"), lax.axis_size("tm")
    c, t = lax.axis_index("chan"), lax.axis_index("tm")
    rows, width = samples.shape
    channels = slab.shape[1]
    count = width // BLOCK
    rep = n_chan // count
    values = samples[...]
    turned = jnp.concatenate([values[:, width - HALF :], values, values[:, :HALF]], 1)
    for j in range(count + 1):
        window[j] = turned[:, BLOCK * j : BLOCK * (j + 1)].astype(jnp.bfloat16)
    pl.semaphore_wait(pltpu.get_barrier_semaphore(), n_chan * n_tm - 1)
    mine = pl.ds(pl.multiple_of(c * rows, rows), rows)
    place = ratio(c, rep)

    def remote(to):
        return pltpu.make_async_remote_copy(
            src_ref=window.at[pl.ds(ratio(to, rep), 2)],
            dst_ref=slab.at[:, mine, :],
            send_sem=sent,
            recv_sem=recv,
            device_id=(to, t),
            device_id_type=MESH,
        )

    def rim(to, shift):
        return pltpu.make_async_remote_copy(
            src_ref=window.at[0],
            dst_ref=edge.at[mine, :],
            send_sem=edge_sent,
            recv_sem=edge_recv,
            device_id=(to, wrap(t + shift, n_tm)),
            device_id_type=MESH,
        )

    each(1, n_chan, lambda k: remote(n_chan - k - jnp.where(c >= n_chan - k, 1, 0)).start())
    for r in range(rep):
        rim(r, 1).start()
        rim((count - 1) * rep + r, n_tm - 1).start()
    for j in range(2):
        slab[j, mine, :] = window[place + j]

    def bytes_of(ref, sem):
        return pltpu.make_async_copy(ref, ref, sem)

    others = channels - rows
    bytes_of(slab.at[:, pl.ds(0, others), :], recv).wait()

    @pl.when(jnp.logical_or(place == 0, place == count - 1))
    def _():
        bytes_of(edge, edge_recv).wait()

    left = lax.broadcasted_iota(jnp.int32, edge.shape, 1) < HALF

    @pl.when(place == 0)
    def _():
        slab[0] = jnp.where(left, edge[...], slab[0])

    @pl.when(place == count - 1)
    def _():
        slab[1] = jnp.where(left, slab[1], edge[...])

    def settle():
        bytes_of(slab.at[:, pl.ds(0, others), :], sent).wait()
        bytes_of(window.at[pl.ds(0, 2 * rep)], edge_sent).wait()

    return settle


def shrink(aa, ab, ba, bb, cut_one, cut_two):
    re1, im1, re2, im2 = aa - bb, ab + ba, aa + bb, ab - ba
    f1 = jnp.maximum(0.5 - cut_one * lax.rsqrt(re1 * re1 + im1 * im1), 0.0)
    f2 = jnp.maximum(0.5 - cut_two * lax.rsqrt(re2 * re2 + im2 * im2), 0.0)
    re1, im1, re2, im2 = re1 * f1, im1 * f1, re2 * f2, im2 * f2
    return re1 + re2, im1 + im2, im1 - im2, re2 - re1


def cut_of(cuts, level, orient):
    scale = math.sqrt(0.5) / 32.0
    return [cuts[level, 2 * orient + k].astype(jnp.float32) * scale for k in range(2)]


def cut_maps(cuts, level, shape):
    row_low = lax.broadcasted_iota(jnp.int32, shape, 0) < shape[0] // 2
    col_low = lax.broadcasted_iota(jnp.int32, shape, 1) < shape[1] // 2
    lh, hl, hh = (cut_of(cuts, level, o) for o in range(3))
    pick = [jnp.where(row_low, lh[k], jnp.where(col_low, hl[k], hh[k])) for k in range(2)]
    return pick[0], pick[1], jnp.logical_and(row_low, col_low)


def quarters(x):
    r, n = x.shape[0] // 2, x.shape[1] // 2
    return x[:r, :n], x[:r, n:], x[r:, :n], x[r:, n:]


def joined(parts):
    aa, ab, ba, bb = parts
    return jnp.concatenate(
        [jnp.concatenate([aa, ab], 1), jnp.concatenate([ba, bb], 1)], 0
    )


def synthesised(x, table):
    rows = x.shape[0]
    y = dot(jnp.concatenate(split(x), 0), table, False)
    return y[:rows, :BLOCK] + (y[:rows, BLOCK:] + y[rows:, :BLOCK])


def denoise(cuts, slab, chosen, tables, picked, cleaned):
    chan, chan_back, time, time_back = tables
    rows = slab.shape[1]
    length = time.shape[1]
    deep = time_back.shape[0]
    x = jnp.concatenate([slab[0], slab[1]], 1)
    y = dot(time[...], x, True)

    def timed(low, high):
        return y[low[0] : low[1]] + y[high[0] : high[1]]

    first_low = split(timed((0, length), (3 * length, 4 * length)))
    first_high = split(timed((length, 2 * length), (2 * length, 3 * length)))
    second = split(timed((4 * length, 5 * length), (5 * length, 6 * length)))
    third = split(timed((6 * length, 6 * length + length // 2), (6 * length + length // 2, 7 * length)))

    a = dot(chan[: 4 * rows, :], first_high[0], True)
    b = dot(chan[: 2 * rows, :], first_high[1], True)
    lh = joined(shrink(*quarters(a[:rows] + (a[3 * rows :] + b[:rows])), *cut_of(cuts, 0, 0)))
    hh = a[rows : 2 * rows] + (a[2 * rows : 3 * rows] + b[rows:])
    hh = joined(shrink(*quarters(hh), *cut_of(cuts, 0, 2)))
    a = dot(chan[rows : 3 * rows, :], first_low[0], True)
    b = dot(chan[rows : 2 * rows, :], first_low[1], True)
    hl = joined(shrink(*quarters(a[:rows] + (a[rows:] + b)), *cut_of(cuts, 0, 1)))

    a = dot(chan[4 * rows : 6 * rows, :], second[0], True)
    z = quarters(a[:rows] + (a[rows:] + dot(chan[4 * rows : 5 * rows, :], second[1], True)))
    one, two, kept = cut_maps(cuts, 1, z[0].shape)
    mid = joined([jnp.where(kept, 0.0, p) for p in shrink(*z, one, two)])

    a = dot(chan[6 * rows :, :], jnp.concatenate(third, 0), True)
    width = a.shape[1] // 2
    z = quarters(a[: rows // 2, :width] + (a[: rows // 2, width:] + a[rows // 2 :, :width]))
    one, two, kept = cut_maps(cuts, 2, z[0].shape)
    last = joined([jnp.where(kept, p, q) for p, q in zip(z, shrink(*z, one, two))])

    back = jnp.concatenate(
        [
            synthesised(lh, time_back[length : 2 * length, :]),
            synthesised(jnp.concatenate([hl, hh], 1), time_back[: 2 * length, :]),
            synthesised(mid, time_back[2 * length : 3 * length, :]),
            synthesised(last, time_back[3 * length : deep, :]),
        ],
        0,
    )
    y = dot(chan_back[...], jnp.concatenate(split(back), 1), False)
    whole = y[:rows, :BLOCK] + (y[:rows, BLOCK:] + y[rows:, :BLOCK])
    result = (0.25 * whole).astype(jnp.bfloat16)
    cleaned[...] = result.astype(jnp.float32).reshape(rows // 8, 8, BLOCK).astype(jnp.bfloat16)
    picked[...] = dot(chosen[...], result, False).astype(jnp.bfloat16)


def spread(picks, cleaned, receivers, sent, recv, crossed, sent_rows, landed):
    n_chan, n_tm = lax.axis_size("chan"), lax.axis_size("tm")
    c, t = lax.axis_index("chan"), lax.axis_index("tm")
    blocks = picks.shape[0]
    count = blocks // n_tm
    rep = n_chan // count
    pairs = n_tm // 2
    share = cleaned.shape[0] * 8 // (n_chan * n_tm)
    place = ratio(c, rep)
    copy_index = c - place * rep
    pair = t // 2
    core = t - 2 * pair
    other_core = t + 1 - 2 * core
    mine = t * count + place

    def move(block, sem, chan, tm):
        return pltpu.make_async_remote_copy(
            src_ref=picks.at[block],
            dst_ref=picks.at[block],
            send_sem=sent,
            recv_sem=sem,
            device_id=(chan, tm),
            device_id_type=MESH,
        )

    def chan_of(place):
        return place * rep + copy_index

    def block_at(k, u):
        tm = t if u == 0 else wrap(pair + pairs - u, pairs) * 2 + core
        return tm * count + (place if isinstance(k, int) and k == 0 else wrap(place + count - k, count))

    def rows_of(dc, dt):
        at = dc * n_tm + dt
        return at * (share // 8) if share % 8 == 0 else at * share // 8

    def personal(k):
        to = k + jnp.where(k >= place * n_tm + t, 1, 0)
        chan, to_tm = chan_of(to // n_tm), lax.rem(to, n_tm)
        return pltpu.make_async_remote_copy(
            src_ref=cleaned.at[rows_of(chan, to_tm)],
            dst_ref=receivers.at[mine],
            send_sem=sent_rows,
            recv_sem=landed,
            device_id=(chan, to_tm),
            device_id_type=MESH,
        )

    def relay(k, u):
        block = block_at(k, u)
        copy = move(block, crossed.at[min(u, 1)], c, other_core)
        if u or not isinstance(k, int) or k:
            move(block, recv.at[block], c, other_core).wait_recv()
        copy.start()

    def along_chan(k):
        to = k + jnp.where(k >= place, 1, 0)
        move(mine, recv.at[mine], chan_of(to), t).start()

    def bytes_of(ref, sem):
        return pltpu.make_async_copy(ref, ref, sem)

    each(0, count - 1, along_chan)
    local = pltpu.make_async_copy(cleaned.at[rows_of(c, t)], receivers.at[mine], landed)
    local.start()
    relay(0, 0)
    each(0, blocks - 1, lambda k: personal(k).start())
    for u in range(1, pairs):
        to = wrap(pair + u, pairs) * 2 + core
        each(0, count, lambda k, to=to: move(mine, recv.at[mine], chan_of(k), to).start())

    def near():
        each(1, count, lambda k: relay(k, 0))
        bytes_of(picks.at[pl.ds(0, count)], crossed.at[0]).wait()
        bytes_of(receivers, landed).wait()

    def far():
        for u in range(1, pairs):
            each(0, count, lambda k, u=u: relay(k, u))
        bytes_of(picks.at[pl.ds(0, (pairs - 1) * count)], crossed.at[1]).wait()

    def settle():
        bytes_of(picks.at[pl.ds(0, blocks - 1)], sent).wait()
        bytes_of(receivers.at[pl.ds(0, blocks - 1)], sent_rows).wait()

    return near, far, settle


def whole_kernel(n_tables, cuts, samples, sources, *refs):
    stored, refs = refs[:n_tables], refs[n_tables:]
    cross, picks, receivers, white, heard, partial = refs[:6]
    held, refs = refs[6 : 6 + n_tables], refs[6 + n_tables :]
    here, refs = refs[:4], refs[4:]
    slab, window, edge, chosen, cleaned, loads = refs[:6]
    gather_sems, spread_sems = refs[6:10], refs[10:]
    inputs = [
        pltpu.make_async_copy(a, b, here[3].at[i])
        for i, (a, b) in enumerate(zip((cuts, samples, sources), here))
    ]
    inputs[1].start()
    greet_all()
    inputs[0].start()
    inputs[2].start()
    copies = [pltpu.make_async_copy(a, b, loads.at[i]) for i, (a, b) in enumerate(zip(stored, held))]
    for copy in copies:
        copy.start()
    inputs[2].wait()
    cuts, samples, sources = here[:3]
    one_hot = jnp.where(
        lax.broadcasted_iota(jnp.int32, chosen.shape[::-1], 0) == sources[...], 1.0, 0.0
    )
    chosen[...] = jnp.transpose(one_hot).astype(jnp.bfloat16)
    inputs[1].wait()
    gathered = gather(samples, slab, window, edge, *gather_sems)
    inputs[0].wait()
    for copy in copies[:-1]:
        copy.wait()
    time, time_back, chan_back = held[:3]
    chan = held[3] if n_tables == 5 else time
    n_tm = lax.axis_size("tm")
    count = picks.shape[0] // n_tm
    rep = lax.axis_size("chan") // count
    mine = lax.axis_index("tm") * count + ratio(lax.axis_index("chan"), rep)
    denoise(cuts, slab, chosen, (chan, chan_back, time, time_back), picks.at[mine], cleaned)
    near, far, settle = spread(picks, cleaned, receivers, *spread_sems)
    copies[-1].wait()
    t = lax.axis_index("tm")
    pair = t // 2
    pairs = n_tm // 2
    near()
    own = [2 * pair, 2 * pair + 1]
    correlate(picks, receivers, held[-1], white, heard, partial, cross, own, True, pairs == 1)
    if pairs > 1:
        far()
        rest = [2 * wrap(pair + u, pairs) + side for u in range(1, pairs) for side in range(2)]
        correlate(picks, receivers, held[-1], white, heard, partial, cross, rest, False, True)
    gathered()
    settle()


def correlate(picks, receivers, table, white, heard, partial, cross, parts, first, final):
    per_window = N // BLOCK
    sources = picks.shape[1]
    count = picks.shape[0] // lax.axis_size("tm")
    starts = [tm * count + i for tm in parts for i in range(0, count, per_window)]
    windows = len(starts)

    def window(ref, start):
        return jnp.concatenate([ref[start + j] for j in range(per_window)], 1)

    rows = [window(receivers, start).astype(jnp.float32) for start in starts]
    block = jnp.concatenate(
        [window(picks, start) for start in starts]
        + [jnp.concatenate(rows, 0).astype(jnp.bfloat16)],
        0,
    )
    spectra = dot(block, table[...], False)
    scale = lax.rsqrt(jnp.mean(spectra * spectra, axis=1, keepdims=True) + 1e-05)
    spectra = (spectra * scale).astype(jnp.bfloat16).astype(jnp.float32)
    base = windows * sources
    chunks = BINS // BLOCK
    weight = jnp.where(lax.broadcasted_iota(jnp.int32, (1, BLOCK), 1) == 0, 1.0, 2.0)
    for part in range(chunks):
        real = spectra[:, BLOCK * part : BLOCK * (part + 1)]
        imag = spectra[:, BINS + BLOCK * part : BINS + BLOCK * (part + 1)]
        white[part, :base, :] = real[:base]
        white[chunks + part, :base, :] = imag[:base]
        white[2 * chunks + part, :base, :] = real[:base] + imag[:base]
        real, imag = (x[base:] * (2.0 if part else weight) for x in (real, imag))
        heard[part, : 8 * windows, :] = real
        heard[chunks + part, : 8 * windows, :] = real + imag
        heard[2 * chunks + part, : 8 * windows, :] = real - imag

    group = math.gcd(16, sources)
    for part in range(chunks):
        around = [
            [heard[kind * chunks + part, 8 * w : 8 * w + 8, :] for kind in range(3)]
            for w in range(windows)
        ]
        columns = [slice(x, x + BLOCK) for x in (part * BLOCK, BINS + part * BLOCK)]

        def body(g, carry, part=part, around=around, columns=columns):
            found = [[], []]
            for j in range(group):
                sums = [None] * 3
                for w in range(windows):
                    spot = pl.ds(w * sources + group * g + j, 8, stride=0)
                    for n, (kind, near) in enumerate(zip((2, 0, 1), around[w])):
                        term = white.at[kind * chunks + part][spot, :] * near
                        sums[n] = term if sums[n] is None else sums[n] + term
                found[0].append(sums[0] - sums[2])
                found[1].append(sums[0] - sums[1])
            spot = pl.ds(pl.multiple_of(8 * group * g, 8 * group), 8 * group)
            for at, values in zip(columns, found):
                value = jnp.concatenate(values, 0)
                if not first:
                    value = value + partial[spot, at]
                if final:
                    cross[spot, at] = value.astype(jnp.bfloat16)
                else:
                    partial[spot, at] = value
            return carry

        lax.fori_loop(0, sources // group, body, 0)


def lag_kernel(scale, cross, lags, out):
    out[...] = dot(cross[...], lags[...], False) * scale


def local(samples, thresholds, sources):
    n_chan, n_tm = lax.axis_size("chan"), lax.axis_size("tm")
    rows, width = samples.shape
    channels = rows * n_chan
    count = width // BLOCK
    rep = n_chan // count
    blocks = count * n_tm
    windows = n_tm * width // N
    picked_count = sources.shape[0]
    most = max(2, n_tm - 2) * (width // N)
    vmem = pl.BlockSpec(memory_space=pltpu.VMEM)
    hbm = pl.BlockSpec(memory_space=pltpu.HBM)
    dma = pltpu.SemaphoreType.DMA
    f32, bf16 = jnp.float32, jnp.bfloat16
    big = (40 if channels == 2 * BLOCK else 55) * 1024 * 1024

    time = stacked(levels_of(2 * BLOCK))
    back = halves(levels_of(2 * BLOCK)[:, HALF : HALF + BLOCK])
    chan = levels_of(channels)
    chan_back = two_halves(np.ascontiguousarray(chan.T))
    tables = [time, np.concatenate([back[0], back[1]], 1), chan_back]
    if channels != 2 * BLOCK:
        tables.append(stacked(chan))
    tables.append(dft_table())

    cross = pl.pallas_call(
        functools.partial(whole_kernel, len(tables)),
        out_shape=pltpu.VMEM((picked_count * 8, N), bf16),
        in_specs=[hbm] * (3 + len(tables)),
        out_specs=vmem,
        scratch_shapes=[
            pltpu.VMEM((blocks, picked_count, BLOCK), bf16),
            pltpu.VMEM((blocks, 8, BLOCK), bf16),
            pltpu.VMEM((3 * BINS // BLOCK, most * picked_count, BLOCK), f32),
            pltpu.VMEM((3 * BINS // BLOCK, most * 8, BLOCK), f32),
            pltpu.VMEM((picked_count * 8, N), f32),
        ]
        + [pltpu.VMEM(a.shape, bf16) for a in tables]
        + [
            pltpu.SMEM(thresholds.shape, jnp.int32),
            pltpu.VMEM(samples.shape, f32),
            pltpu.VMEM((1, picked_count), jnp.int32),
            dma((3,)),
        ]
        + [
            pltpu.VMEM((2, channels, BLOCK), bf16),
            pltpu.VMEM((count + 1, rows, BLOCK), bf16),
            pltpu.VMEM((channels, BLOCK), bf16),
            pltpu.VMEM((picked_count, channels), bf16),
            pltpu.VMEM((channels // 8, 8, BLOCK), bf16),
            dma((len(tables),)),
            dma,
            dma,
            dma,
            dma,
            dma,
            dma((blocks,)),
            dma((2,)),
            dma,
            dma,
        ],
        compiler_params=pltpu.CompilerParams(
            collective_id=0, has_side_effects=True, vmem_limit_bytes=big
        ),
        name="whole",
    )(*[
        pltpu.with_memory_space_constraint(a, pltpu.HBM)
        for a in (thresholds, samples, sources[None, :], *[jnp.asarray(a) for a in tables])
    ])

    half = LAGS // 2
    dft = tables[-1]
    lags = np.ascontiguousarray(np.concatenate([dft[N - half :], dft[:half]], 0).T)
    out = pl.pallas_call(
        functools.partial(lag_kernel, 1.0 / math.sqrt(windows * N)),
        out_shape=jax.ShapeDtypeStruct((picked_count * 8, LAGS), f32),
        in_specs=[vmem, vmem],
        out_specs=vmem,
        compiler_params=pltpu.CompilerParams(vmem_limit_bytes=16 * 1024 * 1024),
        name="lags",
    )(cross, jnp.asarray(lags))

    out = out.reshape(picked_count, 8, LAGS)
    share = channels // (n_chan * n_tm)
    if share < 8:
        place = lax.axis_index("chan") * n_tm + lax.axis_index("tm")
        out = lax.dynamic_slice_in_dim(out, lax.rem(place * share, 8), share, 1)
    return out


def solution(mesh):
    return jax.shard_map(
        local,
        mesh=mesh,
        in_specs=(P("chan", "tm"), P(), P()),
        out_specs=P(None, ("chan", "tm"), None),
        check_vma=False,
    )
```

```python
import functools
import math

import jax
import jax.numpy as jnp
import numpy as np
from jax import lax
from jax.experimental import pallas as pl
from jax.experimental.pallas import tpu as pltpu
from jax.sharding import PartitionSpec as P

N = 1024
LEVELS = 3
BINS = 512
LAGS = 512
BLOCK = 128
HALF = 64
MESH = pl.DeviceIdType.MESH

daubechies = [
    0.2303778133088964,
    0.7148465705529155,
    0.6308807679298587,
    -0.0279837694168599,
    -0.1870348117190931,
    0.0308413818355607,
    0.0328830116668852,
    -0.010597401785069,
]


def filter_bank():
    lowpass = list(daubechies)
    highpass = [(1.0 if k % 2 == 0 else -1.0) * daubechies[7 - k] for k in range(8)]
    return [(lowpass, highpass), (lowpass[::-1], highpass[::-1])]


def bank_matrix(length):
    half = length // 2
    out = np.zeros((2, 2, half, length))
    rows = np.arange(half)
    for tree, pair in enumerate(filter_bank()):
        for band, taps in enumerate(pair):
            for k in range(8):
                np.add.at(out[tree, band], (rows, (2 * rows + k - 3) % length), taps[k])
    return out


def levels_of(length):
    first, second, third = (bank_matrix(length >> level) for level in range(3))
    parts = [first[0, 0], first[1, 0], first[0, 1], first[1, 1]]
    for tree in range(2):
        parts += [second[tree, band] @ first[tree, 0] for band in range(2)]
    for tree in range(2):
        low = second[tree, 0] @ first[tree, 0]
        parts += [third[tree, band] @ low for band in range(2)]
    return np.concatenate(parts, 0)


def halves(matrix):
    m32 = np.asarray(matrix, np.float32)
    hi = m32.astype(jnp.bfloat16)
    lo = (m32 - hi.astype(np.float32)).astype(jnp.bfloat16)
    return np.stack([hi, lo])


def two_halves(matrix):
    return np.concatenate(list(halves(matrix)), 0)


def stacked(matrix):
    hi, lo = halves(matrix)
    n = matrix.shape[1]
    parts = [hi[: 2 * n], lo[n : 2 * n], lo[:n]]
    parts += [x[at] for at in (slice(2 * n, 3 * n), slice(3 * n, None)) for x in (hi, lo)]
    return np.concatenate(parts, 0)


def dft_table():
    t = np.arange(N)
    f = np.arange(BINS)
    phases = ((t[:, None] * f[None, :]) % N).astype(np.float64) * (2.0 * math.pi / N)
    table = np.concatenate([np.cos(phases), -np.sin(phases)], 1)
    return table.astype(np.float32).astype(jnp.bfloat16)


def split(x):
    hi = x.astype(jnp.bfloat16)
    lo = (x - hi.astype(jnp.float32)).astype(jnp.bfloat16)
    return hi, lo


def dot(a, b, trans_b):
    dims = (((1,), (1 if trans_b else 0,)), ((), ()))
    return lax.dot_general(a, b, dims, preferred_element_type=jnp.float32)


def wrap(x, n):
    return jnp.where(x >= n, x - n, x)


def ratio(x, n):
    return x if n == 1 else x // n


def each(low, high, act):
    def body(k, carry):
        act(k)
        return carry

    if high - low <= 1:
        for k in range(low, high):
            act(k)
    else:
        lax.fori_loop(low, high, body, 0)


def greet_all():
    n_chan, n_tm = lax.axis_size("chan"), lax.axis_size("tm")
    c, t = lax.axis_index("chan"), lax.axis_index("tm")
    barrier = pltpu.get_barrier_semaphore()
    for j in range(n_tm):
        to = wrap(t + j, n_tm)

        def greet(k, to=to):
            pl.semaphore_signal(
                barrier, inc=1, device_id=(wrap(c + k, n_chan), to), device_id_type=MESH
            )

        each(0 if j else 1, n_chan, greet)


def gather(samples, slab, window, edge, sent, recv, edge_sent, edge_recv):
    n_chan, n_tm = lax.axis_size("chan"), lax.axis_size("tm")
    c, t = lax.axis_index("chan"), lax.axis_index("tm")
    rows, width = samples.shape
    channels = slab.shape[1]
    count = width // BLOCK
    rep = n_chan // count
    values = samples[...]
    turned = jnp.concatenate([values[:, width - HALF :], values, values[:, :HALF]], 1)
    for j in range(count + 1):
        window[j] = turned[:, BLOCK * j : BLOCK * (j + 1)].astype(jnp.bfloat16)
    pl.semaphore_wait(pltpu.get_barrier_semaphore(), n_chan * n_tm - 1)
    mine = pl.ds(pl.multiple_of(c * rows, rows), rows)
    place = ratio(c, rep)

    def remote(to):
        return pltpu.make_async_remote_copy(
            src_ref=window.at[pl.ds(ratio(to, rep), 2)],
            dst_ref=slab.at[:, mine, :],
            send_sem=sent,
            recv_sem=recv,
            device_id=(to, t),
            device_id_type=MESH,
        )

    def rim(to, shift):
        return pltpu.make_async_remote_copy(
            src_ref=window.at[0],
            dst_ref=edge.at[mine, :],
            send_sem=edge_sent,
            recv_sem=edge_recv,
            device_id=(to, wrap(t + shift, n_tm)),
            device_id_type=MESH,
        )

    each(1, n_chan, lambda k: remote(n_chan - k - jnp.where(c >= n_chan - k, 1, 0)).start())
    for r in range(rep):
        rim(r, 1).start()
        rim((count - 1) * rep + r, n_tm - 1).start()
    for j in range(2):
        slab[j, mine, :] = window[place + j]

    def bytes_of(ref, sem):
        return pltpu.make_async_copy(ref, ref, sem)

    others = channels - rows
    bytes_of(slab.at[:, pl.ds(0, others), :], recv).wait()

    @pl.when(jnp.logical_or(place == 0, place == count - 1))
    def _():
        bytes_of(edge, edge_recv).wait()

    left = lax.broadcasted_iota(jnp.int32, edge.shape, 1) < HALF

    @pl.when(place == 0)
    def _():
        slab[0] = jnp.where(left, edge[...], slab[0])

    @pl.when(place == count - 1)
    def _():
        slab[1] = jnp.where(left, slab[1], edge[...])

    def settle():
        bytes_of(slab.at[:, pl.ds(0, others), :], sent).wait()
        bytes_of(window.at[pl.ds(0, 2 * rep)], edge_sent).wait()

    return settle


def shrink(aa, ab, ba, bb, cut_one, cut_two):
    re1, im1, re2, im2 = aa - bb, ab + ba, aa + bb, ab - ba
    f1 = jnp.maximum(0.5 - cut_one * lax.rsqrt(re1 * re1 + im1 * im1), 0.0)
    f2 = jnp.maximum(0.5 - cut_two * lax.rsqrt(re2 * re2 + im2 * im2), 0.0)
    re1, im1, re2, im2 = re1 * f1, im1 * f1, re2 * f2, im2 * f2
    return re1 + re2, im1 + im2, im1 - im2, re2 - re1


def cut_of(cuts, level, orient):
    scale = math.sqrt(0.5) / 32.0
    return [cuts[level, 2 * orient + k].astype(jnp.float32) * scale for k in range(2)]


def cut_maps(cuts, level, shape):
    row_low = lax.broadcasted_iota(jnp.int32, shape, 0) < shape[0] // 2
    col_low = lax.broadcasted_iota(jnp.int32, shape, 1) < shape[1] // 2
    lh, hl, hh = (cut_of(cuts, level, o) for o in range(3))
    pick = [jnp.where(row_low, lh[k], jnp.where(col_low, hl[k], hh[k])) for k in range(2)]
    return pick[0], pick[1], jnp.logical_and(row_low, col_low)


def quarters(x):
    r, n = x.shape[0] // 2, x.shape[1] // 2
    return x[:r, :n], x[:r, n:], x[r:, :n], x[r:, n:]


def joined(parts):
    aa, ab, ba, bb = parts
    return jnp.concatenate(
        [jnp.concatenate([aa, ab], 1), jnp.concatenate([ba, bb], 1)], 0
    )


def synthesised(x, table):
    rows = x.shape[0]
    y = dot(jnp.concatenate(split(x), 0), table, False)
    return y[:rows, :BLOCK] + (y[:rows, BLOCK:] + y[rows:, :BLOCK])


def denoise(cuts, slab, chosen, tables, picked, cleaned):
    chan, chan_back, time, time_back = tables
    rows = slab.shape[1]
    length = time.shape[1]
    deep = time_back.shape[0]
    x = jnp.concatenate([slab[0], slab[1]], 1)
    y = dot(time[...], x, True)

    def timed(low, high):
        return y[low[0] : low[1]] + y[high[0] : high[1]]

    first_low = split(timed((0, length), (3 * length, 4 * length)))
    first_high = split(timed((length, 2 * length), (2 * length, 3 * length)))
    second = split(timed((4 * length, 5 * length), (5 * length, 6 * length)))
    third = split(timed((6 * length, 6 * length + length // 2), (6 * length + length // 2, 7 * length)))

    a = dot(chan[: 4 * rows, :], first_high[0], True)
    b = dot(chan[: 2 * rows, :], first_high[1], True)
    lh = joined(shrink(*quarters(a[:rows] + (a[3 * rows :] + b[:rows])), *cut_of(cuts, 0, 0)))
    hh = a[rows : 2 * rows] + (a[2 * rows : 3 * rows] + b[rows:])
    hh = joined(shrink(*quarters(hh), *cut_of(cuts, 0, 2)))
    a = dot(chan[rows : 3 * rows, :], first_low[0], True)
    b = dot(chan[rows : 2 * rows, :], first_low[1], True)
    hl = joined(shrink(*quarters(a[:rows] + (a[rows:] + b)), *cut_of(cuts, 0, 1)))

    a = dot(chan[4 * rows : 6 * rows, :], second[0], True)
    z = quarters(a[:rows] + (a[rows:] + dot(chan[4 * rows : 5 * rows, :], second[1], True)))
    one, two, kept = cut_maps(cuts, 1, z[0].shape)
    mid = joined([jnp.where(kept, 0.0, p) for p in shrink(*z, one, two)])

    a = dot(chan[6 * rows :, :], jnp.concatenate(third, 0), True)
    width = a.shape[1] // 2
    z = quarters(a[: rows // 2, :width] + (a[: rows // 2, width:] + a[rows // 2 :, :width]))
    one, two, kept = cut_maps(cuts, 2, z[0].shape)
    last = joined([jnp.where(kept, p, q) for p, q in zip(z, shrink(*z, one, two))])

    back = jnp.concatenate(
        [
            synthesised(lh, time_back[length : 2 * length, :]),
            synthesised(jnp.concatenate([hl, hh], 1), time_back[: 2 * length, :]),
            synthesised(mid, time_back[2 * length : 3 * length, :]),
            synthesised(last, time_back[3 * length : deep, :]),
        ],
        0,
    )
    y = dot(chan_back[...], jnp.concatenate(split(back), 1), False)
    whole = y[:rows, :BLOCK] + (y[:rows, BLOCK:] + y[rows:, :BLOCK])
    result = (0.25 * whole).astype(jnp.bfloat16)
    cleaned[...] = result.astype(jnp.float32).reshape(rows // 8, 8, BLOCK).astype(jnp.bfloat16)
    picked[...] = dot(chosen[...], result, False).astype(jnp.bfloat16)


def spread(picks, cleaned, receivers, sent, recv, crossed, sent_rows, landed):
    n_chan, n_tm = lax.axis_size("chan"), lax.axis_size("tm")
    c, t = lax.axis_index("chan"), lax.axis_index("tm")
    blocks = picks.shape[0]
    count = blocks // n_tm
    rep = n_chan // count
    pairs = n_tm // 2
    share = cleaned.shape[0] * 8 // (n_chan * n_tm)
    place = ratio(c, rep)
    copy_index = c - place * rep
    pair = t // 2
    core = t - 2 * pair
    other_core = t + 1 - 2 * core
    mine = t * count + place

    def move(block, sem, chan, tm):
        return pltpu.make_async_remote_copy(
            src_ref=picks.at[block],
            dst_ref=picks.at[block],
            send_sem=sent,
            recv_sem=sem,
            device_id=(chan, tm),
            device_id_type=MESH,
        )

    def chan_of(place):
        return place * rep + copy_index

    def block_at(k, u):
        tm = t if u == 0 else wrap(pair + pairs - u, pairs) * 2 + core
        return tm * count + (place if isinstance(k, int) and k == 0 else wrap(place + count - k, count))

    def rows_of(dc, dt):
        at = dc * n_tm + dt
        return at * (share // 8) if share % 8 == 0 else at * share // 8

    def personal(k):
        to = k + jnp.where(k >= place * n_tm + t, 1, 0)
        chan, to_tm = chan_of(to // n_tm), lax.rem(to, n_tm)
        return pltpu.make_async_remote_copy(
            src_ref=cleaned.at[rows_of(chan, to_tm)],
            dst_ref=receivers.at[mine],
            send_sem=sent_rows,
            recv_sem=landed,
            device_id=(chan, to_tm),
            device_id_type=MESH,
        )

    def relay(k, u):
        block = block_at(k, u)
        copy = move(block, crossed.at[min(u, 1)], c, other_core)
        if u or not isinstance(k, int) or k:
            move(block, recv.at[block], c, other_core).wait_recv()
        copy.start()

    def along_chan(k):
        to = k + jnp.where(k >= place, 1, 0)
        move(mine, recv.at[mine], chan_of(to), t).start()

    def bytes_of(ref, sem):
        return pltpu.make_async_copy(ref, ref, sem)

    each(0, count - 1, along_chan)
    local = pltpu.make_async_copy(cleaned.at[rows_of(c, t)], receivers.at[mine], landed)
    local.start()
    relay(0, 0)
    each(0, blocks - 1, lambda k: personal(k).start())
    for u in range(1, pairs):
        to = wrap(pair + u, pairs) * 2 + core
        each(0, count, lambda k, to=to: move(mine, recv.at[mine], chan_of(k), to).start())

    def near():
        each(1, count, lambda k: relay(k, 0))
        bytes_of(picks.at[pl.ds(0, count)], crossed.at[0]).wait()
        bytes_of(receivers, landed).wait()

    def far():
        for u in range(1, pairs):
            each(0, count, lambda k, u=u: relay(k, u))
        bytes_of(picks.at[pl.ds(0, (pairs - 1) * count)], crossed.at[1]).wait()

    def settle():
        bytes_of(picks.at[pl.ds(0, blocks - 1)], sent).wait()
        bytes_of(receivers.at[pl.ds(0, blocks - 1)], sent_rows).wait()

    return near, far, settle


def whole_kernel(n_tables, cuts, samples, sources, *refs):
    stored, refs = refs[:n_tables], refs[n_tables:]
    white, heard, partial, picks, receivers, white_own, heard_own = refs[:7]
    held, refs = refs[7 : 7 + n_tables], refs[7 + n_tables :]
    here, refs = refs[:4], refs[4:]
    slab, window, edge, chosen, cleaned, loads = refs[:6]
    gather_sems, spread_sems = refs[6:10], refs[10:]
    inputs = [
        pltpu.make_async_copy(a, b, here[3].at[i])
        for i, (a, b) in enumerate(zip((cuts, samples, sources), here))
    ]
    inputs[1].start()
    greet_all()
    inputs[0].start()
    inputs[2].start()
    copies = [pltpu.make_async_copy(a, b, loads.at[i]) for i, (a, b) in enumerate(zip(stored, held))]
    for copy in copies:
        copy.start()
    inputs[2].wait()
    cuts, samples, sources = here[:3]
    one_hot = jnp.where(
        lax.broadcasted_iota(jnp.int32, chosen.shape[::-1], 0) == sources[...], 1.0, 0.0
    )
    chosen[...] = jnp.transpose(one_hot).astype(jnp.bfloat16)
    inputs[1].wait()
    gathered = gather(samples, slab, window, edge, *gather_sems)
    inputs[0].wait()
    for copy in copies[:-1]:
        copy.wait()
    time, time_back, chan_back = held[:3]
    chan = held[3] if n_tables == 5 else time
    n_tm = lax.axis_size("tm")
    count = picks.shape[0] // n_tm
    rep = lax.axis_size("chan") // count
    mine = lax.axis_index("tm") * count + ratio(lax.axis_index("chan"), rep)
    denoise(cuts, slab, chosen, (chan, chan_back, time, time_back), picks.at[mine], cleaned)
    near, far, settle = spread(picks, cleaned, receivers, *spread_sems)
    copies[-1].wait()
    t = lax.axis_index("tm")
    pair = t // 2
    pairs = n_tm // 2
    near()
    own = [2 * pair, 2 * pair + 1]
    whiten(picks, receivers, held[-1], white_own, heard_own, own)
    windows, sources = heard_own.shape[1] // 8, picks.shape[1]
    partial_products(white_own, heard_own, partial, windows, sources)
    far()
    rest = [2 * wrap(pair + u, pairs) + side for u in range(1, pairs) for side in range(2)]
    whiten(picks, receivers, held[-1], white, heard, rest)
    gathered()
    settle()


def whiten(picks, receivers, table, white, heard, parts):
    per_window = N // BLOCK
    sources = picks.shape[1]
    count = picks.shape[0] // lax.axis_size("tm")
    starts = [tm * count + i for tm in parts for i in range(0, count, per_window)]
    windows = len(starts)

    def window(ref, start):
        return jnp.concatenate([ref[start + j] for j in range(per_window)], 1)

    rows = [window(receivers, start).astype(jnp.float32) for start in starts]
    block = jnp.concatenate(
        [window(picks, start) for start in starts]
        + [jnp.concatenate(rows, 0).astype(jnp.bfloat16)],
        0,
    )
    spectra = dot(block, table[...], False)
    scale = lax.rsqrt(jnp.mean(spectra * spectra, axis=1, keepdims=True) + 1e-05)
    spectra = (spectra * scale).astype(jnp.bfloat16).astype(jnp.float32)
    base = windows * sources
    chunks = BINS // BLOCK
    weight = jnp.where(lax.broadcasted_iota(jnp.int32, (1, BLOCK), 1) == 0, 1.0, 2.0)
    for part in range(chunks):
        real = spectra[:, BLOCK * part : BLOCK * (part + 1)]
        imag = spectra[:, BINS + BLOCK * part : BINS + BLOCK * (part + 1)]
        white[part, :base, :] = real[:base]
        white[chunks + part, :base, :] = imag[:base]
        white[2 * chunks + part, :base, :] = real[:base] + imag[:base]
        real, imag = (x[base:] * (2.0 if part else weight) for x in (real, imag))
        heard[part, : 8 * windows, :] = real
        heard[chunks + part, : 8 * windows, :] = real + imag
        heard[2 * chunks + part, : 8 * windows, :] = real - imag


def products(white, heard, windows, sources, columns, first, count, finish):
    chunks = BINS // BLOCK
    near = [
        [heard[kind * chunks + columns, 8 * w : 8 * w + 8, :] for kind in range(3)]
        for w in range(windows)
    ]
    found = [[], []]
    for j in range(count):
        sums = [None] * 3
        for w in range(windows):
            spot = pl.ds(w * sources + first + j, 8, stride=0)
            for n, kind in enumerate((2, 0, 1)):
                term = white.at[kind * chunks + columns][spot, :] * near[w][n]
                sums[n] = term if sums[n] is None else sums[n] + term
        found[0].append(sums[0] - sums[2])
        found[1].append(sums[0] - sums[1])
    for at, values in zip((columns * BLOCK, BINS + columns * BLOCK), found):
        finish(slice(at, at + BLOCK), jnp.concatenate(values, 0))


def partial_products(white, heard, partial, windows, sources):
    group = math.gcd(32, sources)
    for part in range(BINS // BLOCK):

        def body(g, carry, part=part):
            spot = pl.ds(pl.multiple_of(8 * group * g, 8 * group), 8 * group)

            def finish(at, value):
                partial[spot, at] = value

            products(white, heard, windows, sources, part, group * g, group, finish)
            return carry

        lax.fori_loop(0, sources // group, body, 0)


def lag_kernel(sources, white, heard, partial, lags, out, cross, held, sems):
    parts, rows = held.shape[:2]
    windows = white.shape[1] // sources
    each_part = rows // 8
    group = math.gcd(each_part if windows <= 2 else 16, each_part)
    copies = []
    for i in range(parts):
        for part in range(BINS // BLOCK):

            def body(g, carry, i=i, part=part):
                start = 8 * (i * each_part + group * g)
                if not isinstance(start, int):
                    start = pl.multiple_of(start, 8 * group)
                spot = pl.ds(start, 8 * group)

                def finish(at, value):
                    cross[spot, at] = (value + partial[spot, at]).astype(jnp.bfloat16)

                first = i * each_part + group * g
                products(white, heard, windows, sources, part, first, group, finish)
                return carry

            if group == each_part:
                body(0, 0)
            else:
                lax.fori_loop(0, each_part // group, body, 0)
        part = slice(i * rows, (i + 1) * rows)
        held[i] = dot(cross[part, :], lags[...], False)
        copies.append(pltpu.make_async_copy(held.at[i], out.at[part, :], sems.at[i]))
        copies[i].start()
    for copy in copies:
        copy.wait()


def local(samples, thresholds, sources):
    n_chan, n_tm = lax.axis_size("chan"), lax.axis_size("tm")
    rows, width = samples.shape
    channels = rows * n_chan
    count = width // BLOCK
    rep = n_chan // count
    blocks = count * n_tm
    windows = n_tm * width // N
    picked_count = sources.shape[0]
    vmem = pl.BlockSpec(memory_space=pltpu.VMEM)
    hbm = pl.BlockSpec(memory_space=pltpu.HBM)
    dma = pltpu.SemaphoreType.DMA
    f32, bf16 = jnp.float32, jnp.bfloat16
    big = (40 if channels == 2 * BLOCK else 47) * 1024 * 1024

    time = stacked(levels_of(2 * BLOCK))
    back = halves(levels_of(2 * BLOCK)[:, HALF : HALF + BLOCK])
    chan = levels_of(channels)
    chan_back = two_halves(np.ascontiguousarray(chan.T))
    tables = [time, np.concatenate([back[0], back[1]], 1), chan_back]
    if channels != 2 * BLOCK:
        tables.append(stacked(chan))
    tables.append(dft_table())

    chunks = BINS // BLOCK
    each_tm = width // N
    most = (n_tm - 2) * each_tm
    spectra = pl.pallas_call(
        functools.partial(whole_kernel, len(tables)),
        out_shape=(
            pltpu.VMEM((3 * chunks, most * picked_count, BLOCK), f32),
            pltpu.VMEM((3 * chunks, most * 8, BLOCK), f32),
            pltpu.VMEM((picked_count * 8, N), f32),
        ),
        in_specs=[hbm] * (3 + len(tables)),
        out_specs=(vmem, vmem, vmem),
        scratch_shapes=[
            pltpu.VMEM((blocks, picked_count, BLOCK), bf16),
            pltpu.VMEM((blocks, 8, BLOCK), bf16),
            pltpu.VMEM((3 * chunks, 2 * each_tm * picked_count, BLOCK), f32),
            pltpu.VMEM((3 * chunks, 2 * each_tm * 8, BLOCK), f32),
        ]
        + [pltpu.VMEM(a.shape, bf16) for a in tables]
        + [
            pltpu.SMEM(thresholds.shape, jnp.int32),
            pltpu.VMEM(samples.shape, f32),
            pltpu.VMEM((1, picked_count), jnp.int32),
            dma((3,)),
        ]
        + [
            pltpu.VMEM((2, channels, BLOCK), bf16),
            pltpu.VMEM((count + 1, rows, BLOCK), bf16),
            pltpu.VMEM((channels, BLOCK), bf16),
            pltpu.VMEM((picked_count, channels), bf16),
            pltpu.VMEM((channels // 8, 8, BLOCK), bf16),
            dma((len(tables),)),
            dma,
            dma,
            dma,
            dma,
            dma,
            dma((blocks,)),
            dma((2,)),
            dma,
            dma,
        ],
        compiler_params=pltpu.CompilerParams(
            collective_id=0, has_side_effects=True, vmem_limit_bytes=big
        ),
        name="whole",
    )(*[
        pltpu.with_memory_space_constraint(a, pltpu.HBM)
        for a in (thresholds, samples, sources[None, :], *[jnp.asarray(a) for a in tables])
    ])

    half = LAGS // 2
    dft = tables[-1]
    lags = np.concatenate([dft[N - half :], dft[:half]], 0).T.astype(np.float32)
    lags = (lags / math.sqrt(windows * N)).astype(jnp.bfloat16)
    out = pl.pallas_call(
        functools.partial(lag_kernel, picked_count),
        out_shape=jax.ShapeDtypeStruct((picked_count * 8, LAGS), f32),
        in_specs=[vmem] * 4,
        out_specs=pl.BlockSpec(memory_space=pl.ANY),
        scratch_shapes=[
            pltpu.VMEM((picked_count * 8, N), bf16),
            pltpu.VMEM((2, picked_count * 4, LAGS), f32),
            dma((2,)),
        ],
        compiler_params=pltpu.CompilerParams(vmem_limit_bytes=16 * 1024 * 1024),
        name="lags",
    )(*spectra, jnp.asarray(lags))

    out = out.reshape(picked_count, 8, LAGS)
    share = channels // (n_chan * n_tm)
    if share < 8:
        place = lax.axis_index("chan") * n_tm + lax.axis_index("tm")
        out = lax.dynamic_slice_in_dim(out, lax.rem(place * share, 8), share, 1)
    return out


def solution(mesh):
    return jax.shard_map(
        local,
        mesh=mesh,
        in_specs=(P("chan", "tm"), P(), P()),
        out_specs=P(None, ("chan", "tm"), None),
        check_vma=False,
    )
```

```python
import functools
import math

import jax
import jax.numpy as jnp
import numpy as np
from jax import lax
from jax.experimental import pallas as pl
from jax.experimental.pallas import tpu as pltpu
from jax.sharding import PartitionSpec as P

N = 1024
LEVELS = 3
BINS = 512
LAGS = 512
BLOCK = 128
HALF = 64
MESH = pl.DeviceIdType.MESH

daubechies = [
    0.2303778133088964,
    0.7148465705529155,
    0.6308807679298587,
    -0.0279837694168599,
    -0.1870348117190931,
    0.0308413818355607,
    0.0328830116668852,
    -0.010597401785069,
]


def filter_bank():
    lowpass = list(daubechies)
    highpass = [(1.0 if k % 2 == 0 else -1.0) * daubechies[7 - k] for k in range(8)]
    return [(lowpass, highpass), (lowpass[::-1], highpass[::-1])]


def bank_matrix(length):
    half = length // 2
    out = np.zeros((2, 2, half, length))
    rows = np.arange(half)
    for tree, pair in enumerate(filter_bank()):
        for band, taps in enumerate(pair):
            for k in range(8):
                np.add.at(out[tree, band], (rows, (2 * rows + k - 3) % length), taps[k])
    return out


def levels_of(length):
    first, second, third = (bank_matrix(length >> level) for level in range(3))
    parts = [first[0, 0], first[1, 0], first[0, 1], first[1, 1]]
    for tree in range(2):
        parts += [second[tree, band] @ first[tree, 0] for band in range(2)]
    for tree in range(2):
        low = second[tree, 0] @ first[tree, 0]
        parts += [third[tree, band] @ low for band in range(2)]
    return np.concatenate(parts, 0)


def halves(matrix):
    m32 = np.asarray(matrix, np.float32)
    hi = m32.astype(jnp.bfloat16)
    lo = (m32 - hi.astype(np.float32)).astype(jnp.bfloat16)
    return np.stack([hi, lo])


def two_halves(matrix):
    return np.concatenate(list(halves(matrix)), 0)


def stacked(matrix):
    hi, lo = halves(matrix)
    n = matrix.shape[1]
    parts = [hi[: 2 * n], lo[n : 2 * n], lo[:n]]
    parts += [x[at] for at in (slice(2 * n, 3 * n), slice(3 * n, None)) for x in (hi, lo)]
    return np.concatenate(parts, 0)


def dft_table():
    t = np.arange(N)
    f = np.arange(BINS)
    phases = ((t[:, None] * f[None, :]) % N).astype(np.float64) * (2.0 * math.pi / N)
    table = np.concatenate([np.cos(phases), -np.sin(phases)], 1)
    return table.astype(np.float32).astype(jnp.bfloat16)


def split(x):
    hi = x.astype(jnp.bfloat16)
    lo = (x - hi.astype(jnp.float32)).astype(jnp.bfloat16)
    return hi, lo


def dot(a, b, trans_b):
    dims = (((1,), (1 if trans_b else 0,)), ((), ()))
    return lax.dot_general(a, b, dims, preferred_element_type=jnp.float32)


def wrap(x, n):
    return jnp.where(x >= n, x - n, x)


def ratio(x, n):
    return x if n == 1 else x // n


def each(low, high, act):
    def body(k, carry):
        act(k)
        return carry

    if high - low <= 1:
        for k in range(low, high):
            act(k)
    else:
        lax.fori_loop(low, high, body, 0)


def greet(count):
    n_chan, n_tm = lax.axis_size("chan"), lax.axis_size("tm")
    c, t = lax.axis_index("chan"), lax.axis_index("tm")
    rep = n_chan // count
    place = ratio(c, rep)
    barrier = pltpu.get_barrier_semaphore()

    def signal(chan, tm):
        pl.semaphore_signal(barrier, inc=1, device_id=(chan, tm), device_id_type=MESH)

    each(1, n_chan, lambda k: signal(wrap(c + k, n_chan), t))
    for at, shift in ((0, n_tm - 1), (count - 1, 1)):

        @pl.when(place == at)
        def _(shift=shift):
            each(0, n_chan, lambda k: signal(k, wrap(t + shift, n_tm)))

    for j in range(1, n_tm):
        signal(c, wrap(t + j, n_tm))
    return n_chan - 1 + 2 * rep + n_tm - 1


def gather(answers, samples, slab, window, edge, sent, recv, edge_sent, edge_recv):
    n_chan, n_tm = lax.axis_size("chan"), lax.axis_size("tm")
    c, t = lax.axis_index("chan"), lax.axis_index("tm")
    rows, width = samples.shape
    channels = slab.shape[1]
    count = width // BLOCK
    rep = n_chan // count
    values = samples[...]
    turned = jnp.concatenate([values[:, width - HALF :], values, values[:, :HALF]], 1)
    for j in range(count + 1):
        window[j] = turned[:, BLOCK * j : BLOCK * (j + 1)].astype(jnp.bfloat16)
    pl.semaphore_wait(pltpu.get_barrier_semaphore(), answers)
    mine = pl.ds(pl.multiple_of(c * rows, rows), rows)
    place = ratio(c, rep)

    def remote(to):
        return pltpu.make_async_remote_copy(
            src_ref=window.at[pl.ds(ratio(to, rep), 2)],
            dst_ref=slab.at[:, mine, :],
            send_sem=sent,
            recv_sem=recv,
            device_id=(to, t),
            device_id_type=MESH,
        )

    def rim(to, shift):
        return pltpu.make_async_remote_copy(
            src_ref=window.at[0],
            dst_ref=edge.at[mine, :],
            send_sem=edge_sent,
            recv_sem=edge_recv,
            device_id=(to, wrap(t + shift, n_tm)),
            device_id_type=MESH,
        )

    each(1, n_chan, lambda k: remote(n_chan - k - jnp.where(c >= n_chan - k, 1, 0)).start())
    for r in range(rep):
        rim(r, 1).start()
        rim((count - 1) * rep + r, n_tm - 1).start()
    for j in range(2):
        slab[j, mine, :] = window[place + j]

    def bytes_of(ref, sem):
        return pltpu.make_async_copy(ref, ref, sem)

    others = channels - rows
    bytes_of(slab.at[:, pl.ds(0, others), :], recv).wait()

    @pl.when(jnp.logical_or(place == 0, place == count - 1))
    def _():
        bytes_of(edge, edge_recv).wait()

    left = lax.broadcasted_iota(jnp.int32, edge.shape, 1) < HALF

    @pl.when(place == 0)
    def _():
        slab[0] = jnp.where(left, edge[...], slab[0])

    @pl.when(place == count - 1)
    def _():
        slab[1] = jnp.where(left, slab[1], edge[...])

    def settle():
        bytes_of(slab.at[:, pl.ds(0, others), :], sent).wait()
        bytes_of(window.at[pl.ds(0, 2 * rep)], edge_sent).wait()

    return settle


def shrink(aa, ab, ba, bb, cut_one, cut_two):
    re1, im1, re2, im2 = aa - bb, ab + ba, aa + bb, ab - ba
    f1 = jnp.maximum(0.5 - cut_one * lax.rsqrt(re1 * re1 + im1 * im1), 0.0)
    f2 = jnp.maximum(0.5 - cut_two * lax.rsqrt(re2 * re2 + im2 * im2), 0.0)
    re1, im1, re2, im2 = re1 * f1, im1 * f1, re2 * f2, im2 * f2
    return re1 + re2, im1 + im2, im1 - im2, re2 - re1


def cut_of(cuts, level, orient):
    scale = math.sqrt(0.5) / 32.0
    return [cuts[level, 2 * orient + k].astype(jnp.float32) * scale for k in range(2)]


def cut_maps(cuts, level, shape):
    row_low = lax.broadcasted_iota(jnp.int32, shape, 0) < shape[0] // 2
    col_low = lax.broadcasted_iota(jnp.int32, shape, 1) < shape[1] // 2
    lh, hl, hh = (cut_of(cuts, level, o) for o in range(3))
    pick = [jnp.where(row_low, lh[k], jnp.where(col_low, hl[k], hh[k])) for k in range(2)]
    return pick[0], pick[1], jnp.logical_and(row_low, col_low)


def quarters(x):
    r, n = x.shape[0] // 2, x.shape[1] // 2
    return x[:r, :n], x[:r, n:], x[r:, :n], x[r:, n:]


def joined(parts):
    aa, ab, ba, bb = parts
    return jnp.concatenate(
        [jnp.concatenate([aa, ab], 1), jnp.concatenate([ba, bb], 1)], 0
    )


def synthesised(x, table):
    rows = x.shape[0]
    y = dot(jnp.concatenate(split(x), 0), table, False)
    return y[:rows, :BLOCK] + (y[:rows, BLOCK:] + y[rows:, :BLOCK])


def denoise(cuts, slab, chosen, tables, picked, cleaned):
    chan, chan_back, time, time_back = tables
    rows = slab.shape[1]
    length = time.shape[1]
    deep = time_back.shape[0]
    x = jnp.concatenate([slab[0], slab[1]], 1)
    y = dot(time[...], x, True)

    def timed(low, high):
        return y[low[0] : low[1]] + y[high[0] : high[1]]

    first_low = split(timed((0, length), (3 * length, 4 * length)))
    first_high = split(timed((length, 2 * length), (2 * length, 3 * length)))
    second = split(timed((4 * length, 5 * length), (5 * length, 6 * length)))
    third = split(timed((6 * length, 6 * length + length // 2), (6 * length + length // 2, 7 * length)))

    a = dot(chan[: 4 * rows, :], first_high[0], True)
    b = dot(chan[: 2 * rows, :], first_high[1], True)
    lh = joined(shrink(*quarters(a[:rows] + (a[3 * rows :] + b[:rows])), *cut_of(cuts, 0, 0)))
    hh = a[rows : 2 * rows] + (a[2 * rows : 3 * rows] + b[rows:])
    hh = joined(shrink(*quarters(hh), *cut_of(cuts, 0, 2)))
    a = dot(chan[rows : 3 * rows, :], first_low[0], True)
    b = dot(chan[rows : 2 * rows, :], first_low[1], True)
    hl = joined(shrink(*quarters(a[:rows] + (a[rows:] + b)), *cut_of(cuts, 0, 1)))

    a = dot(chan[4 * rows : 6 * rows, :], second[0], True)
    z = quarters(a[:rows] + (a[rows:] + dot(chan[4 * rows : 5 * rows, :], second[1], True)))
    one, two, kept = cut_maps(cuts, 1, z[0].shape)
    mid = joined([jnp.where(kept, 0.0, p) for p in shrink(*z, one, two)])

    a = dot(chan[6 * rows :, :], jnp.concatenate(third, 0), True)
    width = a.shape[1] // 2
    z = quarters(a[: rows // 2, :width] + (a[: rows // 2, width:] + a[rows // 2 :, :width]))
    one, two, kept = cut_maps(cuts, 2, z[0].shape)
    last = joined([jnp.where(kept, p, q) for p, q in zip(z, shrink(*z, one, two))])

    back = jnp.concatenate(
        [
            synthesised(lh, time_back[length : 2 * length, :]),
            synthesised(jnp.concatenate([hl, hh], 1), time_back[: 2 * length, :]),
            synthesised(mid, time_back[2 * length : 3 * length, :]),
            synthesised(last, time_back[3 * length : deep, :]),
        ],
        0,
    )
    y = dot(chan_back[...], jnp.concatenate(split(back), 1), False)
    whole = y[:rows, :BLOCK] + (y[:rows, BLOCK:] + y[rows:, :BLOCK])
    result = (0.25 * whole).astype(jnp.bfloat16)
    cleaned[...] = result.astype(jnp.float32).reshape(rows // 8, 8, BLOCK).astype(jnp.bfloat16)
    picked[...] = dot(chosen[...], result, False).astype(jnp.bfloat16)


def spread(picks, cleaned, receivers, sent, recv, crossed, sent_rows, landed):
    n_chan, n_tm = lax.axis_size("chan"), lax.axis_size("tm")
    c, t = lax.axis_index("chan"), lax.axis_index("tm")
    blocks = picks.shape[0]
    count = blocks // n_tm
    rep = n_chan // count
    pairs = n_tm // 2
    share = cleaned.shape[0] * 8 // (n_chan * n_tm)
    place = ratio(c, rep)
    copy_index = c - place * rep
    pair = t // 2
    core = t - 2 * pair
    other_core = t + 1 - 2 * core
    mine = t * count + place

    def move(block, sem, chan, tm):
        return pltpu.make_async_remote_copy(
            src_ref=picks.at[block],
            dst_ref=picks.at[block],
            send_sem=sent,
            recv_sem=sem,
            device_id=(chan, tm),
            device_id_type=MESH,
        )

    def chan_of(place):
        return place * rep + copy_index

    def block_at(k, u):
        tm = t if u == 0 else wrap(pair + pairs - u, pairs) * 2 + core
        return tm * count + (place if isinstance(k, int) and k == 0 else wrap(place + count - k, count))

    def rows_of(dc, dt):
        at = dc * n_tm + dt
        return at * (share // 8) if share % 8 == 0 else at * share // 8

    def personal(k):
        to = k + jnp.where(k >= place * n_tm + t, 1, 0)
        chan, to_tm = chan_of(to // n_tm), lax.rem(to, n_tm)
        return pltpu.make_async_remote_copy(
            src_ref=cleaned.at[rows_of(chan, to_tm)],
            dst_ref=receivers.at[mine],
            send_sem=sent_rows,
            recv_sem=landed,
            device_id=(chan, to_tm),
            device_id_type=MESH,
        )

    def relay(k, u):
        block = block_at(k, u)
        copy = move(block, crossed.at[min(u, 1)], c, other_core)
        if u or not isinstance(k, int) or k:
            move(block, recv.at[block], c, other_core).wait_recv()
        copy.start()

    def along_chan(k):
        to = k + jnp.where(k >= place, 1, 0)
        move(mine, recv.at[mine], chan_of(to), t).start()

    def bytes_of(ref, sem):
        return pltpu.make_async_copy(ref, ref, sem)

    each(0, count - 1, along_chan)
    local = pltpu.make_async_copy(cleaned.at[rows_of(c, t)], receivers.at[mine], landed)
    local.start()
    relay(0, 0)
    each(0, blocks - 1, lambda k: personal(k).start())
    for u in range(1, pairs):
        to = wrap(pair + u, pairs) * 2 + core
        each(0, count, lambda k, to=to: move(mine, recv.at[mine], chan_of(k), to).start())

    def near():
        each(1, count, lambda k: relay(k, 0))
        bytes_of(picks.at[pl.ds(0, count)], crossed.at[0]).wait()
        bytes_of(receivers, landed).wait()

    def far():
        for u in range(1, pairs):
            each(0, count, lambda k, u=u: relay(k, u))
        bytes_of(picks.at[pl.ds(0, (pairs - 1) * count)], crossed.at[1]).wait()

    def settle():
        bytes_of(picks.at[pl.ds(0, blocks - 1)], sent).wait()
        bytes_of(receivers.at[pl.ds(0, blocks - 1)], sent_rows).wait()

    return near, far, settle


def whole_kernel(n_tables, cuts, samples, sources, *refs):
    stored, refs = refs[:n_tables], refs[n_tables:]
    white, heard, partial, picks, receivers, white_own, heard_own = refs[:7]
    held, refs = refs[7 : 7 + n_tables], refs[7 + n_tables :]
    here, refs = refs[:4], refs[4:]
    slab, window, edge, chosen, cleaned, loads = refs[:6]
    gather_sems, spread_sems = refs[6:10], refs[10:]
    inputs = [
        pltpu.make_async_copy(a, b, here[3].at[i])
        for i, (a, b) in enumerate(zip((cuts, samples, sources), here))
    ]
    inputs[1].start()
    answers = greet(window.shape[0] - 1)
    inputs[0].start()
    inputs[2].start()
    copies = [pltpu.make_async_copy(a, b, loads.at[i]) for i, (a, b) in enumerate(zip(stored, held))]
    for copy in copies:
        copy.start()
    inputs[2].wait()
    cuts, samples, sources = here[:3]
    one_hot = jnp.where(
        lax.broadcasted_iota(jnp.int32, chosen.shape[::-1], 0) == sources[...], 1.0, 0.0
    )
    chosen[...] = jnp.transpose(one_hot).astype(jnp.bfloat16)
    inputs[1].wait()
    gathered = gather(answers, samples, slab, window, edge, *gather_sems)
    inputs[0].wait()
    for copy in copies[:-1]:
        copy.wait()
    time, time_back, chan_back = held[:3]
    chan = held[3] if n_tables == 5 else time
    n_tm = lax.axis_size("tm")
    count = picks.shape[0] // n_tm
    rep = lax.axis_size("chan") // count
    mine = lax.axis_index("tm") * count + ratio(lax.axis_index("chan"), rep)
    denoise(cuts, slab, chosen, (chan, chan_back, time, time_back), picks.at[mine], cleaned)
    near, far, settle = spread(picks, cleaned, receivers, *spread_sems)
    copies[-1].wait()
    t = lax.axis_index("tm")
    pair = t // 2
    pairs = n_tm // 2
    near()
    own = [2 * pair, 2 * pair + 1]
    whiten(picks, receivers, held[-1], white_own, heard_own, own)
    windows, sources = heard_own.shape[1] // 8, picks.shape[1]
    partial_products(white_own, heard_own, partial, windows, sources)
    far()
    rest = [2 * wrap(pair + u, pairs) + side for u in range(1, pairs) for side in range(2)]
    whiten(picks, receivers, held[-1], white, heard, rest)
    gathered()
    settle()


def whiten(picks, receivers, table, white, heard, parts):
    per_window = N // BLOCK
    sources = picks.shape[1]
    count = picks.shape[0] // lax.axis_size("tm")
    starts = [tm * count + i for tm in parts for i in range(0, count, per_window)]
    windows = len(starts)

    def window(ref, start):
        return jnp.concatenate([ref[start + j] for j in range(per_window)], 1)

    rows = [window(receivers, start).astype(jnp.float32) for start in starts]
    block = jnp.concatenate(
        [window(picks, start) for start in starts]
        + [jnp.concatenate(rows, 0).astype(jnp.bfloat16)],
        0,
    )
    spectra = dot(block, table[...], False)
    scale = lax.rsqrt(jnp.mean(spectra * spectra, axis=1, keepdims=True) + 1e-05)
    spectra = (spectra * scale).astype(jnp.bfloat16).astype(jnp.float32)
    base = windows * sources
    chunks = BINS // BLOCK
    weight = jnp.where(lax.broadcasted_iota(jnp.int32, (1, BLOCK), 1) == 0, 1.0, 2.0)
    for part in range(chunks):
        real = spectra[:, BLOCK * part : BLOCK * (part + 1)]
        imag = spectra[:, BINS + BLOCK * part : BINS + BLOCK * (part + 1)]
        white[part, :base, :] = real[:base]
        white[chunks + part, :base, :] = imag[:base]
        white[2 * chunks + part, :base, :] = real[:base] + imag[:base]
        real, imag = (x[base:] * (2.0 if part else weight) for x in (real, imag))
        heard[part, : 8 * windows, :] = real
        heard[chunks + part, : 8 * windows, :] = real + imag
        heard[2 * chunks + part, : 8 * windows, :] = real - imag


def products(white, heard, windows, sources, columns, first, count, finish):
    chunks = BINS // BLOCK
    near = [
        [heard[kind * chunks + columns, 8 * w : 8 * w + 8, :] for kind in range(3)]
        for w in range(windows)
    ]
    found = [[], []]
    for j in range(count):
        sums = [None] * 3
        for w in range(windows):
            spot = pl.ds(w * sources + first + j, 8, stride=0)
            for n, kind in enumerate((2, 0, 1)):
                term = white.at[kind * chunks + columns][spot, :] * near[w][n]
                sums[n] = term if sums[n] is None else sums[n] + term
        found[0].append(sums[0] - sums[2])
        found[1].append(sums[0] - sums[1])
    for at, values in zip((columns * BLOCK, BINS + columns * BLOCK), found):
        finish(slice(at, at + BLOCK), jnp.concatenate(values, 0))


def partial_products(white, heard, partial, windows, sources):
    group = math.gcd(32, sources)
    for part in range(BINS // BLOCK):

        def body(g, carry, part=part):
            spot = pl.ds(pl.multiple_of(8 * group * g, 8 * group), 8 * group)

            def finish(at, value):
                partial[spot, at] = value

            products(white, heard, windows, sources, part, group * g, group, finish)
            return carry

        lax.fori_loop(0, sources // group, body, 0)


def lag_kernel(sources, white, heard, partial, lags, out, cross, held, sems):
    parts, rows = held.shape[:2]
    windows = white.shape[1] // sources
    each_part = rows // 8
    group = math.gcd(each_part if windows <= 2 else 16, each_part)
    copies = []
    for i in range(parts):
        for part in range(BINS // BLOCK):

            def body(g, carry, i=i, part=part):
                start = 8 * (i * each_part + group * g)
                if not isinstance(start, int):
                    start = pl.multiple_of(start, 8 * group)
                spot = pl.ds(start, 8 * group)

                def finish(at, value):
                    cross[spot, at] = (value + partial[spot, at]).astype(jnp.bfloat16)

                first = i * each_part + group * g
                products(white, heard, windows, sources, part, first, group, finish)
                return carry

            if group == each_part:
                body(0, 0)
            else:
                lax.fori_loop(0, each_part // group, body, 0)
        part = slice(i * rows, (i + 1) * rows)
        held[i] = dot(cross[part, :], lags[...], False)
        copies.append(pltpu.make_async_copy(held.at[i], out.at[part, :], sems.at[i]))
        copies[i].start()
    for copy in copies:
        copy.wait()


def local(samples, thresholds, sources):
    n_chan, n_tm = lax.axis_size("chan"), lax.axis_size("tm")
    rows, width = samples.shape
    channels = rows * n_chan
    count = width // BLOCK
    rep = n_chan // count
    blocks = count * n_tm
    windows = n_tm * width // N
    picked_count = sources.shape[0]
    vmem = pl.BlockSpec(memory_space=pltpu.VMEM)
    hbm = pl.BlockSpec(memory_space=pltpu.HBM)
    dma = pltpu.SemaphoreType.DMA
    f32, bf16 = jnp.float32, jnp.bfloat16
    big = (40 if channels == 2 * BLOCK else 47) * 1024 * 1024

    time = stacked(levels_of(2 * BLOCK))
    back = halves(levels_of(2 * BLOCK)[:, HALF : HALF + BLOCK])
    chan = levels_of(channels)
    chan_back = two_halves(np.ascontiguousarray(chan.T))
    tables = [time, np.concatenate([back[0], back[1]], 1), chan_back]
    if channels != 2 * BLOCK:
        tables.append(stacked(chan))
    tables.append(dft_table())

    chunks = BINS // BLOCK
    each_tm = width // N
    most = (n_tm - 2) * each_tm
    spectra = pl.pallas_call(
        functools.partial(whole_kernel, len(tables)),
        out_shape=(
            pltpu.VMEM((3 * chunks, most * picked_count, BLOCK), f32),
            pltpu.VMEM((3 * chunks, most * 8, BLOCK), f32),
            pltpu.VMEM((picked_count * 8, N), f32),
        ),
        in_specs=[hbm] * (3 + len(tables)),
        out_specs=(vmem, vmem, vmem),
        scratch_shapes=[
            pltpu.VMEM((blocks, picked_count, BLOCK), bf16),
            pltpu.VMEM((blocks, 8, BLOCK), bf16),
            pltpu.VMEM((3 * chunks, 2 * each_tm * picked_count, BLOCK), f32),
            pltpu.VMEM((3 * chunks, 2 * each_tm * 8, BLOCK), f32),
        ]
        + [pltpu.VMEM(a.shape, bf16) for a in tables]
        + [
            pltpu.SMEM(thresholds.shape, jnp.int32),
            pltpu.VMEM(samples.shape, f32),
            pltpu.VMEM((1, picked_count), jnp.int32),
            dma((3,)),
        ]
        + [
            pltpu.VMEM((2, channels, BLOCK), bf16),
            pltpu.VMEM((count + 1, rows, BLOCK), bf16),
            pltpu.VMEM((channels, BLOCK), bf16),
            pltpu.VMEM((picked_count, channels), bf16),
            pltpu.VMEM((channels // 8, 8, BLOCK), bf16),
            dma((len(tables),)),
            dma,
            dma,
            dma,
            dma,
            dma,
            dma((blocks,)),
            dma((2,)),
            dma,
            dma,
        ],
        compiler_params=pltpu.CompilerParams(
            collective_id=0, has_side_effects=True, vmem_limit_bytes=big
        ),
        name="whole",
    )(*[
        pltpu.with_memory_space_constraint(a, pltpu.HBM)
        for a in (thresholds, samples, sources[None, :], *[jnp.asarray(a) for a in tables])
    ])

    half = LAGS // 2
    dft = tables[-1]
    lags = np.concatenate([dft[N - half :], dft[:half]], 0).T.astype(np.float32)
    lags = (lags / math.sqrt(windows * N)).astype(jnp.bfloat16)
    out = pl.pallas_call(
        functools.partial(lag_kernel, picked_count),
        out_shape=jax.ShapeDtypeStruct((picked_count * 8, LAGS), f32),
        in_specs=[vmem] * 4,
        out_specs=pl.BlockSpec(memory_space=pl.ANY),
        scratch_shapes=[
            pltpu.VMEM((picked_count * 8, N), bf16),
            pltpu.VMEM((2, picked_count * 4, LAGS), f32),
            dma((2,)),
        ],
        compiler_params=pltpu.CompilerParams(vmem_limit_bytes=16 * 1024 * 1024),
        name="lags",
    )(*spectra, jnp.asarray(lags))

    out = out.reshape(picked_count, 8, LAGS)
    share = channels // (n_chan * n_tm)
    if share < 8:
        place = lax.axis_index("chan") * n_tm + lax.axis_index("tm")
        out = lax.dynamic_slice_in_dim(out, lax.rem(place * share, 8), share, 1)
    return out


def solution(mesh):
    return jax.shard_map(
        local,
        mesh=mesh,
        in_specs=(P("chan", "tm"), P(), P()),
        out_specs=P(None, ("chan", "tm"), None),
        check_vma=False,
    )
```

```python
import functools
import math

import jax
import jax.numpy as jnp
import numpy as np
from jax import lax
from jax.experimental import pallas as pl
from jax.experimental.pallas import tpu as pltpu
from jax.sharding import PartitionSpec as P

N = 1024
LEVELS = 3
BINS = 512
LAGS = 512
BLOCK = 128
HALF = 64
MESH = pl.DeviceIdType.MESH

daubechies = [
    0.2303778133088964,
    0.7148465705529155,
    0.6308807679298587,
    -0.0279837694168599,
    -0.1870348117190931,
    0.0308413818355607,
    0.0328830116668852,
    -0.010597401785069,
]


def filter_bank():
    lowpass = list(daubechies)
    highpass = [(1.0 if k % 2 == 0 else -1.0) * daubechies[7 - k] for k in range(8)]
    return [(lowpass, highpass), (lowpass[::-1], highpass[::-1])]


def bank_matrix(length):
    half = length // 2
    out = np.zeros((2, 2, half, length))
    rows = np.arange(half)
    for tree, pair in enumerate(filter_bank()):
        for band, taps in enumerate(pair):
            for k in range(8):
                np.add.at(out[tree, band], (rows, (2 * rows + k - 3) % length), taps[k])
    return out


def levels_of(length):
    first, second, third = (bank_matrix(length >> level) for level in range(3))
    parts = [first[0, 0], first[1, 0], first[0, 1], first[1, 1]]
    for tree in range(2):
        parts += [second[tree, band] @ first[tree, 0] for band in range(2)]
    for tree in range(2):
        low = second[tree, 0] @ first[tree, 0]
        parts += [third[tree, band] @ low for band in range(2)]
    return np.concatenate(parts, 0)


def halves(matrix):
    m32 = np.asarray(matrix, np.float32)
    hi = m32.astype(jnp.bfloat16)
    lo = (m32 - hi.astype(np.float32)).astype(jnp.bfloat16)
    return np.stack([hi, lo])


def two_halves(matrix):
    return np.concatenate(list(halves(matrix)), 0)


def stacked(matrix):
    hi, lo = halves(matrix)
    n = matrix.shape[1]
    parts = [hi[: 2 * n], lo[n : 2 * n], lo[:n]]
    parts += [x[at] for at in (slice(2 * n, 3 * n), slice(3 * n, None)) for x in (hi, lo)]
    return np.concatenate(parts, 0)


def dft_table():
    t = np.arange(N)
    f = np.arange(BINS)
    phases = ((t[:, None] * f[None, :]) % N).astype(np.float64) * (2.0 * math.pi / N)
    table = np.concatenate([np.cos(phases), -np.sin(phases)], 1)
    return table.astype(np.float32).astype(jnp.bfloat16)


def split(x):
    hi = x.astype(jnp.bfloat16)
    lo = (x - hi.astype(jnp.float32)).astype(jnp.bfloat16)
    return hi, lo


def dot(a, b, trans_b):
    dims = (((1,), (1 if trans_b else 0,)), ((), ()))
    return lax.dot_general(a, b, dims, preferred_element_type=jnp.float32)


def wrap(x, n):
    return jnp.where(x >= n, x - n, x)


def ratio(x, n):
    return x if n == 1 else x // n


def turned(seat, count):
    return wrap(seat + count // 2, count)


def each(low, high, act):
    def body(k, carry):
        act(k)
        return carry

    if high - low <= 1:
        for k in range(low, high):
            act(k)
    else:
        lax.fori_loop(low, high, body, 0)


def greet(count):
    n_chan, n_tm = lax.axis_size("chan"), lax.axis_size("tm")
    c, t = lax.axis_index("chan"), lax.axis_index("tm")
    rep = n_chan // count
    place = turned(ratio(c, rep), count)
    barrier = pltpu.get_barrier_semaphore()

    def signal(chan, tm):
        pl.semaphore_signal(barrier, inc=1, device_id=(chan, tm), device_id_type=MESH)

    each(1, n_chan, lambda k: signal(wrap(c + k, n_chan), t))
    for at, shift in ((0, n_tm - 1), (count - 1, 1)):

        @pl.when(place == at)
        def _(shift=shift):
            each(0, n_chan, lambda k: signal(k, wrap(t + shift, n_tm)))

    for j in range(1, n_tm):
        signal(c, wrap(t + j, n_tm))
    return n_chan - 1 + 2 * rep + n_tm - 1


def gather(meanwhile, answers, samples, slab, window, edge, sent, recv, edge_sent, edge_recv):
    n_chan, n_tm = lax.axis_size("chan"), lax.axis_size("tm")
    c, t = lax.axis_index("chan"), lax.axis_index("tm")
    rows, width = samples.shape
    channels = slab.shape[1]
    count = width // BLOCK
    rep = n_chan // count
    values = samples[...]
    around = jnp.concatenate([values[:, width - HALF :], values, values[:, :HALF]], 1)
    for j in range(count + 1):
        window[j] = around[:, BLOCK * j : BLOCK * (j + 1)].astype(jnp.bfloat16)
    pl.semaphore_wait(pltpu.get_barrier_semaphore(), answers)
    mine = pl.ds(pl.multiple_of(c * rows, rows), rows)
    place = turned(ratio(c, rep), count)

    def remote(to):
        return pltpu.make_async_remote_copy(
            src_ref=window.at[pl.ds(turned(ratio(to, rep), count), 2)],
            dst_ref=slab.at[:, mine, :],
            send_sem=sent,
            recv_sem=recv,
            device_id=(to, t),
            device_id_type=MESH,
        )

    def rim(block, r, shift):
        tm = wrap(t + shift, n_tm)
        return pltpu.make_async_remote_copy(
            src_ref=window.at[0],
            dst_ref=edge.at[mine, :],
            send_sem=edge_sent,
            recv_sem=edge_recv,
            device_id=(turned(block, count) * rep + r, tm),
            device_id_type=MESH,
        )

    each(1, n_chan, lambda k: remote(n_chan - k - jnp.where(c >= n_chan - k, 1, 0)).start())
    for r in range(rep):
        rim(0, r, 1).start()
        rim(count - 1, r, n_tm - 1).start()
    for j in range(2):
        slab[j, mine, :] = window[place + j]
    meanwhile()

    def bytes_of(ref, sem):
        return pltpu.make_async_copy(ref, ref, sem)

    others = channels - rows
    bytes_of(slab.at[:, pl.ds(0, others), :], recv).wait()

    @pl.when(jnp.logical_or(place == 0, place == count - 1))
    def _():
        bytes_of(edge, edge_recv).wait()

    left = lax.broadcasted_iota(jnp.int32, edge.shape, 1) < HALF

    @pl.when(place == 0)
    def _():
        slab[0] = jnp.where(left, edge[...], slab[0])

    @pl.when(place == count - 1)
    def _():
        slab[1] = jnp.where(left, slab[1], edge[...])

    def settle():
        bytes_of(slab.at[:, pl.ds(0, others), :], sent).wait()
        bytes_of(window.at[pl.ds(0, 2 * rep)], edge_sent).wait()

    return settle


def shrink(aa, ab, ba, bb, cut_one, cut_two):
    re1, im1, re2, im2 = aa - bb, ab + ba, aa + bb, ab - ba
    f1 = jnp.maximum(0.5 - cut_one * lax.rsqrt(re1 * re1 + im1 * im1), 0.0)
    f2 = jnp.maximum(0.5 - cut_two * lax.rsqrt(re2 * re2 + im2 * im2), 0.0)
    re1, im1, re2, im2 = re1 * f1, im1 * f1, re2 * f2, im2 * f2
    return re1 + re2, im1 + im2, im1 - im2, re2 - re1


def cut_of(cuts, level, orient):
    scale = math.sqrt(0.5) / 32.0
    return [cuts[level, 2 * orient + k].astype(jnp.float32) * scale for k in range(2)]


def cut_maps(cuts, level, shape):
    row_low = lax.broadcasted_iota(jnp.int32, shape, 0) < shape[0] // 2
    col_low = lax.broadcasted_iota(jnp.int32, shape, 1) < shape[1] // 2
    lh, hl, hh = (cut_of(cuts, level, o) for o in range(3))
    pick = [jnp.where(row_low, lh[k], jnp.where(col_low, hl[k], hh[k])) for k in range(2)]
    return pick[0], pick[1], jnp.logical_and(row_low, col_low)


def quarters(x):
    r, n = x.shape[0] // 2, x.shape[1] // 2
    return x[:r, :n], x[:r, n:], x[r:, :n], x[r:, n:]


def joined(parts):
    aa, ab, ba, bb = parts
    return jnp.concatenate(
        [jnp.concatenate([aa, ab], 1), jnp.concatenate([ba, bb], 1)], 0
    )


def synthesised(x, table):
    rows = x.shape[0]
    y = dot(jnp.concatenate(split(x), 0), table, False)
    return y[:rows, :BLOCK] + (y[:rows, BLOCK:] + y[rows:, :BLOCK])


def denoise(cuts, slab, chosen, tables, picked, cleaned):
    chan, chan_back, time, time_back = tables
    rows = slab.shape[1]
    length = time.shape[1]
    deep = time_back.shape[0]
    x = jnp.concatenate([slab[0], slab[1]], 1)
    y = dot(time[...], x, True)

    def timed(low, high):
        return y[low[0] : low[1]] + y[high[0] : high[1]]

    first_low = split(timed((0, length), (3 * length, 4 * length)))
    first_high = split(timed((length, 2 * length), (2 * length, 3 * length)))
    second = split(timed((4 * length, 5 * length), (5 * length, 6 * length)))
    third = split(timed((6 * length, 6 * length + length // 2), (6 * length + length // 2, 7 * length)))

    a = dot(chan[: 4 * rows, :], first_high[0], True)
    b = dot(chan[: 2 * rows, :], first_high[1], True)
    lh = joined(shrink(*quarters(a[:rows] + (a[3 * rows :] + b[:rows])), *cut_of(cuts, 0, 0)))
    hh = a[rows : 2 * rows] + (a[2 * rows : 3 * rows] + b[rows:])
    hh = joined(shrink(*quarters(hh), *cut_of(cuts, 0, 2)))
    a = dot(chan[rows : 3 * rows, :], first_low[0], True)
    b = dot(chan[rows : 2 * rows, :], first_low[1], True)
    hl = joined(shrink(*quarters(a[:rows] + (a[rows:] + b)), *cut_of(cuts, 0, 1)))

    a = dot(chan[4 * rows : 6 * rows, :], second[0], True)
    z = quarters(a[:rows] + (a[rows:] + dot(chan[4 * rows : 5 * rows, :], second[1], True)))
    one, two, kept = cut_maps(cuts, 1, z[0].shape)
    mid = joined([jnp.where(kept, 0.0, p) for p in shrink(*z, one, two)])

    a = dot(chan[6 * rows :, :], jnp.concatenate(third, 0), True)
    width = a.shape[1] // 2
    z = quarters(a[: rows // 2, :width] + (a[: rows // 2, width:] + a[rows // 2 :, :width]))
    one, two, kept = cut_maps(cuts, 2, z[0].shape)
    last = joined([jnp.where(kept, p, q) for p, q in zip(z, shrink(*z, one, two))])

    back = jnp.concatenate(
        [
            synthesised(lh, time_back[length : 2 * length, :]),
            synthesised(jnp.concatenate([hl, hh], 1), time_back[: 2 * length, :]),
            synthesised(mid, time_back[2 * length : 3 * length, :]),
            synthesised(last, time_back[3 * length : deep, :]),
        ],
        0,
    )
    y = dot(chan_back[...], jnp.concatenate(split(back), 1), False)
    whole = y[:rows, :BLOCK] + (y[:rows, BLOCK:] + y[rows:, :BLOCK])
    result = (0.25 * whole).astype(jnp.bfloat16)
    cleaned[...] = result.astype(jnp.float32).reshape(rows // 8, 8, BLOCK).astype(jnp.bfloat16)
    picked[...] = dot(chosen[...], result, False).astype(jnp.bfloat16)


def spread(picks, cleaned, receivers, sent, recv, crossed, sent_rows, landed):
    n_chan, n_tm = lax.axis_size("chan"), lax.axis_size("tm")
    c, t = lax.axis_index("chan"), lax.axis_index("tm")
    blocks = picks.shape[0]
    count = blocks // n_tm
    rep = n_chan // count
    pairs = n_tm // 2
    share = cleaned.shape[0] * 8 // (n_chan * n_tm)
    seat = ratio(c, rep)
    copy_index = c - seat * rep
    place = turned(seat, count)
    pair = t // 2
    core = t - 2 * pair
    other_core = t + 1 - 2 * core
    mine = t * count + place

    def move(block, sem, chan, tm):
        return pltpu.make_async_remote_copy(
            src_ref=picks.at[block],
            dst_ref=picks.at[block],
            send_sem=sent,
            recv_sem=sem,
            device_id=(chan, tm),
            device_id_type=MESH,
        )

    def chan_of(seat):
        return seat * rep + copy_index

    def block_at(k, u):
        tm = t if u == 0 else wrap(pair + pairs - u, pairs) * 2 + core
        return tm * count + (place if isinstance(k, int) and k == 0 else wrap(place + count - k, count))

    def rows_of(dc, dt):
        at = dc * n_tm + dt
        return at * (share // 8) if share % 8 == 0 else at * share // 8

    def personal(k):
        to = k + jnp.where(k >= seat * n_tm + t, 1, 0)
        chan, to_tm = chan_of(to // n_tm), lax.rem(to, n_tm)
        return pltpu.make_async_remote_copy(
            src_ref=cleaned.at[rows_of(chan, to_tm)],
            dst_ref=receivers.at[mine],
            send_sem=sent_rows,
            recv_sem=landed,
            device_id=(chan, to_tm),
            device_id_type=MESH,
        )

    def relay(k, u):
        block = block_at(k, u)
        copy = move(block, crossed.at[min(u, 1)], c, other_core)
        if u or not isinstance(k, int) or k:
            move(block, recv.at[block], c, other_core).wait_recv()
        copy.start()

    def along_chan(k):
        to = k + jnp.where(k >= seat, 1, 0)
        move(mine, recv.at[mine], chan_of(to), t).start()

    def bytes_of(ref, sem):
        return pltpu.make_async_copy(ref, ref, sem)

    each(0, count - 1, along_chan)
    local = pltpu.make_async_copy(cleaned.at[rows_of(c, t)], receivers.at[mine], landed)
    local.start()
    relay(0, 0)
    each(0, blocks - 1, lambda k: personal(k).start())
    for u in range(1, pairs):
        to = wrap(pair + u, pairs) * 2 + core
        each(0, count, lambda k, to=to: move(mine, recv.at[mine], chan_of(k), to).start())

    def near():
        each(1, count, lambda k: relay(k, 0))
        bytes_of(picks.at[pl.ds(0, count)], crossed.at[0]).wait()
        bytes_of(receivers, landed).wait()

    def far():
        for u in range(1, pairs):
            each(0, count, lambda k, u=u: relay(k, u))
        bytes_of(picks.at[pl.ds(0, (pairs - 1) * count)], crossed.at[1]).wait()

    def settle():
        bytes_of(picks.at[pl.ds(0, blocks - 1)], sent).wait()
        bytes_of(receivers.at[pl.ds(0, blocks - 1)], sent_rows).wait()

    return near, far, settle


def whole_kernel(n_tables, cuts, samples, sources, *refs):
    stored, refs = refs[:n_tables], refs[n_tables:]
    white, heard, partial, picks, receivers, white_own, heard_own = refs[:7]
    held, refs = refs[7 : 7 + n_tables], refs[7 + n_tables :]
    here, refs = refs[:4], refs[4:]
    slab, window, edge, chosen, cleaned, loads = refs[:6]
    gather_sems, spread_sems = refs[6:10], refs[10:]
    inputs = [
        pltpu.make_async_copy(a, b, here[3].at[i])
        for i, (a, b) in enumerate(zip((cuts, samples, sources), here))
    ]
    inputs[1].start()
    answers = greet(window.shape[0] - 1)
    copies = [pltpu.make_async_copy(a, b, loads.at[i]) for i, (a, b) in enumerate(zip(stored, held))]

    def meanwhile():
        inputs[2].start()
        inputs[0].start()
        for copy in copies:
            copy.start()
        inputs[2].wait()
        shape = chosen.shape[::-1]
        one_hot = jnp.where(lax.broadcasted_iota(jnp.int32, shape, 0) == here[2][...], 1.0, 0.0)
        chosen[...] = jnp.transpose(one_hot).astype(jnp.bfloat16)

    inputs[1].wait()
    gathered = gather(meanwhile, answers, here[1], slab, window, edge, *gather_sems)
    inputs[0].wait()
    for copy in copies[:-1]:
        copy.wait()
    time, time_back, chan_back = held[:3]
    chan = held[3] if n_tables == 5 else time
    n_tm = lax.axis_size("tm")
    count = picks.shape[0] // n_tm
    rep = lax.axis_size("chan") // count
    t = lax.axis_index("tm")
    mine = t * count + turned(ratio(lax.axis_index("chan"), rep), count)
    denoise(here[0], slab, chosen, (chan, chan_back, time, time_back), picks.at[mine], cleaned)
    near, far, settle = spread(picks, cleaned, receivers, *spread_sems)
    copies[-1].wait()
    t = lax.axis_index("tm")
    pair = t // 2
    pairs = n_tm // 2
    near()
    own = [2 * pair, 2 * pair + 1]
    whiten(picks, receivers, held[-1], white_own, heard_own, own)
    windows, sources = heard_own.shape[1] // 8, picks.shape[1]
    partial_products(white_own, heard_own, partial, windows, sources)
    far()
    rest = [2 * wrap(pair + u, pairs) + side for u in range(1, pairs) for side in range(2)]
    whiten(picks, receivers, held[-1], white, heard, rest)
    gathered()
    settle()


def whiten(picks, receivers, table, white, heard, parts):
    per_window = N // BLOCK
    sources = picks.shape[1]
    count = picks.shape[0] // lax.axis_size("tm")
    starts = [tm * count + i for tm in parts for i in range(0, count, per_window)]
    windows = len(starts)

    def window(ref, start):
        return jnp.concatenate([ref[start + j] for j in range(per_window)], 1)

    rows = [window(receivers, start).astype(jnp.float32) for start in starts]
    block = jnp.concatenate(
        [window(picks, start) for start in starts]
        + [jnp.concatenate(rows, 0).astype(jnp.bfloat16)],
        0,
    )
    spectra = dot(block, table[...], False)
    scale = lax.rsqrt(jnp.mean(spectra * spectra, axis=1, keepdims=True) + 1e-05)
    spectra = (spectra * scale).astype(jnp.bfloat16).astype(jnp.float32)
    base = windows * sources
    chunks = BINS // BLOCK
    weight = jnp.where(lax.broadcasted_iota(jnp.int32, (1, BLOCK), 1) == 0, 1.0, 2.0)
    for part in range(chunks):
        real = spectra[:, BLOCK * part : BLOCK * (part + 1)]
        imag = spectra[:, BINS + BLOCK * part : BINS + BLOCK * (part + 1)]
        white[part, :base, :] = real[:base]
        white[chunks + part, :base, :] = imag[:base]
        white[2 * chunks + part, :base, :] = real[:base] + imag[:base]
        real, imag = (x[base:] * (2.0 if part else weight) for x in (real, imag))
        heard[part, : 8 * windows, :] = real
        heard[chunks + part, : 8 * windows, :] = real + imag
        heard[2 * chunks + part, : 8 * windows, :] = real - imag


def products(white, heard, windows, sources, columns, first, count, finish):
    chunks = BINS // BLOCK
    near = [
        [heard[kind * chunks + columns, 8 * w : 8 * w + 8, :] for kind in range(3)]
        for w in range(windows)
    ]
    found = [[], []]
    for j in range(count):
        sums = [None] * 3
        for w in range(windows):
            spot = pl.ds(w * sources + first + j, 8, stride=0)
            for n, kind in enumerate((2, 0, 1)):
                term = white.at[kind * chunks + columns][spot, :] * near[w][n]
                sums[n] = term if sums[n] is None else sums[n] + term
        found[0].append(sums[0] - sums[2])
        found[1].append(sums[0] - sums[1])
    for at, values in zip((columns * BLOCK, BINS + columns * BLOCK), found):
        finish(slice(at, at + BLOCK), jnp.concatenate(values, 0))


def partial_products(white, heard, partial, windows, sources):
    group = math.gcd(32, sources)
    for part in range(BINS // BLOCK):

        def body(g, carry, part=part):
            spot = pl.ds(pl.multiple_of(8 * group * g, 8 * group), 8 * group)

            def finish(at, value):
                partial[spot, at] = value

            products(white, heard, windows, sources, part, group * g, group, finish)
            return carry

        lax.fori_loop(0, sources // group, body, 0)


def lag_kernel(sources, white, heard, partial, lags, out, cross, held, sems):
    parts, rows = held.shape[:2]
    windows = white.shape[1] // sources
    each_part = rows // 8
    group = math.gcd(each_part if windows <= 2 else 16, each_part)
    copies = []
    for i in range(parts):
        for part in range(BINS // BLOCK):

            def body(g, carry, i=i, part=part):
                start = 8 * (i * each_part + group * g)
                if not isinstance(start, int):
                    start = pl.multiple_of(start, 8 * group)
                spot = pl.ds(start, 8 * group)

                def finish(at, value):
                    cross[spot, at] = (value + partial[spot, at]).astype(jnp.bfloat16)

                first = i * each_part + group * g
                products(white, heard, windows, sources, part, first, group, finish)
                return carry

            if group == each_part:
                body(0, 0)
            else:
                lax.fori_loop(0, each_part // group, body, 0)
        part = slice(i * rows, (i + 1) * rows)
        held[i] = dot(cross[part, :], lags[...], False)
        copies.append(pltpu.make_async_copy(held.at[i], out.at[part, :], sems.at[i]))
        copies[i].start()
    for copy in copies:
        copy.wait()


def local(samples, thresholds, sources):
    n_chan, n_tm = lax.axis_size("chan"), lax.axis_size("tm")
    rows, width = samples.shape
    channels = rows * n_chan
    count = width // BLOCK
    rep = n_chan // count
    blocks = count * n_tm
    windows = n_tm * width // N
    picked_count = sources.shape[0]
    vmem = pl.BlockSpec(memory_space=pltpu.VMEM)
    hbm = pl.BlockSpec(memory_space=pltpu.HBM)
    dma = pltpu.SemaphoreType.DMA
    f32, bf16 = jnp.float32, jnp.bfloat16
    big = (40 if channels == 2 * BLOCK else 47) * 1024 * 1024

    time = stacked(levels_of(2 * BLOCK))
    back = halves(levels_of(2 * BLOCK)[:, HALF : HALF + BLOCK])
    chan = levels_of(channels)
    chan_back = two_halves(np.ascontiguousarray(chan.T))
    tables = [time, np.concatenate([back[0], back[1]], 1), chan_back]
    if channels != 2 * BLOCK:
        tables.append(stacked(chan))
    tables.append(dft_table())

    chunks = BINS // BLOCK
    each_tm = width // N
    most = (n_tm - 2) * each_tm
    spectra = pl.pallas_call(
        functools.partial(whole_kernel, len(tables)),
        out_shape=(
            pltpu.VMEM((3 * chunks, most * picked_count, BLOCK), f32),
            pltpu.VMEM((3 * chunks, most * 8, BLOCK), f32),
            pltpu.VMEM((picked_count * 8, N), f32),
        ),
        in_specs=[hbm] * (3 + len(tables)),
        out_specs=(vmem, vmem, vmem),
        scratch_shapes=[
            pltpu.VMEM((blocks, picked_count, BLOCK), bf16),
            pltpu.VMEM((blocks, 8, BLOCK), bf16),
            pltpu.VMEM((3 * chunks, 2 * each_tm * picked_count, BLOCK), f32),
            pltpu.VMEM((3 * chunks, 2 * each_tm * 8, BLOCK), f32),
        ]
        + [pltpu.VMEM(a.shape, bf16) for a in tables]
        + [
            pltpu.SMEM(thresholds.shape, jnp.int32),
            pltpu.VMEM(samples.shape, f32),
            pltpu.VMEM((1, picked_count), jnp.int32),
            dma((3,)),
        ]
        + [
            pltpu.VMEM((2, channels, BLOCK), bf16),
            pltpu.VMEM((count + 1, rows, BLOCK), bf16),
            pltpu.VMEM((channels, BLOCK), bf16),
            pltpu.VMEM((picked_count, channels), bf16),
            pltpu.VMEM((channels // 8, 8, BLOCK), bf16),
            dma((len(tables),)),
            dma,
            dma,
            dma,
            dma,
            dma,
            dma((blocks,)),
            dma((2,)),
            dma,
            dma,
        ],
        compiler_params=pltpu.CompilerParams(
            collective_id=0, has_side_effects=True, vmem_limit_bytes=big
        ),
        name="whole",
    )(*[
        pltpu.with_memory_space_constraint(a, pltpu.HBM)
        for a in (thresholds, samples, sources[None, :], *[jnp.asarray(a) for a in tables])
    ])

    half = LAGS // 2
    dft = tables[-1]
    lags = np.concatenate([dft[N - half :], dft[:half]], 0).T.astype(np.float32)
    lags = (lags / math.sqrt(windows * N)).astype(jnp.bfloat16)
    out = pl.pallas_call(
        functools.partial(lag_kernel, picked_count),
        out_shape=jax.ShapeDtypeStruct((picked_count * 8, LAGS), f32),
        in_specs=[vmem] * 4,
        out_specs=pl.BlockSpec(memory_space=pl.ANY),
        scratch_shapes=[
            pltpu.VMEM((picked_count * 8, N), bf16),
            pltpu.VMEM((2, picked_count * 4, LAGS), f32),
            dma((2,)),
        ],
        compiler_params=pltpu.CompilerParams(vmem_limit_bytes=16 * 1024 * 1024),
        name="lags",
    )(*spectra, jnp.asarray(lags))

    out = out.reshape(picked_count, 8, LAGS)
    share = channels // (n_chan * n_tm)
    if share < 8:
        place = lax.axis_index("chan") * n_tm + lax.axis_index("tm")
        out = lax.dynamic_slice_in_dim(out, lax.rem(place * share, 8), share, 1)
    return out


def solution(mesh):
    return jax.shard_map(
        local,
        mesh=mesh,
        in_specs=(P("chan", "tm"), P(), P()),
        out_specs=P(None, ("chan", "tm"), None),
        check_vma=False,
    )
```

```python
import functools
import math

import jax
import jax.numpy as jnp
import numpy as np
from jax import lax
from jax.experimental import pallas as pl
from jax.experimental.pallas import tpu as pltpu
from jax.sharding import PartitionSpec as P

N = 1024
LEVELS = 3
BINS = 512
LAGS = 512
BLOCK = 128
HALF = 64
MESH = pl.DeviceIdType.MESH

daubechies = [
    0.2303778133088964,
    0.7148465705529155,
    0.6308807679298587,
    -0.0279837694168599,
    -0.1870348117190931,
    0.0308413818355607,
    0.0328830116668852,
    -0.010597401785069,
]


def filter_bank():
    lowpass = list(daubechies)
    highpass = [(1.0 if k % 2 == 0 else -1.0) * daubechies[7 - k] for k in range(8)]
    return [(lowpass, highpass), (lowpass[::-1], highpass[::-1])]


def bank_matrix(length):
    half = length // 2
    out = np.zeros((2, 2, half, length))
    rows = np.arange(half)
    for tree, pair in enumerate(filter_bank()):
        for band, taps in enumerate(pair):
            for k in range(8):
                np.add.at(out[tree, band], (rows, (2 * rows + k - 3) % length), taps[k])
    return out


def levels_of(length):
    first, second, third = (bank_matrix(length >> level) for level in range(3))
    parts = [first[0, 0], first[1, 0], first[0, 1], first[1, 1]]
    for tree in range(2):
        parts += [second[tree, band] @ first[tree, 0] for band in range(2)]
    for tree in range(2):
        low = second[tree, 0] @ first[tree, 0]
        parts += [third[tree, band] @ low for band in range(2)]
    return np.concatenate(parts, 0)


def halves(matrix):
    m32 = np.asarray(matrix, np.float32)
    hi = m32.astype(jnp.bfloat16)
    lo = (m32 - hi.astype(np.float32)).astype(jnp.bfloat16)
    return np.stack([hi, lo])


def two_halves(matrix):
    return np.concatenate(list(halves(matrix)), 0)


def stacked(matrix):
    hi, lo = halves(matrix)
    n = matrix.shape[1]
    parts = [hi[: 2 * n], lo[n : 2 * n], lo[:n]]
    parts += [x[at] for at in (slice(2 * n, 3 * n), slice(3 * n, None)) for x in (hi, lo)]
    return np.concatenate(parts, 0)


def dft_table():
    t = np.arange(N)
    f = np.arange(BINS)
    phases = ((t[:, None] * f[None, :]) % N).astype(np.float64) * (2.0 * math.pi / N)
    table = np.concatenate([np.cos(phases), -np.sin(phases)], 1)
    return table.astype(np.float32).astype(jnp.bfloat16)


def split(x):
    hi = x.astype(jnp.bfloat16)
    lo = (x - hi.astype(jnp.float32)).astype(jnp.bfloat16)
    return hi, lo


def dot(a, b, trans_b):
    dims = (((1,), (1 if trans_b else 0,)), ((), ()))
    return lax.dot_general(a, b, dims, preferred_element_type=jnp.float32)


def wrap(x, n):
    return jnp.where(x >= n, x - n, x)


def ratio(x, n):
    return x if n == 1 else x // n


def turned(seat, count):
    return wrap(seat + count // 2, count)


def each(low, high, act):
    def body(k, carry):
        act(k)
        return carry

    if high - low <= 1:
        for k in range(low, high):
            act(k)
    else:
        lax.fori_loop(low, high, body, 0)


def greet(count):
    n_chan, n_tm = lax.axis_size("chan"), lax.axis_size("tm")
    c, t = lax.axis_index("chan"), lax.axis_index("tm")
    rep = n_chan // count
    place = turned(ratio(c, rep), count)
    barrier = pltpu.get_barrier_semaphore()

    def signal(chan, tm):
        pl.semaphore_signal(barrier, inc=1, device_id=(chan, tm), device_id_type=MESH)

    each(1, n_chan, lambda k: signal(wrap(c + k, n_chan), t))
    for at, shift in ((0, n_tm - 1), (count - 1, 1)):

        @pl.when(place == at)
        def _(shift=shift):
            each(0, n_chan, lambda k: signal(k, wrap(t + shift, n_tm)))

    for j in range(1, n_tm):
        signal(c, wrap(t + j, n_tm))
    return n_chan - 1 + 2 * rep + n_tm - 1


def gather(meanwhile, answers, samples, slab, window, edge, sent, recv, edge_sent, edge_recv):
    n_chan, n_tm = lax.axis_size("chan"), lax.axis_size("tm")
    c, t = lax.axis_index("chan"), lax.axis_index("tm")
    rows, width = samples.shape
    channels = slab.shape[1]
    count = width // BLOCK
    rep = n_chan // count
    values = samples[...]
    around = jnp.concatenate([values[:, width - HALF :], values, values[:, :HALF]], 1)
    for j in range(count + 1):
        window[j] = around[:, BLOCK * j : BLOCK * (j + 1)].astype(jnp.bfloat16)
    pl.semaphore_wait(pltpu.get_barrier_semaphore(), answers)
    mine = pl.ds(pl.multiple_of(c * rows, rows), rows)
    place = turned(ratio(c, rep), count)

    def remote(to):
        return pltpu.make_async_remote_copy(
            src_ref=window.at[pl.ds(turned(ratio(to, rep), count), 2)],
            dst_ref=slab.at[:, mine, :],
            send_sem=sent,
            recv_sem=recv,
            device_id=(to, t),
            device_id_type=MESH,
        )

    def rim(block, r, shift):
        tm = wrap(t + shift, n_tm)
        return pltpu.make_async_remote_copy(
            src_ref=window.at[0],
            dst_ref=edge.at[mine, :],
            send_sem=edge_sent,
            recv_sem=edge_recv,
            device_id=(turned(block, count) * rep + r, tm),
            device_id_type=MESH,
        )

    each(1, n_chan, lambda k: remote(wrap(c + k, n_chan)).start())
    for r in range(rep):
        rim(0, r, 1).start()
        rim(count - 1, r, n_tm - 1).start()
    for j in range(2):
        slab[j, mine, :] = window[place + j]
    meanwhile()

    def bytes_of(ref, sem):
        return pltpu.make_async_copy(ref, ref, sem)

    others = channels - rows
    bytes_of(slab.at[:, pl.ds(0, others), :], recv).wait()

    @pl.when(jnp.logical_or(place == 0, place == count - 1))
    def _():
        bytes_of(edge, edge_recv).wait()

    left = lax.broadcasted_iota(jnp.int32, edge.shape, 1) < HALF

    @pl.when(place == 0)
    def _():
        slab[0] = jnp.where(left, edge[...], slab[0])

    @pl.when(place == count - 1)
    def _():
        slab[1] = jnp.where(left, slab[1], edge[...])

    def settle():
        bytes_of(slab.at[:, pl.ds(0, others), :], sent).wait()
        bytes_of(window.at[pl.ds(0, 2 * rep)], edge_sent).wait()

    return settle


def shrink(aa, ab, ba, bb, cut_one, cut_two):
    re1, im1, re2, im2 = aa - bb, ab + ba, aa + bb, ab - ba
    f1 = jnp.maximum(0.5 - cut_one * lax.rsqrt(re1 * re1 + im1 * im1), 0.0)
    f2 = jnp.maximum(0.5 - cut_two * lax.rsqrt(re2 * re2 + im2 * im2), 0.0)
    re1, im1, re2, im2 = re1 * f1, im1 * f1, re2 * f2, im2 * f2
    return re1 + re2, im1 + im2, im1 - im2, re2 - re1


def cut_of(cuts, level, orient):
    scale = math.sqrt(0.5) / 32.0
    return [cuts[level, 2 * orient + k].astype(jnp.float32) * scale for k in range(2)]


def cut_maps(cuts, level, shape):
    row_low = lax.broadcasted_iota(jnp.int32, shape, 0) < shape[0] // 2
    col_low = lax.broadcasted_iota(jnp.int32, shape, 1) < shape[1] // 2
    lh, hl, hh = (cut_of(cuts, level, o) for o in range(3))
    pick = [jnp.where(row_low, lh[k], jnp.where(col_low, hl[k], hh[k])) for k in range(2)]
    return pick[0], pick[1], jnp.logical_and(row_low, col_low)


def quarters(x):
    r, n = x.shape[0] // 2, x.shape[1] // 2
    return x[:r, :n], x[:r, n:], x[r:, :n], x[r:, n:]


def joined(parts):
    aa, ab, ba, bb = parts
    return jnp.concatenate(
        [jnp.concatenate([aa, ab], 1), jnp.concatenate([ba, bb], 1)], 0
    )


def synthesised(x, table):
    rows = x.shape[0]
    y = dot(jnp.concatenate(split(x), 0), table, False)
    return y[:rows, :BLOCK] + (y[:rows, BLOCK:] + y[rows:, :BLOCK])


def denoise(cuts, slab, chosen, tables, picked, cleaned):
    chan, chan_back, time, time_back = tables
    rows = slab.shape[1]
    length = time.shape[1]
    deep = time_back.shape[0]
    x = jnp.concatenate([slab[0], slab[1]], 1)
    y = dot(time[...], x, True)

    def timed(low, high):
        return y[low[0] : low[1]] + y[high[0] : high[1]]

    first_low = split(timed((0, length), (3 * length, 4 * length)))
    first_high = split(timed((length, 2 * length), (2 * length, 3 * length)))
    second = split(timed((4 * length, 5 * length), (5 * length, 6 * length)))
    third = split(timed((6 * length, 6 * length + length // 2), (6 * length + length // 2, 7 * length)))

    a = dot(chan[: 4 * rows, :], first_high[0], True)
    b = dot(chan[: 2 * rows, :], first_high[1], True)
    lh = joined(shrink(*quarters(a[:rows] + (a[3 * rows :] + b[:rows])), *cut_of(cuts, 0, 0)))
    hh = a[rows : 2 * rows] + (a[2 * rows : 3 * rows] + b[rows:])
    hh = joined(shrink(*quarters(hh), *cut_of(cuts, 0, 2)))
    a = dot(chan[rows : 3 * rows, :], first_low[0], True)
    b = dot(chan[rows : 2 * rows, :], first_low[1], True)
    hl = joined(shrink(*quarters(a[:rows] + (a[rows:] + b)), *cut_of(cuts, 0, 1)))

    a = dot(chan[4 * rows : 6 * rows, :], second[0], True)
    z = quarters(a[:rows] + (a[rows:] + dot(chan[4 * rows : 5 * rows, :], second[1], True)))
    one, two, kept = cut_maps(cuts, 1, z[0].shape)
    mid = joined([jnp.where(kept, 0.0, p) for p in shrink(*z, one, two)])

    a = dot(chan[6 * rows :, :], jnp.concatenate(third, 0), True)
    width = a.shape[1] // 2
    z = quarters(a[: rows // 2, :width] + (a[: rows // 2, width:] + a[rows // 2 :, :width]))
    one, two, kept = cut_maps(cuts, 2, z[0].shape)
    last = joined([jnp.where(kept, p, q) for p, q in zip(z, shrink(*z, one, two))])

    back = jnp.concatenate(
        [
            synthesised(lh, time_back[length : 2 * length, :]),
            synthesised(jnp.concatenate([hl, hh], 1), time_back[: 2 * length, :]),
            synthesised(mid, time_back[2 * length : 3 * length, :]),
            synthesised(last, time_back[3 * length : deep, :]),
        ],
        0,
    )
    y = dot(chan_back[...], jnp.concatenate(split(back), 1), False)
    whole = y[:rows, :BLOCK] + (y[:rows, BLOCK:] + y[rows:, :BLOCK])
    result = (0.25 * whole).astype(jnp.bfloat16)
    cleaned[...] = result.astype(jnp.float32).reshape(rows // 8, 8, BLOCK).astype(jnp.bfloat16)
    picked[...] = dot(chosen[...], result, False).astype(jnp.bfloat16)


def spread(picks, cleaned, receivers, sent, recv, crossed, sent_rows, landed):
    n_chan, n_tm = lax.axis_size("chan"), lax.axis_size("tm")
    c, t = lax.axis_index("chan"), lax.axis_index("tm")
    blocks = picks.shape[0]
    count = blocks // n_tm
    rep = n_chan // count
    pairs = n_tm // 2
    share = cleaned.shape[0] * 8 // (n_chan * n_tm)
    seat = ratio(c, rep)
    copy_index = c - seat * rep
    place = turned(seat, count)
    pair = t // 2
    core = t - 2 * pair
    other_core = t + 1 - 2 * core
    mine = t * count + place

    def move(block, sem, chan, tm):
        return pltpu.make_async_remote_copy(
            src_ref=picks.at[block],
            dst_ref=picks.at[block],
            send_sem=sent,
            recv_sem=sem,
            device_id=(chan, tm),
            device_id_type=MESH,
        )

    def chan_of(seat):
        return seat * rep + copy_index

    def block_at(k, u):
        tm = t if u == 0 else wrap(pair + pairs - u, pairs) * 2 + core
        return tm * count + (place if isinstance(k, int) and k == 0 else wrap(place + count - k, count))

    def rows_of(dc, dt):
        at = dc * n_tm + dt
        return at * (share // 8) if share % 8 == 0 else at * share // 8

    def personal(k):
        to = k + jnp.where(k >= seat * n_tm + t, 1, 0)
        chan, to_tm = chan_of(to // n_tm), lax.rem(to, n_tm)
        return pltpu.make_async_remote_copy(
            src_ref=cleaned.at[rows_of(chan, to_tm)],
            dst_ref=receivers.at[mine],
            send_sem=sent_rows,
            recv_sem=landed,
            device_id=(chan, to_tm),
            device_id_type=MESH,
        )

    def relay(k, u):
        block = block_at(k, u)
        copy = move(block, crossed.at[min(u, 1)], c, other_core)
        if u or not isinstance(k, int) or k:
            move(block, recv.at[block], c, other_core).wait_recv()
        copy.start()

    def along_chan(k):
        to = k + jnp.where(k >= seat, 1, 0)
        move(mine, recv.at[mine], chan_of(to), t).start()

    def bytes_of(ref, sem):
        return pltpu.make_async_copy(ref, ref, sem)

    each(0, count - 1, along_chan)
    local = pltpu.make_async_copy(cleaned.at[rows_of(c, t)], receivers.at[mine], landed)
    local.start()
    relay(0, 0)
    each(0, blocks - 1, lambda k: personal(k).start())
    for u in range(1, pairs):
        to = wrap(pair + u, pairs) * 2 + core
        each(0, count, lambda k, to=to: move(mine, recv.at[mine], chan_of(k), to).start())

    def near():
        each(1, count, lambda k: relay(k, 0))
        bytes_of(picks.at[pl.ds(0, count)], crossed.at[0]).wait()
        bytes_of(receivers, landed).wait()

    def far():
        for u in range(1, pairs):
            each(0, count, lambda k, u=u: relay(k, u))
        bytes_of(picks.at[pl.ds(0, (pairs - 1) * count)], crossed.at[1]).wait()

    def settle():
        bytes_of(picks.at[pl.ds(0, blocks - 1)], sent).wait()
        bytes_of(receivers.at[pl.ds(0, blocks - 1)], sent_rows).wait()

    return near, far, settle


def whole_kernel(n_tables, cuts, samples, sources, *refs):
    stored, refs = refs[:n_tables], refs[n_tables:]
    white, heard, partial, picks, receivers, white_own, heard_own = refs[:7]
    held, refs = refs[7 : 7 + n_tables], refs[7 + n_tables :]
    here, refs = refs[:4], refs[4:]
    slab, window, edge, chosen, cleaned, loads = refs[:6]
    gather_sems, spread_sems = refs[6:10], refs[10:]
    inputs = [
        pltpu.make_async_copy(a, b, here[3].at[i])
        for i, (a, b) in enumerate(zip((cuts, samples, sources), here))
    ]
    inputs[1].start()
    answers = greet(window.shape[0] - 1)
    copies = [pltpu.make_async_copy(a, b, loads.at[i]) for i, (a, b) in enumerate(zip(stored, held))]

    def meanwhile():
        inputs[2].start()
        inputs[0].start()
        for copy in copies:
            copy.start()
        inputs[2].wait()
        shape = chosen.shape[::-1]
        one_hot = jnp.where(lax.broadcasted_iota(jnp.int32, shape, 0) == here[2][...], 1.0, 0.0)
        chosen[...] = jnp.transpose(one_hot).astype(jnp.bfloat16)

    inputs[1].wait()
    gathered = gather(meanwhile, answers, here[1], slab, window, edge, *gather_sems)
    inputs[0].wait()
    for copy in copies[:-1]:
        copy.wait()
    time, time_back, chan_back = held[:3]
    chan = held[3] if n_tables == 5 else time
    n_tm = lax.axis_size("tm")
    count = picks.shape[0] // n_tm
    rep = lax.axis_size("chan") // count
    t = lax.axis_index("tm")
    mine = t * count + turned(ratio(lax.axis_index("chan"), rep), count)
    denoise(here[0], slab, chosen, (chan, chan_back, time, time_back), picks.at[mine], cleaned)
    near, far, settle = spread(picks, cleaned, receivers, *spread_sems)
    copies[-1].wait()
    t = lax.axis_index("tm")
    pair = t // 2
    pairs = n_tm // 2
    near()
    own = [2 * pair, 2 * pair + 1]
    whiten(picks, receivers, held[-1], white_own, heard_own, own)
    windows, sources = heard_own.shape[1] // 8, picks.shape[1]
    partial_products(white_own, heard_own, partial, windows, sources)
    far()
    rest = [2 * wrap(pair + u, pairs) + side for u in range(1, pairs) for side in range(2)]
    whiten(picks, receivers, held[-1], white, heard, rest)
    gathered()
    settle()


def whiten(picks, receivers, table, white, heard, parts):
    per_window = N // BLOCK
    sources = picks.shape[1]
    count = picks.shape[0] // lax.axis_size("tm")
    starts = [tm * count + i for tm in parts for i in range(0, count, per_window)]
    windows = len(starts)

    def window(ref, start):
        return jnp.concatenate([ref[start + j] for j in range(per_window)], 1)

    rows = [window(receivers, start).astype(jnp.float32) for start in starts]
    block = jnp.concatenate(
        [window(picks, start) for start in starts]
        + [jnp.concatenate(rows, 0).astype(jnp.bfloat16)],
        0,
    )
    spectra = dot(block, table[...], False)
    scale = lax.rsqrt(jnp.mean(spectra * spectra, axis=1, keepdims=True) + 1e-05)
    spectra = (spectra * scale).astype(jnp.bfloat16).astype(jnp.float32)
    base = windows * sources
    chunks = BINS // BLOCK
    weight = jnp.where(lax.broadcasted_iota(jnp.int32, (1, BLOCK), 1) == 0, 1.0, 2.0)
    for part in range(chunks):
        real = spectra[:, BLOCK * part : BLOCK * (part + 1)]
        imag = spectra[:, BINS + BLOCK * part : BINS + BLOCK * (part + 1)]
        white[part, :base, :] = real[:base]
        white[chunks + part, :base, :] = imag[:base]
        white[2 * chunks + part, :base, :] = real[:base] + imag[:base]
        real, imag = (x[base:] * (2.0 if part else weight) for x in (real, imag))
        heard[part, : 8 * windows, :] = real
        heard[chunks + part, : 8 * windows, :] = real + imag
        heard[2 * chunks + part, : 8 * windows, :] = real - imag


def products(white, heard, windows, sources, columns, first, count, finish):
    chunks = BINS // BLOCK
    near = [
        [heard[kind * chunks + columns, 8 * w : 8 * w + 8, :] for kind in range(3)]
        for w in range(windows)
    ]
    found = [[], []]
    for j in range(count):
        sums = [None] * 3
        for w in range(windows):
            spot = pl.ds(w * sources + first + j, 8, stride=0)
            for n, kind in enumerate((2, 0, 1)):
                term = white.at[kind * chunks + columns][spot, :] * near[w][n]
                sums[n] = term if sums[n] is None else sums[n] + term
        found[0].append(sums[0] - sums[2])
        found[1].append(sums[0] - sums[1])
    for at, values in zip((columns * BLOCK, BINS + columns * BLOCK), found):
        finish(slice(at, at + BLOCK), jnp.concatenate(values, 0))


def partial_products(white, heard, partial, windows, sources):
    group = math.gcd(32, sources)
    for part in range(BINS // BLOCK):

        def body(g, carry, part=part):
            spot = pl.ds(pl.multiple_of(8 * group * g, 8 * group), 8 * group)

            def finish(at, value):
                partial[spot, at] = value

            products(white, heard, windows, sources, part, group * g, group, finish)
            return carry

        lax.fori_loop(0, sources // group, body, 0)


def lag_kernel(sources, white, heard, partial, lags, out, cross, held, sems):
    parts, rows = held.shape[:2]
    windows = white.shape[1] // sources
    each_part = rows // 8
    group = math.gcd(each_part if windows <= 2 else 16, each_part)
    copies = []
    for i in range(parts):
        for part in range(BINS // BLOCK):

            def body(g, carry, i=i, part=part):
                start = 8 * (i * each_part + group * g)
                if not isinstance(start, int):
                    start = pl.multiple_of(start, 8 * group)
                spot = pl.ds(start, 8 * group)

                def finish(at, value):
                    cross[spot, at] = (value + partial[spot, at]).astype(jnp.bfloat16)

                first = i * each_part + group * g
                products(white, heard, windows, sources, part, first, group, finish)
                return carry

            if group == each_part:
                body(0, 0)
            else:
                lax.fori_loop(0, each_part // group, body, 0)
        part = slice(i * rows, (i + 1) * rows)
        held[i] = dot(cross[part, :], lags[...], False)
        copies.append(pltpu.make_async_copy(held.at[i], out.at[part, :], sems.at[i]))
        copies[i].start()
    for copy in copies:
        copy.wait()


def local(samples, thresholds, sources):
    n_chan, n_tm = lax.axis_size("chan"), lax.axis_size("tm")
    rows, width = samples.shape
    channels = rows * n_chan
    count = width // BLOCK
    rep = n_chan // count
    blocks = count * n_tm
    windows = n_tm * width // N
    picked_count = sources.shape[0]
    vmem = pl.BlockSpec(memory_space=pltpu.VMEM)
    hbm = pl.BlockSpec(memory_space=pltpu.HBM)
    dma = pltpu.SemaphoreType.DMA
    f32, bf16 = jnp.float32, jnp.bfloat16
    big = (40 if channels == 2 * BLOCK else 47) * 1024 * 1024

    time = stacked(levels_of(2 * BLOCK))
    back = halves(levels_of(2 * BLOCK)[:, HALF : HALF + BLOCK])
    chan = levels_of(channels)
    chan_back = two_halves(np.ascontiguousarray(chan.T))
    tables = [time, np.concatenate([back[0], back[1]], 1), chan_back]
    if channels != 2 * BLOCK:
        tables.append(stacked(chan))
    tables.append(dft_table())

    chunks = BINS // BLOCK
    each_tm = width // N
    most = (n_tm - 2) * each_tm
    spectra = pl.pallas_call(
        functools.partial(whole_kernel, len(tables)),
        out_shape=(
            pltpu.VMEM((3 * chunks, most * picked_count, BLOCK), f32),
            pltpu.VMEM((3 * chunks, most * 8, BLOCK), f32),
            pltpu.VMEM((picked_count * 8, N), f32),
        ),
        in_specs=[hbm] * (3 + len(tables)),
        out_specs=(vmem, vmem, vmem),
        scratch_shapes=[
            pltpu.VMEM((blocks, picked_count, BLOCK), bf16),
            pltpu.VMEM((blocks, 8, BLOCK), bf16),
            pltpu.VMEM((3 * chunks, 2 * each_tm * picked_count, BLOCK), f32),
            pltpu.VMEM((3 * chunks, 2 * each_tm * 8, BLOCK), f32),
        ]
        + [pltpu.VMEM(a.shape, bf16) for a in tables]
        + [
            pltpu.SMEM(thresholds.shape, jnp.int32),
            pltpu.VMEM(samples.shape, f32),
            pltpu.VMEM((1, picked_count), jnp.int32),
            dma((3,)),
        ]
        + [
            pltpu.VMEM((2, channels, BLOCK), bf16),
            pltpu.VMEM((count + 1, rows, BLOCK), bf16),
            pltpu.VMEM((channels, BLOCK), bf16),
            pltpu.VMEM((picked_count, channels), bf16),
            pltpu.VMEM((channels // 8, 8, BLOCK), bf16),
            dma((len(tables),)),
            dma,
            dma,
            dma,
            dma,
            dma,
            dma((blocks,)),
            dma((2,)),
            dma,
            dma,
        ],
        compiler_params=pltpu.CompilerParams(
            collective_id=0, has_side_effects=True, vmem_limit_bytes=big
        ),
        name="whole",
    )(*[
        pltpu.with_memory_space_constraint(a, pltpu.HBM)
        for a in (thresholds, samples, sources[None, :], *[jnp.asarray(a) for a in tables])
    ])

    half = LAGS // 2
    dft = tables[-1]
    lags = np.concatenate([dft[N - half :], dft[:half]], 0).T.astype(np.float32)
    lags = (lags / math.sqrt(windows * N)).astype(jnp.bfloat16)
    out = pl.pallas_call(
        functools.partial(lag_kernel, picked_count),
        out_shape=jax.ShapeDtypeStruct((picked_count * 8, LAGS), f32),
        in_specs=[vmem] * 4,
        out_specs=pl.BlockSpec(memory_space=pl.ANY),
        scratch_shapes=[
            pltpu.VMEM((picked_count * 8, N), bf16),
            pltpu.VMEM((2, picked_count * 4, LAGS), f32),
            dma((2,)),
        ],
        compiler_params=pltpu.CompilerParams(vmem_limit_bytes=16 * 1024 * 1024),
        name="lags",
    )(*spectra, jnp.asarray(lags))

    out = out.reshape(picked_count, 8, LAGS)
    share = channels // (n_chan * n_tm)
    if share < 8:
        place = lax.axis_index("chan") * n_tm + lax.axis_index("tm")
        out = lax.dynamic_slice_in_dim(out, lax.rem(place * share, 8), share, 1)
    return out


def solution(mesh):
    return jax.shard_map(
        local,
        mesh=mesh,
        in_specs=(P("chan", "tm"), P(), P()),
        out_specs=P(None, ("chan", "tm"), None),
        check_vma=False,
    )
```

```python
import functools
import math

import jax
import jax.numpy as jnp
import numpy as np
from jax import lax
from jax.experimental import pallas as pl
from jax.experimental.pallas import tpu as pltpu
from jax.sharding import PartitionSpec as P

N = 1024
LEVELS = 3
BINS = 512
LAGS = 512
BLOCK = 128
HALF = 64
MESH = pl.DeviceIdType.MESH

daubechies = [
    0.2303778133088964,
    0.7148465705529155,
    0.6308807679298587,
    -0.0279837694168599,
    -0.1870348117190931,
    0.0308413818355607,
    0.0328830116668852,
    -0.010597401785069,
]


def filter_bank():
    lowpass = list(daubechies)
    highpass = [(1.0 if k % 2 == 0 else -1.0) * daubechies[7 - k] for k in range(8)]
    return [(lowpass, highpass), (lowpass[::-1], highpass[::-1])]


def bank_matrix(length):
    half = length // 2
    out = np.zeros((2, 2, half, length))
    rows = np.arange(half)
    for tree, pair in enumerate(filter_bank()):
        for band, taps in enumerate(pair):
            for k in range(8):
                np.add.at(out[tree, band], (rows, (2 * rows + k - 3) % length), taps[k])
    return out


def levels_of(length):
    first, second, third = (bank_matrix(length >> level) for level in range(3))
    parts = [first[0, 0], first[1, 0], first[0, 1], first[1, 1]]
    for tree in range(2):
        parts += [second[tree, band] @ first[tree, 0] for band in range(2)]
    for tree in range(2):
        low = second[tree, 0] @ first[tree, 0]
        parts += [third[tree, band] @ low for band in range(2)]
    return np.concatenate(parts, 0)


def halves(matrix):
    m32 = np.asarray(matrix, np.float32)
    hi = m32.astype(jnp.bfloat16)
    lo = (m32 - hi.astype(np.float32)).astype(jnp.bfloat16)
    return np.stack([hi, lo])


def two_halves(matrix):
    return np.concatenate(list(halves(matrix)), 0)


def stacked(matrix):
    hi, lo = halves(matrix)
    n = matrix.shape[1]
    parts = [hi[: 2 * n], lo[n : 2 * n], lo[:n]]
    parts += [x[at] for at in (slice(2 * n, 3 * n), slice(3 * n, None)) for x in (hi, lo)]
    return np.concatenate(parts, 0)


def dft_table():
    t = np.arange(N)
    f = np.arange(BINS)
    phases = ((t[:, None] * f[None, :]) % N).astype(np.float64) * (2.0 * math.pi / N)
    table = np.concatenate([np.cos(phases), -np.sin(phases)], 1)
    return table.astype(np.float32).astype(jnp.bfloat16)


def split(x):
    hi = x.astype(jnp.bfloat16)
    lo = (x - hi.astype(jnp.float32)).astype(jnp.bfloat16)
    return hi, lo


def dot(a, b, trans_b):
    dims = (((1,), (1 if trans_b else 0,)), ((), ()))
    return lax.dot_general(a, b, dims, preferred_element_type=jnp.float32)


def wrap(x, n):
    return jnp.where(x >= n, x - n, x)


def ratio(x, n):
    return x if n == 1 else x // n


def turned(seat, count):
    return wrap(seat + count // 2, count)


def each(low, high, act):
    def body(k, carry):
        act(k)
        return carry

    if high - low <= 1:
        for k in range(low, high):
            act(k)
    else:
        lax.fori_loop(low, high, body, 0)


def greet(count):
    n_chan, n_tm = lax.axis_size("chan"), lax.axis_size("tm")
    c, t = lax.axis_index("chan"), lax.axis_index("tm")
    rep = n_chan // count
    place = turned(ratio(c, rep), count)
    barrier = pltpu.get_barrier_semaphore()

    def signal(chan, tm):
        pl.semaphore_signal(barrier, inc=1, device_id=(chan, tm), device_id_type=MESH)

    each(1, n_chan, lambda k: signal(wrap(c + k, n_chan), t))
    for at, shift in ((0, n_tm - 1), (count - 1, 1)):

        @pl.when(place == at)
        def _(shift=shift):
            each(0, n_chan, lambda k: signal(k, wrap(t + shift, n_tm)))

    for j in range(1, n_tm):
        signal(c, wrap(t + j, n_tm))
    return n_chan - 1 + 2 * rep + n_tm - 1


def gather(meanwhile, answers, samples, slab, window, edge, sent, recv, edge_sent, edge_recv):
    n_chan, n_tm = lax.axis_size("chan"), lax.axis_size("tm")
    c, t = lax.axis_index("chan"), lax.axis_index("tm")
    rows, width = samples.shape
    channels = slab.shape[1]
    count = width // BLOCK
    rep = n_chan // count
    values = samples[...]
    around = jnp.concatenate([values[:, width - HALF :], values, values[:, :HALF]], 1)
    for j in range(count + 1):
        window[j] = around[:, BLOCK * j : BLOCK * (j + 1)].astype(jnp.bfloat16)
    pl.semaphore_wait(pltpu.get_barrier_semaphore(), answers)
    mine = pl.ds(pl.multiple_of(c * rows, rows), rows)
    place = turned(ratio(c, rep), count)

    def remote(to):
        return pltpu.make_async_remote_copy(
            src_ref=window.at[pl.ds(turned(ratio(to, rep), count), 2)],
            dst_ref=slab.at[:, mine, :],
            send_sem=sent,
            recv_sem=recv,
            device_id=(to, t),
            device_id_type=MESH,
        )

    def rim(block, r, shift):
        tm = wrap(t + shift, n_tm)
        return pltpu.make_async_remote_copy(
            src_ref=window.at[0],
            dst_ref=edge.at[mine, :],
            send_sem=edge_sent,
            recv_sem=edge_recv,
            device_id=(turned(block, count) * rep + r, tm),
            device_id_type=MESH,
        )

    each(1, n_chan, lambda k: remote(wrap(c + k, n_chan)).start())
    for r in range(rep):
        rim(0, r, 1).start()
        rim(count - 1, r, n_tm - 1).start()
    for j in range(2):
        slab[j, mine, :] = window[place + j]
    meanwhile()

    def bytes_of(ref, sem):
        return pltpu.make_async_copy(ref, ref, sem)

    others = channels - rows
    bytes_of(slab.at[:, pl.ds(0, others), :], recv).wait()

    @pl.when(jnp.logical_or(place == 0, place == count - 1))
    def _():
        bytes_of(edge, edge_recv).wait()

    left = lax.broadcasted_iota(jnp.int32, edge.shape, 1) < HALF

    @pl.when(place == 0)
    def _():
        slab[0] = jnp.where(left, edge[...], slab[0])

    @pl.when(place == count - 1)
    def _():
        slab[1] = jnp.where(left, slab[1], edge[...])

    def settle():
        bytes_of(slab.at[:, pl.ds(0, others), :], sent).wait()
        bytes_of(window.at[pl.ds(0, 2 * rep)], edge_sent).wait()

    return settle


def shrink(aa, ab, ba, bb, cut_one, cut_two):
    re1, im1, re2, im2 = aa - bb, ab + ba, aa + bb, ab - ba
    f1 = jnp.maximum(0.5 - cut_one * lax.rsqrt(re1 * re1 + im1 * im1), 0.0)
    f2 = jnp.maximum(0.5 - cut_two * lax.rsqrt(re2 * re2 + im2 * im2), 0.0)
    re1, im1, re2, im2 = re1 * f1, im1 * f1, re2 * f2, im2 * f2
    return re1 + re2, im1 + im2, im1 - im2, re2 - re1


def cut_of(cuts, level, orient):
    scale = math.sqrt(0.5) / 32.0
    return [cuts[level, 2 * orient + k].astype(jnp.float32) * scale for k in range(2)]


def cut_maps(cuts, level, shape):
    row_low = lax.broadcasted_iota(jnp.int32, shape, 0) < shape[0] // 2
    col_low = lax.broadcasted_iota(jnp.int32, shape, 1) < shape[1] // 2
    lh, hl, hh = (cut_of(cuts, level, o) for o in range(3))
    pick = [jnp.where(row_low, lh[k], jnp.where(col_low, hl[k], hh[k])) for k in range(2)]
    return pick[0], pick[1], jnp.logical_and(row_low, col_low)


def quarters(x):
    r, n = x.shape[0] // 2, x.shape[1] // 2
    return x[:r, :n], x[:r, n:], x[r:, :n], x[r:, n:]


def joined(parts):
    aa, ab, ba, bb = parts
    return jnp.concatenate(
        [jnp.concatenate([aa, ab], 1), jnp.concatenate([ba, bb], 1)], 0
    )


def synthesised(x, table):
    rows = x.shape[0]
    y = dot(jnp.concatenate(split(x), 0), table, False)
    return y[:rows, :BLOCK] + (y[:rows, BLOCK:] + y[rows:, :BLOCK])


def denoise(cuts, slab, chosen, tables, picked, cleaned):
    chan, chan_back, time, time_back = tables
    rows = slab.shape[1]
    length = time.shape[1]
    deep = time_back.shape[0]
    x = jnp.concatenate([slab[0], slab[1]], 1)
    y = dot(time[...], x, True)

    def timed(low, high):
        return y[low[0] : low[1]] + y[high[0] : high[1]]

    first_low = split(timed((0, length), (3 * length, 4 * length)))
    first_high = split(timed((length, 2 * length), (2 * length, 3 * length)))
    second = split(timed((4 * length, 5 * length), (5 * length, 6 * length)))
    third = split(timed((6 * length, 6 * length + length // 2), (6 * length + length // 2, 7 * length)))

    a = dot(chan[: 4 * rows, :], first_high[0], True)
    b = dot(chan[: 2 * rows, :], first_high[1], True)
    lh = joined(shrink(*quarters(a[:rows] + (a[3 * rows :] + b[:rows])), *cut_of(cuts, 0, 0)))
    hh = a[rows : 2 * rows] + (a[2 * rows : 3 * rows] + b[rows:])
    hh = joined(shrink(*quarters(hh), *cut_of(cuts, 0, 2)))
    a = dot(chan[rows : 3 * rows, :], first_low[0], True)
    b = dot(chan[rows : 2 * rows, :], first_low[1], True)
    hl = joined(shrink(*quarters(a[:rows] + (a[rows:] + b)), *cut_of(cuts, 0, 1)))

    a = dot(chan[4 * rows : 6 * rows, :], second[0], True)
    z = quarters(a[:rows] + (a[rows:] + dot(chan[4 * rows : 5 * rows, :], second[1], True)))
    one, two, kept = cut_maps(cuts, 1, z[0].shape)
    mid = joined([jnp.where(kept, 0.0, p) for p in shrink(*z, one, two)])

    a = dot(chan[6 * rows :, :], jnp.concatenate(third, 0), True)
    width = a.shape[1] // 2
    z = quarters(a[: rows // 2, :width] + (a[: rows // 2, width:] + a[rows // 2 :, :width]))
    one, two, kept = cut_maps(cuts, 2, z[0].shape)
    last = joined([jnp.where(kept, p, q) for p, q in zip(z, shrink(*z, one, two))])

    back = jnp.concatenate(
        [
            synthesised(lh, time_back[length : 2 * length, :]),
            synthesised(jnp.concatenate([hl, hh], 1), time_back[: 2 * length, :]),
            synthesised(mid, time_back[2 * length : 3 * length, :]),
            synthesised(last, time_back[3 * length : deep, :]),
        ],
        0,
    )
    y = dot(chan_back[...], jnp.concatenate(split(back), 1), False)
    whole = y[:rows, :BLOCK] + (y[:rows, BLOCK:] + y[rows:, :BLOCK])
    result = (0.25 * whole).astype(jnp.bfloat16)
    cleaned[...] = result.astype(jnp.float32).reshape(rows // 8, 8, BLOCK).astype(jnp.bfloat16)
    picked[...] = dot(chosen[...], result, False).astype(jnp.bfloat16)


def spread(picks, cleaned, receivers, sent, recv, crossed, sent_rows, landed):
    n_chan, n_tm = lax.axis_size("chan"), lax.axis_size("tm")
    c, t = lax.axis_index("chan"), lax.axis_index("tm")
    blocks = picks.shape[0]
    count = blocks // n_tm
    rep = n_chan // count
    pairs = n_tm // 2
    share = cleaned.shape[0] * 8 // (n_chan * n_tm)
    seat = ratio(c, rep)
    copy_index = c - seat * rep
    place = turned(seat, count)
    pair = t // 2
    core = t - 2 * pair
    other_core = t + 1 - 2 * core
    mine = t * count + place

    def move(block, sem, chan, tm):
        return pltpu.make_async_remote_copy(
            src_ref=picks.at[block],
            dst_ref=picks.at[block],
            send_sem=sent,
            recv_sem=sem,
            device_id=(chan, tm),
            device_id_type=MESH,
        )

    def chan_of(seat):
        return seat * rep + copy_index

    def block_at(k, u):
        tm = t if u == 0 else wrap(pair + pairs - u, pairs) * 2 + core
        return tm * count + (place if isinstance(k, int) and k == 0 else wrap(place + count - k, count))

    def rows_of(dc, dt):
        at = dc * n_tm + dt
        return at * (share // 8) if share % 8 == 0 else at * share // 8

    def personal(k):
        to = k + jnp.where(k >= seat * n_tm + t, 1, 0)
        chan, to_tm = chan_of(to // n_tm), lax.rem(to, n_tm)
        return pltpu.make_async_remote_copy(
            src_ref=cleaned.at[rows_of(chan, to_tm)],
            dst_ref=receivers.at[mine],
            send_sem=sent_rows,
            recv_sem=landed,
            device_id=(chan, to_tm),
            device_id_type=MESH,
        )

    def relay(k, u):
        block = block_at(k, u)
        copy = move(block, crossed.at[min(u, 1)], c, other_core)
        if u or not isinstance(k, int) or k:
            move(block, recv.at[block], c, other_core).wait_recv()
        copy.start()

    def along_chan(k):
        to = k + jnp.where(k >= seat, 1, 0)
        move(mine, recv.at[mine], chan_of(to), t).start()

    def bytes_of(ref, sem):
        return pltpu.make_async_copy(ref, ref, sem)

    each(0, count - 1, along_chan)
    local = pltpu.make_async_copy(cleaned.at[rows_of(c, t)], receivers.at[mine], landed)
    local.start()
    relay(0, 0)
    each(0, blocks - 1, lambda k: personal(k).start())
    for u in range(1, pairs):
        to = wrap(pair + u, pairs) * 2 + core
        each(0, count, lambda k, to=to: move(mine, recv.at[mine], chan_of(k), to).start())

    def near():
        each(1, count, lambda k: relay(k, 0))
        bytes_of(picks.at[pl.ds(0, count)], crossed.at[0]).wait()
        bytes_of(receivers, landed).wait()

    def far():
        for u in range(1, pairs):
            each(0, count, lambda k, u=u: relay(k, u))
        bytes_of(picks.at[pl.ds(0, (pairs - 1) * count)], crossed.at[1]).wait()

    def settle():
        bytes_of(picks.at[pl.ds(0, blocks - 1)], sent).wait()
        bytes_of(receivers.at[pl.ds(0, blocks - 1)], sent_rows).wait()

    return near, far, settle


def whole_kernel(n_tables, cuts, samples, sources, *refs):
    stored, refs = refs[:n_tables], refs[n_tables:]
    white, heard, partial, picks, receivers, white_own, heard_own = refs[:7]
    held, refs = refs[7 : 7 + n_tables], refs[7 + n_tables :]
    here, refs = refs[:4], refs[4:]
    slab, window, edge, chosen, cleaned, loads = refs[:6]
    gather_sems, spread_sems = refs[6:10], refs[10:]
    inputs = [
        pltpu.make_async_copy(a, b, here[3].at[i])
        for i, (a, b) in enumerate(zip((cuts, samples, sources), here))
    ]
    inputs[1].start()
    answers = greet(window.shape[0] - 1)
    copies = [pltpu.make_async_copy(a, b, loads.at[i]) for i, (a, b) in enumerate(zip(stored, held))]

    def meanwhile():
        inputs[2].start()
        inputs[0].start()
        for copy in copies:
            copy.start()
        inputs[2].wait()
        shape = chosen.shape[::-1]
        one_hot = jnp.where(lax.broadcasted_iota(jnp.int32, shape, 0) == here[2][...], 1.0, 0.0)
        chosen[...] = jnp.transpose(one_hot).astype(jnp.bfloat16)

    inputs[1].wait()
    gathered = gather(meanwhile, answers, here[1], slab, window, edge, *gather_sems)
    inputs[0].wait()
    for copy in copies[:-1]:
        copy.wait()
    time, time_back, chan_back = held[:3]
    chan = held[3] if n_tables == 5 else time
    n_tm = lax.axis_size("tm")
    count = picks.shape[0] // n_tm
    rep = lax.axis_size("chan") // count
    t = lax.axis_index("tm")
    mine = t * count + turned(ratio(lax.axis_index("chan"), rep), count)
    denoise(here[0], slab, chosen, (chan, chan_back, time, time_back), picks.at[mine], cleaned)
    near, far, settle = spread(picks, cleaned, receivers, *spread_sems)
    copies[-1].wait()
    t = lax.axis_index("tm")
    pair = t // 2
    pairs = n_tm // 2
    near()
    own = [2 * pair, 2 * pair + 1]
    rest = [2 * wrap(pair + u, pairs) + side for u in range(1, pairs) for side in range(2)]
    heards = [(heard_own, own), (heard, rest)]
    whiten(picks, receivers, held[-1], white_own, own, heards)
    windows, sources = heard_own.shape[1] // 8, picks.shape[1]
    partial_products(white_own, heard_own, partial, windows, sources)
    far()
    whiten(picks, receivers, held[-1], white, rest, [])
    gathered()
    settle()


def whiten(picks, receivers, table, white, parts, heards):
    per_window = N // BLOCK
    sources = picks.shape[1]
    count = picks.shape[0] // lax.axis_size("tm")

    def starts_of(parts):
        return [tm * count + i for tm in parts for i in range(0, count, per_window)]

    starts = starts_of(parts)
    windows = len(starts)

    def window(ref, start):
        return jnp.concatenate([ref[start + j] for j in range(per_window)], 1)

    block = [window(picks, start) for start in starts]
    if heards:
        near = [start for _, at in heards for start in starts_of(at)]
        rows = [window(receivers, start).astype(jnp.float32) for start in near]
        block.append(jnp.concatenate(rows, 0).astype(jnp.bfloat16))
    block = jnp.concatenate(block, 0)
    spectra = dot(block, table[...], False)
    scale = lax.rsqrt(jnp.mean(spectra * spectra, axis=1, keepdims=True) + 1e-05)
    spectra = (spectra * scale).astype(jnp.bfloat16).astype(jnp.float32)
    base = windows * sources
    chunks = BINS // BLOCK
    weight = jnp.where(lax.broadcasted_iota(jnp.int32, (1, BLOCK), 1) == 0, 1.0, 2.0)
    for part in range(chunks):
        real = spectra[:, BLOCK * part : BLOCK * (part + 1)]
        imag = spectra[:, BINS + BLOCK * part : BINS + BLOCK * (part + 1)]
        white[part, :base, :] = real[:base]
        white[chunks + part, :base, :] = imag[:base]
        white[2 * chunks + part, :base, :] = real[:base] + imag[:base]
        first = base
        for heard, at in heards:
            height = 8 * len(starts_of(at))
            twice = 2.0 if part else weight
            near_real = real[first : first + height] * twice
            near_imag = imag[first : first + height] * twice
            heard[part] = near_real
            heard[chunks + part] = near_real + near_imag
            heard[2 * chunks + part] = near_real - near_imag
            first += height


def products(white, heard, windows, sources, columns, first, count, finish):
    chunks = BINS // BLOCK
    near = [
        [heard[kind * chunks + columns, 8 * w : 8 * w + 8, :] for kind in range(3)]
        for w in range(windows)
    ]
    found = [[], []]
    for j in range(count):
        sums = [None] * 3
        for w in range(windows):
            spot = pl.ds(w * sources + first + j, 8, stride=0)
            for n, kind in enumerate((2, 0, 1)):
                term = white.at[kind * chunks + columns][spot, :] * near[w][n]
                sums[n] = term if sums[n] is None else sums[n] + term
        found[0].append(sums[0] - sums[2])
        found[1].append(sums[0] - sums[1])
    for at, values in zip((columns * BLOCK, BINS + columns * BLOCK), found):
        finish(slice(at, at + BLOCK), jnp.concatenate(values, 0))


def partial_products(white, heard, partial, windows, sources):
    group = math.gcd(32, sources)
    for part in range(BINS // BLOCK):

        def body(g, carry, part=part):
            spot = pl.ds(pl.multiple_of(8 * group * g, 8 * group), 8 * group)

            def finish(at, value):
                partial[spot, at] = value

            products(white, heard, windows, sources, part, group * g, group, finish)
            return carry

        lax.fori_loop(0, sources // group, body, 0)


def lag_kernel(sources, white, heard, partial, lags, out, cross, held, sems):
    parts, rows = held.shape[:2]
    windows = white.shape[1] // sources
    each_part = rows // 8
    group = math.gcd(each_part if windows <= 2 else 16, each_part)
    copies = []
    for i in range(parts):
        for part in range(BINS // BLOCK):

            def body(g, carry, i=i, part=part):
                start = 8 * (i * each_part + group * g)
                if not isinstance(start, int):
                    start = pl.multiple_of(start, 8 * group)
                spot = pl.ds(start, 8 * group)

                def finish(at, value):
                    cross[spot, at] = (value + partial[spot, at]).astype(jnp.bfloat16)

                first = i * each_part + group * g
                products(white, heard, windows, sources, part, first, group, finish)
                return carry

            if group == each_part:
                body(0, 0)
            else:
                lax.fori_loop(0, each_part // group, body, 0)
        part = slice(i * rows, (i + 1) * rows)
        held[i] = dot(cross[part, :], lags[...], False)
        copies.append(pltpu.make_async_copy(held.at[i], out.at[part, :], sems.at[i]))
        copies[i].start()
    for copy in copies:
        copy.wait()


def local(samples, thresholds, sources):
    n_chan, n_tm = lax.axis_size("chan"), lax.axis_size("tm")
    rows, width = samples.shape
    channels = rows * n_chan
    count = width // BLOCK
    rep = n_chan // count
    blocks = count * n_tm
    windows = n_tm * width // N
    picked_count = sources.shape[0]
    vmem = pl.BlockSpec(memory_space=pltpu.VMEM)
    hbm = pl.BlockSpec(memory_space=pltpu.HBM)
    dma = pltpu.SemaphoreType.DMA
    f32, bf16 = jnp.float32, jnp.bfloat16
    big = (40 if channels == 2 * BLOCK else 47) * 1024 * 1024

    time = stacked(levels_of(2 * BLOCK))
    back = halves(levels_of(2 * BLOCK)[:, HALF : HALF + BLOCK])
    chan = levels_of(channels)
    chan_back = two_halves(np.ascontiguousarray(chan.T))
    tables = [time, np.concatenate([back[0], back[1]], 1), chan_back]
    if channels != 2 * BLOCK:
        tables.append(stacked(chan))
    tables.append(dft_table())

    chunks = BINS // BLOCK
    each_tm = width // N
    most = (n_tm - 2) * each_tm
    spectra = pl.pallas_call(
        functools.partial(whole_kernel, len(tables)),
        out_shape=(
            pltpu.VMEM((3 * chunks, most * picked_count, BLOCK), f32),
            pltpu.VMEM((3 * chunks, most * 8, BLOCK), f32),
            pltpu.VMEM((picked_count * 8, N), f32),
        ),
        in_specs=[hbm] * (3 + len(tables)),
        out_specs=(vmem, vmem, vmem),
        scratch_shapes=[
            pltpu.VMEM((blocks, picked_count, BLOCK), bf16),
            pltpu.VMEM((blocks, 8, BLOCK), bf16),
            pltpu.VMEM((3 * chunks, 2 * each_tm * picked_count, BLOCK), f32),
            pltpu.VMEM((3 * chunks, 2 * each_tm * 8, BLOCK), f32),
        ]
        + [pltpu.VMEM(a.shape, bf16) for a in tables]
        + [
            pltpu.SMEM(thresholds.shape, jnp.int32),
            pltpu.VMEM(samples.shape, f32),
            pltpu.VMEM((1, picked_count), jnp.int32),
            dma((3,)),
        ]
        + [
            pltpu.VMEM((2, channels, BLOCK), bf16),
            pltpu.VMEM((count + 1, rows, BLOCK), bf16),
            pltpu.VMEM((channels, BLOCK), bf16),
            pltpu.VMEM((picked_count, channels), bf16),
            pltpu.VMEM((channels // 8, 8, BLOCK), bf16),
            dma((len(tables),)),
            dma,
            dma,
            dma,
            dma,
            dma,
            dma((blocks,)),
            dma((2,)),
            dma,
            dma,
        ],
        compiler_params=pltpu.CompilerParams(
            collective_id=0, has_side_effects=True, vmem_limit_bytes=big
        ),
        name="whole",
    )(*[
        pltpu.with_memory_space_constraint(a, pltpu.HBM)
        for a in (thresholds, samples, sources[None, :], *[jnp.asarray(a) for a in tables])
    ])

    half = LAGS // 2
    dft = tables[-1]
    lags = np.concatenate([dft[N - half :], dft[:half]], 0).T.astype(np.float32)
    lags = (lags / math.sqrt(windows * N)).astype(jnp.bfloat16)
    out = pl.pallas_call(
        functools.partial(lag_kernel, picked_count),
        out_shape=jax.ShapeDtypeStruct((picked_count * 8, LAGS), f32),
        in_specs=[vmem] * 4,
        out_specs=pl.BlockSpec(memory_space=pl.ANY),
        scratch_shapes=[
            pltpu.VMEM((picked_count * 8, N), bf16),
            pltpu.VMEM((2, picked_count * 4, LAGS), f32),
            dma((2,)),
        ],
        compiler_params=pltpu.CompilerParams(vmem_limit_bytes=16 * 1024 * 1024),
        name="lags",
    )(*spectra, jnp.asarray(lags))

    out = out.reshape(picked_count, 8, LAGS)
    share = channels // (n_chan * n_tm)
    if share < 8:
        place = lax.axis_index("chan") * n_tm + lax.axis_index("tm")
        out = lax.dynamic_slice_in_dim(out, lax.rem(place * share, 8), share, 1)
    return out


def solution(mesh):
    return jax.shard_map(
        local,
        mesh=mesh,
        in_specs=(P("chan", "tm"), P(), P()),
        out_specs=P(None, ("chan", "tm"), None),
        check_vma=False,
    )
```
